512 devices in a mesh: seq: 16 (over y, z_hi, core), blk: 32 (over z_lo, x).
Axes of the slice: x: 4, y: 4, z: 16 (z_hi: 2, z_lo: 8; z = z_hi * 8 + z_lo), core: 2. Of those that a mesh axis runs over, the one named last changes fastest.
Arguments:
- hidden_states: bfloat16 [2048, 4096], P('seq'), may hold values from -6 to 6
- query_weight: bfloat16 [4096, 4096], P('seq', 'blk')
- key_weight: bfloat16 [4096, 4096], P('seq', 'blk')
- value_weight: bfloat16 [4096, 4096], P('seq', 'blk'), may hold values from -0.09375 to 0.09375
- output_weight: bfloat16 [4096, 4096], P('blk', 'seq'), may hold values from -0.1875 to 0.1875
- query_gain: float32 [4096], P('blk'), may hold values from 0.7 to 3
- key_gain: float32 [4096], P('blk'), may hold values from 0.7 to 3
- attention_gain: float32 [4096], replicated, may hold values from 0.5 to 1.5
- gate_weight: bfloat16 [4096, 11008], P('seq', 'blk'), may hold values from -0.09375 to 0.09375
- up_weight: bfloat16 [4096, 11008], P('seq', 'blk'), may hold values from -0.09375 to 0.09375
- down_weight: bfloat16 [11008, 4096], P('blk', 'seq'), may hold values from -0.109375 to 0.109375
- feedforward_gain: float32 [4096], replicated, may hold values from 0.5 to 1.5
- cached_keys: bfloat16 [16, 1024, 4096], P('seq', None, 'blk'), may hold values from -6 to 6
- cached_values: bfloat16 [16, 1024, 4096], P('seq', None, 'blk'), may hold values from -6 to 6
- passage_order: int32 [16], replicated, may hold values from 0 to 15, each once
- separators: int32 [8, 2], replicated, may hold values from 1 to 64
- recompute_index: int32 [16, 96], replicated, may hold values from 0 to 1023, as said below
- prompt_lengths: int32 [8], replicated, may hold values from 16 to 64, as said below
Outputs:
- hidden_out: bfloat16 [2048, 4096], P(('seq', 'blk'))
- blended_keys: bfloat16 [16, 1024, 4096], P('seq', None, 'blk')
- blended_values: bfloat16 [16, 1024, 4096], P('seq', None, 'blk')
The draws below stay inside these ranges and needn't reach their ends.
Inputs may be any that keep to these rules, and one draw needn't show every extreme that they name: `passage_order`: each passage id appears once. `recompute_index`: distinct within each passage. `prompt_lengths`: some request has all 64 of its new tokens live.
All inputs are finite; a program needn't handle non-finite values.
Results may differ from the reference program's by a relative error of at most 0.035.
Values may be sent and summed in bfloat16 or wider, within the bound.
No kernel may reach another device: no remote copies, remote signals or barrier semaphores. Data moves between devices by JAX's collectives and lax.ppermute only.
A program may use at most 64 MiB of HBM per device.

```python
import math
import jax
import jax.numpy as jnp
from jax import lax

D = 4096
HEADS = 32
HD = 128
FF = 11008
PLEN = 1024
SEL = 96
PPR = 2
TOKN_DEV = 32
ROW_DEV = 128
ROWS = 2048
PASSAGES = 16
REQS = 8
N_SEQ = 16
N_BLK = 32


def column_scales(key, columns):
    ramp = 3.0 ** (jnp.arange(columns, dtype=jnp.float32) / (columns - 1))
    rough = jax.random.uniform(key, (columns,), jnp.float32, 0.6, 1.6)
    return ramp * rough


def shared_noise(key):
    return jax.random.normal(jax.random.fold_in(key, 11), (D, HEADS * HD), jnp.float32)


def draw_key_weight(key, part):
    scales = column_scales(jax.random.fold_in(key, 12), HEADS * HD)
    return (shared_noise(key) * scales[None, :] * D ** (-0.5)).astype(jnp.bfloat16)


def draw_query_weight(key, part):
    noise = jax.random.normal(jax.random.fold_in(key, 21), (D, HEADS * HD), jnp.float32)
    scales = column_scales(jax.random.fold_in(key, 23), HEADS * HD)
    return (noise * scales[None, :] * D ** (-0.5)).astype(jnp.bfloat16)


def norm_gain(key):
    return jax.random.uniform(key, (HEADS * HD,), jnp.float32, 0.7, 1.4)


def draw_query_gain(key, part):
    return norm_gain(jax.random.fold_in(key, 31))


def draw_key_gain(key, part):
    return norm_gain(jax.random.fold_in(key, 32))


def draw_recompute_index(key, part):
    passage_keys = jax.random.split(jax.random.fold_in(key, 41), PASSAGES)

    def pick_rows(single_key):
        return jax.random.permutation(single_key, PLEN)[:SEL]
    return jax.vmap(pick_rows)(passage_keys).astype(jnp.int32)


def draw_prompt_lengths(key, part):
    longest = PPR * TOKN_DEV
    drawn = jax.random.randint(jax.random.fold_in(key, 51), (REQS,), longest // 4, longest + 1)
    chosen = jax.random.randint(jax.random.fold_in(key, 52), (), 0, REQS)
    return jnp.where(jnp.arange(REQS) == chosen, longest, drawn).astype(jnp.int32)


def touch_ends(result, rng, least, largest):
    index_at = [jax.random.randint(jax.random.fold_in(rng, axis), (), 0, length) for axis, length in enumerate(result.shape)]
    widest = result.shape.index(max(result.shape))
    neighbour = index_at[:widest] + [(index_at[widest] + 1) % result.shape[widest]] + index_at[widest + 1:]
    return result.at[tuple(index_at)].set(least).at[tuple(neighbour)].set(largest)


def strengthened(entries, key, source, target, shards_of, factor):
    owner, partner = [(jnp.arange(entries.shape[position]) // (entries.shape[position] // shards_of)).reshape([-1 if axis == position else 1 for axis in range(entries.ndim)]) for position in (source, target)]
    chosen = jax.random.permutation(key, shards_of)[partner]
    strong = (owner == chosen) | (owner == (partner + shards_of // 2) % shards_of)
    return jnp.where(strong, factor * entries, entries)


def level_of(stream_key, extent, shards, low, largest):
    level = 1.0
    for axis_at, shards_of in shards:
        heights = jax.random.uniform(jax.random.fold_in(jax.random.fold_in(stream_key, 6), axis_at), (shards_of,), jnp.float32, low / len(shards), largest / len(shards))
        level = level * jnp.repeat(jnp.exp(heights), extent[axis_at] // shards_of).reshape((-1,) + (1,) * (len(extent) - 1 - axis_at))
    return level


def centred(key, extent, spread, bound, shards=(), held_as=jnp.bfloat16):
    entries = spread * jax.random.normal(key, extent, jnp.float32)
    if shards:
        entries = entries * level_of(key, extent, shards, -0.22, 0.18)
    return jnp.clip(entries, -bound, bound).astype(held_as)


def heavy_noise(key, dims, scale, limit, cuts, heavy, kind=jnp.bfloat16):
    array = scale * jax.random.normal(key, dims, jnp.float32)
    if cuts:
        array = array * level_of(key, dims, cuts, -0.22, 0.18)
    return jnp.clip(strengthened(array, jax.random.fold_in(key, 3), *heavy), -limit, limit).astype(kind)


def setup_inputs(seed: int = 0) -> dict:
    key_list = jax.random.split(jax.random.key(seed), 19)
    return {
        "hidden_states": centred(key_list[0], (ROWS, D), 1.0, 6.0, ((0, 16),)),
        "query_weight": draw_query_weight(jax.random.fold_in(key_list[18], 71), 0),
        "key_weight": draw_key_weight(jax.random.fold_in(key_list[18], 71), 0),
        "value_weight": centred(key_list[3], (D, HEADS * HD), D ** -0.5, 0.09375, ((0, 16), (1, 32))),
        "output_weight": heavy_noise(key_list[4], (HEADS * HD, D), (HEADS * HD) ** -0.5, 0.1875, ((0, 32), (1, 16)), (0, 1, 32, 2.75)),
        "query_gain": draw_query_gain(jax.random.fold_in(key_list[18], 71), 0),
        "key_gain": draw_key_gain(jax.random.fold_in(key_list[18], 71), 0),
        "attention_gain": jnp.clip(1.0 + 0.1 * jax.random.normal(key_list[7], (D,), jnp.float32), 0.5, 1.5),
        "gate_weight": centred(key_list[8], (D, FF), D ** -0.5, 0.09375, ((0, 16), (1, 32))),
        "up_weight": centred(key_list[9], (D, FF), D ** -0.5, 0.09375, ((0, 16), (1, 32))),
        "down_weight": heavy_noise(key_list[10], (FF, D), FF ** -0.5, 0.109375, ((0, 32), (1, 16)), (0, 1, 32, 2.75)),
        "feedforward_gain": jnp.clip(1.0 + 0.1 * jax.random.normal(key_list[11], (D,), jnp.float32), 0.5, 1.5),
        "cached_keys": centred(key_list[12], (PASSAGES, PLEN, HEADS * HD), 1.0, 6.0, ((0, 16), (2, 32))),
        "cached_values": centred(key_list[13], (PASSAGES, PLEN, HEADS * HD), 1.0, 6.0, ((0, 16), (2, 32))),
        "passage_order": jax.random.permutation(key_list[14], PASSAGES).astype(jnp.int32),
        "separators": touch_ends(jax.random.randint(key_list[15], (REQS, PPR), 1, 65), jax.random.fold_in(key_list[15], 1), 1, 64).astype(jnp.int32),
        "recompute_index": draw_recompute_index(jax.random.fold_in(key_list[18], 71), 0),
        "prompt_lengths": draw_prompt_lengths(jax.random.fold_in(key_list[18], 71), 0),
    }


EPSILON = 1e-06
ROPE_THETA = 500000.0
MASKED_SCORE = -1e+30

def frequencies():
    indices = jnp.arange(HD // 2, dtype=jnp.float32)
    return jnp.exp(indices * (-2.0 * math.log(ROPE_THETA) / HD))

def rotate(values, angles):
    half_width = values.shape[-1] // 2
    cosine = jnp.cos(angles)[:, None, :]
    sine = jnp.sin(angles)[:, None, :]
    first = values[..., :half_width]
    second = values[..., half_width:]
    return jnp.concatenate([first * cosine - second * sine, second * cosine + first * sine], axis=-1)

def normalize(matrix):
    return matrix * lax.rsqrt(lax.optimization_barrier(jnp.mean(matrix * matrix, axis=-1, keepdims=True)) + EPSILON)

def layout(passage_order, separators, recompute_index, prompt_lengths, seq_count):
    request_count = seq_count // PPR
    ordering = passage_order.reshape(request_count, PPR)
    slot_ids = jnp.arange(PPR, dtype=jnp.int32)
    opening = (slot_ids[None, :] * PLEN + jnp.cumsum(separators, axis=1)).astype(jnp.int32)
    flattened = ordering.reshape(-1)
    starts = jnp.zeros((seq_count,), jnp.int32).at[flattened].set(opening.reshape(-1))
    request_ids = jnp.repeat(jnp.arange(request_count, dtype=jnp.int32), PPR)
    owners = jnp.zeros((seq_count,), jnp.int32).at[flattened].set(request_ids)
    prompt_start = (opening[:, PPR - 1] + PLEN).astype(jnp.int32)
    devices = jnp.arange(seq_count, dtype=jnp.int32)
    new_request = (devices // PPR).astype(jnp.int32)
    new_index = ((devices % PPR)[:, None] * TOKN_DEV + jnp.arange(TOKN_DEV, dtype=jnp.int32)[None, :]).astype(jnp.int32)
    new_positions = (prompt_start[new_request][:, None] + new_index).astype(jnp.int32)
    new_live = new_index < prompt_lengths[new_request][:, None]
    picked_positions = (starts[:, None] + recompute_index).astype(jnp.int32)
    row_positions = jnp.concatenate([picked_positions, new_positions], axis=1).reshape(-1)
    row_live = jnp.concatenate([jnp.ones(picked_positions.shape, bool), new_live], axis=1).reshape(-1)
    return (starts, owners, new_request, new_positions, new_live, row_positions, row_live)

def grouped_sum(left, right, groups):
    inner = left.shape[1] // groups
    left_blocks = left.reshape(left.shape[0], groups, inner).transpose(1, 0, 2)
    right_blocks = right.reshape(groups, inner, right.shape[1])

    def add_block(carry, operands):
        term = jnp.dot(operands[0], operands[1], preferred_element_type=jnp.float32).astype(jnp.bfloat16)
        return (carry + lax.optimization_barrier(term).astype(jnp.float32), None)
    summed, unused = lax.scan(add_block, jnp.zeros((left.shape[0], right.shape[1]), jnp.float32), (left_blocks, right_blocks))
    return summed

def reference(hidden_states, query_weight, key_weight, value_weight, output_weight, query_gain, key_gain, attention_gain, gate_weight, up_weight, down_weight, feedforward_gain, cached_keys, cached_values, passage_order, separators, recompute_index, prompt_lengths):
    width = HEADS * HD
    starts, owners, new_request, new_positions, new_live, row_positions, row_live = layout(passage_order, separators, recompute_index, prompt_lengths, N_SEQ)
    frequency = frequencies()
    query_raw = jnp.dot(hidden_states, query_weight, preferred_element_type=jnp.float32)
    key_raw = jnp.dot(hidden_states, key_weight, preferred_element_type=jnp.float32)
    value_raw = jnp.dot(hidden_states, value_weight, preferred_element_type=jnp.float32)
    angles = row_positions.astype(jnp.float32)[:, None] * frequency[None, :]
    query_scaled = query_raw * lax.rsqrt(lax.optimization_barrier(jnp.mean(query_raw * query_raw, axis=1, keepdims=True)) + EPSILON) * query_gain
    key_scaled = key_raw * lax.rsqrt(lax.optimization_barrier(jnp.mean(key_raw * key_raw, axis=1, keepdims=True)) + EPSILON) * key_gain
    query = rotate(query_scaled.reshape(ROWS, HEADS, HD), angles).reshape(ROWS, width).astype(jnp.bfloat16)
    key_rows = rotate(key_scaled.reshape(ROWS, HEADS, HD), angles).reshape(ROWS, width).astype(jnp.bfloat16)
    value_rows = value_raw.astype(jnp.bfloat16)

    def shift_passage(passage_cache, passage_start):
        turned = jnp.broadcast_to(passage_start.astype(jnp.float32) * frequency, (PLEN, HD // 2))
        return rotate(passage_cache.astype(jnp.float32).reshape(PLEN, HEADS, HD), turned).reshape(PLEN, width).astype(jnp.bfloat16)
    moved = jax.vmap(shift_passage)(cached_keys, starts)
    passage_ids = jnp.arange(PASSAGES, dtype=jnp.int32)
    device_keys = key_rows.reshape(N_SEQ, ROW_DEV, width)
    device_values = value_rows.reshape(N_SEQ, ROW_DEV, width)
    blended_keys = moved.at[passage_ids[:, None], recompute_index].set(device_keys[:, :SEL])
    blended_values = cached_values.at[passage_ids[:, None], recompute_index].set(device_values[:, :SEL])
    all_keys = jnp.concatenate([blended_keys.reshape(PASSAGES * PLEN, width), device_keys[:, SEL:].reshape(-1, width)], axis=0)
    all_values = jnp.concatenate([blended_values.reshape(PASSAGES * PLEN, width), device_values[:, SEL:].reshape(-1, width)], axis=0)
    key_positions = jnp.concatenate([(starts[:, None] + jnp.arange(PLEN, dtype=jnp.int32)[None, :]).reshape(-1), new_positions.reshape(-1)])
    key_requests = jnp.concatenate([jnp.repeat(owners, PLEN), jnp.repeat(new_request, TOKN_DEV)])
    key_live = jnp.concatenate([jnp.ones((PASSAGES * PLEN,), bool), new_live.reshape(-1)])
    row_requests = jnp.concatenate([jnp.broadcast_to(owners[:, None], (N_SEQ, SEL)), jnp.broadcast_to(new_request[:, None], (N_SEQ, TOKN_DEV))], axis=1).reshape(-1)
    visible = (row_requests[:, None] == key_requests[None, :]) & (key_positions[None, :] <= row_positions[:, None]) & key_live[None, :]

    def one_head(operands):
        head_query, head_key, head_value = operands
        scores = jnp.dot(head_query, head_key.T, preferred_element_type=jnp.float32) * HD ** (-0.5)
        masked = jnp.where(visible, scores, MASKED_SCORE)
        peaks = lax.optimization_barrier(jnp.max(masked, axis=1, keepdims=True))
        exponentials = jnp.where(visible, jnp.exp(masked - peaks), 0.0)
        weighted = jnp.dot(exponentials.astype(jnp.bfloat16), head_value, preferred_element_type=jnp.float32)
        return weighted / lax.optimization_barrier(jnp.sum(exponentials, axis=1, keepdims=True))
    heads_first = lax.map(one_head, (query.reshape(ROWS, HEADS, HD).transpose(1, 0, 2), all_keys.reshape(-1, HEADS, HD).transpose(1, 0, 2), all_values.reshape(-1, HEADS, HD).transpose(1, 0, 2)))
    attention = heads_first.transpose(1, 0, 2).reshape(ROWS, width).astype(jnp.bfloat16)
    summed = grouped_sum(attention, output_weight, N_BLK)
    mixed = (hidden_states.astype(jnp.float32) + normalize(summed) * attention_gain).astype(jnp.bfloat16)
    gate_values = jnp.dot(mixed, gate_weight, preferred_element_type=jnp.float32)
    up_values = jnp.dot(mixed, up_weight, preferred_element_type=jnp.float32)
    activation = (jax.nn.silu(gate_values) * up_values).astype(jnp.bfloat16)
    feedforward = grouped_sum(activation, down_weight, N_BLK)
    hidden_out = (mixed.astype(jnp.float32) + normalize(feedforward) * feedforward_gain).astype(jnp.bfloat16)
    return (hidden_out, blended_keys, blended_values)
```

```python
import math

import jax
import jax.numpy as jnp
from jax import lax
from jax.sharding import Mesh, PartitionSpec as P

HD = 128
PLEN = 1024
SEL = 96
PPR = 2
TOKN_DEV = 32
ROW_DEV = 128

EPSILON = 1e-06
ROPE_THETA = 500000.0
MASKED = -1e30

SEQ = ("y", "zh", "core")
BLK = ("zl", "x")
NY, NZH, NCORE, NZL, NX = 4, 2, 2, 8, 4
N_SEQ = NY * NZH * NCORE
bf16 = jnp.bfloat16
f32 = jnp.float32


def frequencies():
    indices = jnp.arange(HD // 2, dtype=f32)
    return jnp.exp(indices * (-2.0 * math.log(ROPE_THETA) / HD))


def rotate(values, cosine, sine):
    first = values[:, : HD // 2]
    second = values[:, HD // 2 :]
    return jnp.concatenate(
        [first * cosine - second * sine, second * cosine + first * sine], axis=-1
    )


def copies_to_all(a, axis, count):
    return lax.all_to_all(
        jnp.broadcast_to(a[None], (count,) + a.shape), axis, 0, 0, tiled=True
    )


def gather_seq(a):
    a = copies_to_all(a, "zh", NZH)
    a = copies_to_all(a, "y", NY)
    a = copies_to_all(a, "core", NCORE)
    return a.reshape((N_SEQ,) + a.shape[3:])


def seq_slot(s):
    return (s % 2) * 8 + (s // 4) * 2 + (s // 2) % 2


def swap(a, axis, count):
    return lax.ppermute(a, axis, [(i, i ^ 1) for i in range(count)])


def layout(passage_order, separators, recompute_index, prompt_lengths):
    requests = N_SEQ // PPR
    slot_ids = jnp.arange(PPR, dtype=jnp.int32)
    opening = slot_ids[None, :] * PLEN + jnp.cumsum(separators, axis=1)
    flat = passage_order.reshape(-1)
    hit = flat[None, :] == jnp.arange(N_SEQ, dtype=jnp.int32)[:, None]
    starts = jnp.sum(jnp.where(hit, opening.reshape(-1)[None, :], 0), axis=1)
    place = jnp.sum(jnp.where(hit, jnp.arange(N_SEQ, dtype=jnp.int32)[None, :], 0), axis=1)
    owners = place // PPR
    prompt_start = opening[:, PPR - 1] + PLEN
    new_index = jnp.arange(PPR * TOKN_DEV, dtype=jnp.int32)
    new_positions = (prompt_start[:, None] + new_index[None, :]).reshape(N_SEQ, TOKN_DEV)
    new_live = (new_index[None, :] < prompt_lengths[:, None]).reshape(N_SEQ, TOKN_DEV)
    picked = starts[:, None] + recompute_index
    positions = jnp.concatenate([picked, new_positions], axis=1)
    return starts, owners, positions, new_live


def partial_attention(queries, keys, values, visible):
    scores = lax.dot_general(
        queries, keys, (((1,), (1,)), ((), ())), preferred_element_type=f32
    ) * HD ** (-0.5)
    scores = jnp.where(visible, scores, MASKED)
    peak = jnp.max(scores, axis=1, keepdims=True)
    weights = jnp.where(visible, jnp.exp(scores - peak), 0.0)
    total = jnp.sum(weights, axis=1, keepdims=True)
    some = total > 0.0
    safe = jnp.where(some, total, 1.0)
    out = jnp.dot(weights.astype(bf16), values, preferred_element_type=f32) / safe
    return out, jnp.where(some, peak + jnp.log(safe), MASKED)


def merge(parts):
    top = parts[0][1]
    for _, level in parts[1:]:
        top = jnp.maximum(top, level)
    num = 0.0
    den = 0.0
    for out, level in parts:
        w = jnp.exp(level - top)
        num = num + w * out
        den = den + w
    return num / den


def pack(out, level):
    high = lax.reduce_precision(level, 8, 7)
    rest = level - high
    mid = lax.reduce_precision(rest, 8, 7)
    low = rest - mid
    tail = jnp.zeros((out.shape[0], HD - 3), f32)
    return jnp.concatenate([out, high, mid, low, tail], axis=1).astype(bf16)


def unpack(block):
    block = block.astype(f32)
    level = block[:, HD : HD + 1] + block[:, HD + 1 : HD + 2] + block[:, HD + 2 : HD + 3]
    return block[:, :HD], level


def shards(
    hidden_states,
    query_weight,
    key_weight,
    value_weight,
    output_weight,
    query_gain,
    key_gain,
    attention_gain,
    gate_weight,
    up_weight,
    down_weight,
    feedforward_gain,
    cached_keys,
    cached_values,
    passage_order,
    separators,
    recompute_index,
    prompt_lengths,
):
    zh = lax.axis_index("zh")
    core = lax.axis_index("core")
    zl = lax.axis_index("zl")
    x_at = lax.axis_index("x")
    seq = lax.axis_index("y") * 4 + zh * 2 + core
    width = query_weight.shape[1]
    hidden_units = gate_weight.shape[1]
    model = hidden_states.shape[1]
    depth = query_weight.shape[0]

    out_all = lax.all_gather(output_weight.T, SEQ, axis=0, tiled=True)
    pad = (-hidden_units) % 128
    ff_mine = jnp.concatenate(
        [jnp.pad(down_weight.T, ((0, 0), (0, pad))), gate_weight, up_weight], axis=1
    )
    ff_all = lax.all_gather(ff_mine, SEQ, axis=0, tiled=True)
    up_from = hidden_units + pad

    mine = jnp.concatenate([query_weight, key_weight, value_weight], axis=1)
    theirs = swap(mine, "zh", NZH)
    near = copies_to_all(mine, "y", NY)
    near_other = swap(near, "core", NCORE)
    far = copies_to_all(theirs, "y", NY)
    far_other = swap(far, "core", NCORE)

    columns = hidden_states.reshape(ROW_DEV, NY, NZH, NCORE, depth)

    def block(i, j):
        return columns[:, :, i, j].reshape(ROW_DEV, NY * depth)

    by_zh = [
        [jnp.where(zh == 0, block(i, j), block(1 - i, j)) for j in range(2)] for i in range(2)
    ]
    picked_x = [
        [jnp.where(core == 0, by_zh[i][j], by_zh[i][1 - j]) for j in range(2)] for i in range(2)
    ]

    def product(x, w):
        return jnp.dot(x, w.reshape(NY * depth, 3 * width), preferred_element_type=f32)

    raw = product(picked_x[0][0], near) + product(picked_x[0][1], near_other)
    raw = raw + product(picked_x[1][0], far) + product(picked_x[1][1], far_other)
    query_raw, key_raw, value_raw = (raw[:, i * width : (i + 1) * width] for i in range(3))

    starts, owners, positions, new_live = layout(
        passage_order, separators, recompute_index, prompt_lengths
    )
    frequency = frequencies()
    my_positions = lax.dynamic_index_in_dim(positions, seq, 0, False)
    angles = my_positions.astype(f32)[:, None] * frequency[None, :]
    cosine, sine = jnp.cos(angles), jnp.sin(angles)
    start = lax.dynamic_index_in_dim(starts, seq, 0, False)
    turn = (start.astype(f32) * frequency)[None, :]
    moved = rotate(cached_keys[0].astype(f32), jnp.cos(turn), jnp.sin(turn)).astype(bf16)

    squares = jnp.stack(
        [jnp.sum(query_raw * query_raw, axis=1), jnp.sum(key_raw * key_raw, axis=1)]
    )
    squares = lax.all_to_all(
        jnp.broadcast_to(squares[None], (NZL * NX,) + squares.shape), BLK, 0, 0, tiled=True
    )
    squares = jnp.sum(squares, axis=0)
    scale = lax.rsqrt(squares / model + EPSILON)
    query = rotate(query_raw * scale[0][:, None] * query_gain, cosine, sine).astype(bf16)
    key = rotate(key_raw * scale[1][:, None] * key_gain, cosine, sine).astype(bf16)
    value = value_raw.astype(bf16)

    picked = lax.dynamic_index_in_dim(recompute_index, seq, 0, False)
    passage_keys = moved.at[picked].set(key[:SEL], unique_indices=True)
    passage_values = cached_values[0].at[picked].set(value[:SEL], unique_indices=True)

    request = lax.dynamic_index_in_dim(owners, seq, 0, False)
    order = passage_order.reshape(-1, PPR)
    chosen = lax.dynamic_index_in_dim(order, request, 0, False)
    all_queries = gather_seq(query)

    def rows_of(table, s):
        return lax.dynamic_index_in_dim(table, s, 0, False)

    sources = [chosen[0], chosen[1], request * 2, request * 2 + 1]
    cuts = [slice(0, SEL), slice(0, SEL), slice(SEL, None), slice(SEL, None)]
    wanted = jnp.concatenate(
        [rows_of(all_queries, seq_slot(s))[c] for s, c in zip(sources, cuts)]
    )
    wanted_at = jnp.concatenate([rows_of(positions, s)[c] for s, c in zip(sources, cuts)])
    key_at = start + jnp.arange(PLEN, dtype=jnp.int32)
    part, level = partial_attention(
        wanted, passage_keys, passage_values, key_at[None, :] <= wanted_at[:, None]
    )

    new_mine = jnp.concatenate([key[SEL:], value[SEL:]])
    new_other = swap(new_mine, "core", NCORE)
    new_keys = jnp.concatenate([key[SEL:], new_other[:TOKN_DEV]])
    new_values = jnp.concatenate([value[SEL:], new_other[TOKN_DEV:]])
    partner = seq + 1 - 2 * core
    new_at = jnp.concatenate([my_positions[SEL:], rows_of(positions, partner)[SEL:]])
    live = jnp.concatenate([rows_of(new_live, seq), rows_of(new_live, partner)])
    new_part = partial_attention(
        query[SEL:],
        new_keys,
        new_values,
        (new_at[None, :] <= my_positions[SEL:][:, None]) & live[None, :],
    )

    returned = gather_seq(pack(part[SEL:], level[SEL:]))
    first = chosen[0] == seq
    own = (
        jnp.where(first, part[:SEL], part[SEL : 2 * SEL]),
        jnp.where(first, level[:SEL], level[SEL : 2 * SEL]),
    )
    remote, remote_level = unpack(rows_of(returned, seq_slot(chosen[0]))[:SEL])
    old_rows = merge([own, (remote, jnp.where(first, MASKED, remote_level))])
    my_order = rows_of(order, seq // 2)
    parts = [new_part]
    for i in range(PPR):
        theirs_back = rows_of(returned, seq_slot(my_order[i]))
        parts.append(
            unpack(
                jnp.where(
                    core == 0,
                    theirs_back[SEL : SEL + TOKN_DEV],
                    theirs_back[SEL + TOKN_DEV : SEL + 2 * TOKN_DEV],
                )
            )
        )
    attention = jnp.concatenate([old_rows, merge(parts)]).astype(bf16)

    blocks = NX * NZL
    out_blocks = out_all.reshape(blocks, model // blocks, width)
    terms = jnp.einsum("rk,bck->brc", attention, out_blocks, preferred_element_type=f32)
    terms = terms.astype(bf16).reshape(NX, NZL, ROW_DEV, model // blocks)
    terms = lax.all_to_all(terms, "x", 0, 0, tiled=True)
    terms = jnp.sum(terms.astype(f32), axis=0).astype(bf16)
    terms = lax.all_to_all(terms, "zl", 0, 0, tiled=True)
    summed = jnp.sum(terms.astype(f32), axis=0).astype(bf16)
    summed = copies_to_all(summed, "zl", NZL)
    summed = copies_to_all(summed, "x", NX).reshape(blocks, ROW_DEV, model // blocks)
    summed = summed.transpose(1, 0, 2).reshape(ROW_DEV, model).astype(f32)
    norm = lax.rsqrt(jnp.mean(summed * summed, axis=1, keepdims=True) + EPSILON)
    mixed = (hidden_states.astype(f32) + summed * norm * attention_gain).astype(bf16)

    both = jnp.dot(mixed, ff_all[:, up_from:], preferred_element_type=f32)
    gate_values, up_values = both[:, :hidden_units], both[:, hidden_units:]
    activation = (jax.nn.silu(gate_values) * up_values).astype(bf16)
    rows = ROW_DEV // blocks
    activation = (
        activation.reshape(NZL, NX, rows, hidden_units)
        .transpose(1, 0, 2, 3)
        .reshape(ROW_DEV, hidden_units)
    )
    terms = lax.dot_general(
        activation,
        ff_all[:, :hidden_units],
        (((1,), (1,)), ((), ())),
        preferred_element_type=f32,
    ).astype(bf16)
    terms = lax.all_to_all(terms.reshape(NX, NZL * rows, model), "x", 0, 0, tiled=True)
    terms = jnp.sum(terms.astype(f32), axis=0).astype(bf16)
    terms = lax.all_to_all(terms.reshape(NZL, rows, model), "zl", 0, 0, tiled=True)
    total = jnp.sum(terms.astype(f32), axis=0)
    norm = lax.rsqrt(jnp.mean(total * total, axis=1, keepdims=True) + EPSILON)
    my_rows = lax.dynamic_slice_in_dim(mixed, (zl * NX + x_at) * rows, rows, 0)
    hidden_out = (my_rows.astype(f32) + total * norm * feedforward_gain).astype(bf16)
    return (hidden_out, passage_keys[None], passage_values[None])


def solution(mesh):
    fine = Mesh(
        mesh.devices.reshape(NY, NZH, NCORE, NZL, NX), ("y", "zh", "core", "zl", "x")
    )
    by_both = P(SEQ, BLK)
    return jax.shard_map(
        shards,
        mesh=fine,
        in_specs=(
            P(SEQ, None),
            by_both,
            by_both,
            by_both,
            P(BLK, SEQ),
            P(BLK),
            P(BLK),
            P(),
            by_both,
            by_both,
            P(BLK, SEQ),
            P(),
            P(SEQ, None, BLK),
            P(SEQ, None, BLK),
            P(),
            P(),
            P(),
            P(),
        ),
        out_specs=(P(SEQ + BLK, None), P(SEQ, None, BLK), P(SEQ, None, BLK)),
        check_vma=False,
    )
```

```python
import math

import jax
import jax.numpy as jnp
from jax import lax
from jax.experimental import pallas as pl
from jax.experimental.pallas import tpu as pltpu
from jax.sharding import Mesh, PartitionSpec as P

HD = 128
PLEN = 1024
SEL = 96
PPR = 2
TOKN_DEV = 32
ROW_DEV = 128

EPSILON = 1e-06
ROPE_THETA = 500000.0
MASKED = -1e30

SEQ = ("y", "zh", "core")
BLK = ("zl", "x")
NY, NZH, NCORE, NZL, NX = 4, 2, 2, 8, 4
N_SEQ = NY * NZH * NCORE
bf16 = jnp.bfloat16
f32 = jnp.float32


def frequencies():
    indices = jnp.arange(HD // 2, dtype=f32)
    return jnp.exp(indices * (-2.0 * math.log(ROPE_THETA) / HD))


def rotate(values, cosine, sine):
    first = values[:, : HD // 2]
    second = values[:, HD // 2 :]
    return jnp.concatenate(
        [first * cosine - second * sine, second * cosine + first * sine], axis=-1
    )


def copies_to_all(a, axis, count):
    return lax.all_to_all(
        jnp.broadcast_to(a[None], (count,) + a.shape), axis, 0, 0, tiled=True
    )


def gather_seq(a):
    a = copies_to_all(a, "zh", NZH)
    a = copies_to_all(a, "y", NY)
    a = copies_to_all(a, "core", NCORE)
    return a.reshape((N_SEQ,) + a.shape[3:])


def seq_slot(s):
    return (s % 2) * 8 + (s // 4) * 2 + (s // 2) % 2


def swap(a, axis, count):
    return lax.ppermute(a, axis, [(i, i ^ 1) for i in range(count)])


def layout(passage_order, separators, recompute_index, prompt_lengths):
    requests = N_SEQ // PPR
    slot_ids = jnp.arange(PPR, dtype=jnp.int32)
    opening = slot_ids[None, :] * PLEN + jnp.cumsum(separators, axis=1)
    flat = passage_order.reshape(-1)
    hit = flat[None, :] == jnp.arange(N_SEQ, dtype=jnp.int32)[:, None]
    starts = jnp.sum(jnp.where(hit, opening.reshape(-1)[None, :], 0), axis=1)
    place = jnp.sum(jnp.where(hit, jnp.arange(N_SEQ, dtype=jnp.int32)[None, :], 0), axis=1)
    owners = place // PPR
    prompt_start = opening[:, PPR - 1] + PLEN
    new_index = jnp.arange(PPR * TOKN_DEV, dtype=jnp.int32)
    new_positions = (prompt_start[:, None] + new_index[None, :]).reshape(N_SEQ, TOKN_DEV)
    new_live = (new_index[None, :] < prompt_lengths[:, None]).reshape(N_SEQ, TOKN_DEV)
    picked = starts[:, None] + recompute_index
    positions = jnp.concatenate([picked, new_positions], axis=1)
    return starts, owners, positions, new_live


def partial_attention(queries, keys, values, visible):
    scores = lax.dot_general(
        queries, keys, (((1,), (1,)), ((), ())), preferred_element_type=f32
    ) * HD ** (-0.5)
    scores = jnp.where(visible, scores, MASKED)
    peak = jnp.max(scores, axis=1, keepdims=True)
    weights = jnp.where(visible, jnp.exp(scores - peak), 0.0)
    total = jnp.sum(weights, axis=1, keepdims=True)
    some = total > 0.0
    safe = jnp.where(some, total, 1.0)
    out = jnp.dot(weights.astype(bf16), values, preferred_element_type=f32) / safe
    return out, jnp.where(some, peak + jnp.log(safe), MASKED)


def merge(parts):
    top = parts[0][1]
    for _, level in parts[1:]:
        top = jnp.maximum(top, level)
    num = 0.0
    den = 0.0
    for out, level in parts:
        w = jnp.exp(level - top)
        num = num + w * out
        den = den + w
    return num / den


def pack(out, level):
    high = lax.reduce_precision(level, 8, 7)
    rest = level - high
    mid = lax.reduce_precision(rest, 8, 7)
    low = rest - mid
    tail = jnp.zeros((out.shape[0], HD - 3), f32)
    return jnp.concatenate([out, high, mid, low, tail], axis=1).astype(bf16)


def unpack(block):
    block = block.astype(f32)
    level = block[:, HD : HD + 1] + block[:, HD + 1 : HD + 2] + block[:, HD + 2 : HD + 3]
    return block[:, :HD], level


def merge_and_project(control, own, new_part, returned, later):
    own_out, own_level = own
    new_out, new_level = new_part
    width = own_out.shape[1]
    blocks = later.shape[0] // width

    def kernel(c_ref, own_ref, own_l_ref, new_ref, new_l_ref, back_ref, w_ref, out_ref, att_ref):
        remote, remote_level = unpack(back_ref[c_ref[0], :SEL, :])
        remote_level = jnp.where(c_ref[4] == 1, MASKED, remote_level)
        att_ref[:SEL, :] = merge([(own_ref[...], own_l_ref[...]), (remote, remote_level)])
        at = pl.multiple_of(SEL + c_ref[3] * TOKN_DEV, TOKN_DEV)
        parts = [(new_ref[...], new_l_ref[...])]
        for i in range(PPR):
            parts.append(unpack(back_ref[c_ref[1 + i], pl.ds(at, TOKN_DEV), :]))
        att_ref[SEL:, :] = merge(parts)
        attention = att_ref[...].astype(bf16)
        for b in range(blocks):
            out_ref[b] = lax.dot_general(
                attention,
                w_ref[b * width : (b + 1) * width, :],
                (((1,), (1,)), ((), ())),
                preferred_element_type=f32,
            ).astype(bf16)

    def whole(a):
        return pl.BlockSpec(a.shape, lambda i: (0,) * a.ndim)

    return pl.pallas_call(
        kernel,
        grid=(1,),
        out_shape=jax.ShapeDtypeStruct((blocks, ROW_DEV, width), bf16),
        in_specs=[
            pl.BlockSpec(memory_space=pltpu.SMEM),
            whole(own_out),
            whole(own_level),
            whole(new_out),
            whole(new_level),
            whole(returned),
            pl.BlockSpec((later.shape[0], width), lambda i: (0, 0)),
        ],
        out_specs=pl.BlockSpec((blocks, ROW_DEV, width), lambda i: (0, 0, 0)),
        scratch_shapes=[pltpu.VMEM((ROW_DEV, width), f32)],
        compiler_params=pltpu.CompilerParams(vmem_limit_bytes=24 << 20),
        name="merge_and_project",
    )(control, own_out, own_level, new_out, new_level, returned, later)


def feed_forward(summed, hidden, gain, later, width, units):
    blocks, rows, part = summed.shape
    model = blocks * part
    steps = 8
    chunk = model // steps
    each = chunk // part
    down_from, gate_from = width, width + units
    per = rows // (NZL * NX)

    def kernel(s_ref, x_ref, g_ref, w_ref, out_ref, mixed_ref, norm_ref, acc_ref, down_ref):
        k = pl.program_id(0)

        @pl.when(k == 0)
        def _():
            squares = jnp.zeros((rows, part), f32)
            for b in range(blocks):
                block = s_ref[b].astype(f32)
                squares = squares + block * block
            norm_ref[...] = lax.rsqrt(
                jnp.sum(squares, axis=1, keepdims=True) / model + EPSILON
            )
            acc_ref[...] = jnp.zeros_like(acc_ref)

        for j in range(each):
            cols = slice(j * part, (j + 1) * part)
            mixed_ref[:, cols] = (
                x_ref[:, cols].astype(f32)
                + s_ref[k * each + j].astype(f32) * norm_ref[...] * g_ref[:, cols]
            ).astype(bf16)
        acc_ref[...] += jnp.dot(
            mixed_ref[...], w_ref[:, gate_from:], preferred_element_type=f32
        )
        down_ref[k] = w_ref[:, down_from:gate_from]

        @pl.when(k == steps - 1)
        def _():
            gate, up = acc_ref[:, :units], acc_ref[:, units:]
            activation = (gate / (1.0 + jnp.exp(-gate)) * up).astype(bf16)
            to = lax.broadcasted_iota(jnp.int32, (rows, rows), 0)
            at = lax.broadcasted_iota(jnp.int32, (rows, rows), 1)
            source = (to // per) % NZL * (NX * per) + to // (NZL * per) * per + to % per
            move = jnp.where(at == source, 1.0, 0.0).astype(bf16)
            activation = jnp.dot(move, activation, preferred_element_type=f32).astype(bf16)
            for c in range(steps):
                out_ref[:, c * chunk : (c + 1) * chunk] = lax.dot_general(
                    activation,
                    down_ref[c],
                    (((1,), (1,)), ((), ())),
                    preferred_element_type=f32,
                ).astype(bf16)

    return pl.pallas_call(
        kernel,
        grid=(steps,),
        out_shape=(
            jax.ShapeDtypeStruct((rows, model), bf16),
            jax.ShapeDtypeStruct((rows, model), bf16),
        ),
        in_specs=[
            pl.BlockSpec((blocks, rows, part), lambda k: (0, 0, 0)),
            pl.BlockSpec((rows, chunk), lambda k: (0, k)),
            pl.BlockSpec((1, chunk), lambda k: (0, k)),
            pl.BlockSpec((chunk, later.shape[1]), lambda k: (k, 0)),
        ],
        out_specs=(
            pl.BlockSpec((rows, model), lambda k: (0, 0)),
            pl.BlockSpec((rows, chunk), lambda k: (0, k)),
        ),
        scratch_shapes=[
            pltpu.VMEM((rows, 1), f32),
            pltpu.VMEM((rows, 2 * units), f32),
            pltpu.VMEM((steps, chunk, units), bf16),
        ],
        compiler_params=pltpu.CompilerParams(vmem_limit_bytes=32 << 20),
        name="feed_forward",
    )(summed, hidden, gain, later)


def shards(
    hidden_states,
    query_weight,
    key_weight,
    value_weight,
    output_weight,
    query_gain,
    key_gain,
    attention_gain,
    gate_weight,
    up_weight,
    down_weight,
    feedforward_gain,
    cached_keys,
    cached_values,
    passage_order,
    separators,
    recompute_index,
    prompt_lengths,
):
    zh = lax.axis_index("zh")
    core = lax.axis_index("core")
    zl = lax.axis_index("zl")
    x_at = lax.axis_index("x")
    seq = lax.axis_index("y") * 4 + zh * 2 + core
    width = query_weight.shape[1]
    hidden_units = gate_weight.shape[1]
    model = hidden_states.shape[1]
    depth = query_weight.shape[0]

    pad = (-hidden_units) % 128
    later = lax.all_gather(
        jnp.concatenate(
            [
                output_weight.T,
                jnp.pad(down_weight.T, ((0, 0), (0, pad))),
                jnp.pad(gate_weight, ((0, 0), (0, pad))),
                jnp.pad(up_weight, ((0, 0), (0, pad))),
            ],
            axis=1,
        ),
        SEQ,
        axis=0,
        tiled=True,
    )

    mine = jnp.concatenate([query_weight, key_weight, value_weight], axis=1)
    theirs = swap(mine, "zh", NZH)
    starts, owners, positions, new_live = layout(
        passage_order, separators, recompute_index, prompt_lengths
    )
    frequency = frequencies()
    my_positions = lax.dynamic_index_in_dim(positions, seq, 0, False)
    angles = my_positions.astype(f32)[:, None] * frequency[None, :]
    cosine, sine = jnp.cos(angles), jnp.sin(angles)
    start = lax.dynamic_index_in_dim(starts, seq, 0, False)
    turn = (start.astype(f32) * frequency)[None, :]
    moved = rotate(cached_keys[0].astype(f32), jnp.cos(turn), jnp.sin(turn)).astype(bf16)
    near = copies_to_all(mine, "y", NY)
    theirs, cosine, sine, moved = lax.optimization_barrier((theirs, cosine, sine, moved))
    near_other = swap(near, "core", NCORE)
    far = copies_to_all(theirs, "y", NY)
    far_other = swap(far, "core", NCORE)

    columns = hidden_states.reshape(ROW_DEV, NY, NZH, NCORE, depth)

    def block(i, j):
        return columns[:, :, i, j].reshape(ROW_DEV, NY * depth)

    by_zh = [
        [jnp.where(zh == 0, block(i, j), block(1 - i, j)) for j in range(2)] for i in range(2)
    ]
    picked_x = [
        [jnp.where(core == 0, by_zh[i][j], by_zh[i][1 - j]) for j in range(2)] for i in range(2)
    ]

    def product(x, w):
        return jnp.dot(x, w.reshape(NY * depth, 3 * width), preferred_element_type=f32)

    raw = product(picked_x[0][0], near) + product(picked_x[0][1], near_other)
    raw = raw + product(picked_x[1][0], far) + product(picked_x[1][1], far_other)
    query_raw, key_raw, value_raw = (raw[:, i * width : (i + 1) * width] for i in range(3))

    squares = jnp.stack(
        [jnp.sum(query_raw * query_raw, axis=1), jnp.sum(key_raw * key_raw, axis=1)]
    )
    squares = lax.all_to_all(
        jnp.broadcast_to(squares[None], (NZL * NX,) + squares.shape), BLK, 0, 0, tiled=True
    )
    squares = jnp.sum(squares, axis=0)
    scale = lax.rsqrt(squares / model + EPSILON)
    query = rotate(query_raw * scale[0][:, None] * query_gain, cosine, sine).astype(bf16)
    key = rotate(key_raw * scale[1][:, None] * key_gain, cosine, sine).astype(bf16)
    value = value_raw.astype(bf16)

    picked = lax.dynamic_index_in_dim(recompute_index, seq, 0, False)
    passage_keys = moved.at[picked].set(key[:SEL], unique_indices=True)
    passage_values = cached_values[0].at[picked].set(value[:SEL], unique_indices=True)

    request = lax.dynamic_index_in_dim(owners, seq, 0, False)
    order = passage_order.reshape(-1, PPR)
    chosen = lax.dynamic_index_in_dim(order, request, 0, False)
    all_queries = gather_seq(query)

    def rows_of(table, s):
        return lax.dynamic_index_in_dim(table, s, 0, False)

    sources = [chosen[0], chosen[1], request * 2, request * 2 + 1]
    cuts = [slice(0, SEL), slice(0, SEL), slice(SEL, None), slice(SEL, None)]
    wanted = jnp.concatenate(
        [rows_of(all_queries, seq_slot(s))[c] for s, c in zip(sources, cuts)]
    )
    wanted_at = jnp.concatenate([rows_of(positions, s)[c] for s, c in zip(sources, cuts)])
    key_at = start + jnp.arange(PLEN, dtype=jnp.int32)
    part, level = partial_attention(
        wanted, passage_keys, passage_values, key_at[None, :] <= wanted_at[:, None]
    )

    new_mine = jnp.concatenate([key[SEL:], value[SEL:]])
    new_other = swap(new_mine, "core", NCORE)
    new_keys = jnp.concatenate([key[SEL:], new_other[:TOKN_DEV]])
    new_values = jnp.concatenate([value[SEL:], new_other[TOKN_DEV:]])
    partner = seq + 1 - 2 * core
    new_at = jnp.concatenate([my_positions[SEL:], rows_of(positions, partner)[SEL:]])
    live = jnp.concatenate([rows_of(new_live, seq), rows_of(new_live, partner)])
    new_part = partial_attention(
        query[SEL:],
        new_keys,
        new_values,
        (new_at[None, :] <= my_positions[SEL:][:, None]) & live[None, :],
    )

    returned = gather_seq(pack(part[SEL:], level[SEL:]))
    first = chosen[0] == seq
    own = (
        jnp.where(first, part[:SEL], part[SEL : 2 * SEL]),
        jnp.where(first, level[:SEL], level[SEL : 2 * SEL]),
    )
    my_order = rows_of(order, seq // 2)
    control = jnp.stack(
        [seq_slot(chosen[0]), seq_slot(my_order[0]), seq_slot(my_order[1]), core, first]
    ).astype(jnp.int32)

    blocks = NX * NZL
    terms = merge_and_project(control, own, new_part, returned, later)
    terms = lax.all_to_all(terms.reshape(NX, NZL, ROW_DEV, width), "x", 0, 0, tiled=True)
    terms = jnp.sum(terms.astype(f32), axis=0).astype(bf16)
    terms = lax.all_to_all(terms, "zl", 0, 0, tiled=True)
    summed = jnp.sum(terms.astype(f32), axis=0).astype(bf16)
    summed = copies_to_all(summed, "zl", NZL)
    summed = copies_to_all(summed, "x", NX).reshape(blocks, ROW_DEV, model // blocks)

    rows = ROW_DEV // blocks
    terms, mixed = feed_forward(
        summed, hidden_states, attention_gain[None], later, width, hidden_units + pad
    )
    terms = lax.all_to_all(terms.reshape(NX, NZL * rows, model), "x", 0, 0, tiled=True)
    terms = jnp.sum(terms.astype(f32), axis=0).astype(bf16)
    terms = lax.all_to_all(terms.reshape(NZL, rows, model), "zl", 0, 0, tiled=True)
    total = jnp.sum(terms.astype(f32), axis=0)
    norm = lax.rsqrt(jnp.mean(total * total, axis=1, keepdims=True) + EPSILON)
    my_rows = lax.dynamic_slice_in_dim(mixed, (zl * NX + x_at) * rows, rows, 0)
    hidden_out = (my_rows.astype(f32) + total * norm * feedforward_gain).astype(bf16)
    return (hidden_out, passage_keys[None], passage_values[None])


def solution(mesh):
    fine = Mesh(
        mesh.devices.reshape(NY, NZH, NCORE, NZL, NX), ("y", "zh", "core", "zl", "x")
    )
    by_both = P(SEQ, BLK)
    return jax.shard_map(
        shards,
        mesh=fine,
        in_specs=(
            P(SEQ, None),
            by_both,
            by_both,
            by_both,
            P(BLK, SEQ),
            P(BLK),
            P(BLK),
            P(),
            by_both,
            by_both,
            P(BLK, SEQ),
            P(),
            P(SEQ, None, BLK),
            P(SEQ, None, BLK),
            P(),
            P(),
            P(),
            P(),
        ),
        out_specs=(P(SEQ + BLK, None), P(SEQ, None, BLK), P(SEQ, None, BLK)),
        check_vma=False,
    )
```

```python
import functools
import math

import jax
import jax.numpy as jnp
from jax import lax
from jax.experimental import pallas as pl
from jax.experimental.pallas import tpu as pltpu
from jax.sharding import Mesh, PartitionSpec as P

HD = 128
PLEN = 1024
SEL = 96
PPR = 2
TOKN_DEV = 32
ROW_DEV = 128

EPSILON = 1e-06
ROPE_THETA = 500000.0
MASKED = -1e30

SEQ = ("y", "zh", "core")
BLK = ("zl", "x")
NY, NZH, NCORE, NZL, NX = 4, 2, 2, 8, 4
N_SEQ = NY * NZH * NCORE
bf16 = jnp.bfloat16
f32 = jnp.float32


def frequencies():
    indices = jnp.arange(HD // 2, dtype=f32)
    return jnp.exp(indices * (-2.0 * math.log(ROPE_THETA) / HD))


def rotate(values, cosine, sine):
    first = values[:, : HD // 2]
    second = values[:, HD // 2 :]
    return jnp.concatenate(
        [first * cosine - second * sine, second * cosine + first * sine], axis=-1
    )


def copies_to_all(a, axis, count):
    return lax.all_to_all(
        jnp.broadcast_to(a[None], (count,) + a.shape), axis, 0, 0, tiled=True
    )


def gather_seq(a):
    a = copies_to_all(a, "zh", NZH)
    a = copies_to_all(a, "y", NY)
    a = copies_to_all(a, "core", NCORE)
    return a.reshape((N_SEQ,) + a.shape[3:])


def own_first(blocks, zh, core):
    by_zh = [
        [jnp.where(zh == 0, blocks[i][j], blocks[1 - i][j]) for j in range(2)] for i in range(2)
    ]
    return [
        [jnp.where(core == 0, by_zh[i][j], by_zh[i][1 - j]) for j in range(2)] for i in range(2)
    ]


def seq_slot(s):
    return (s % 2) * 8 + (s // 4) * 2 + (s // 2) % 2


def swap(a, axis, count):
    return lax.ppermute(a, axis, [(i, i ^ 1) for i in range(count)])


def layout(passage_order, separators, recompute_index, prompt_lengths):
    requests = N_SEQ // PPR
    slot_ids = jnp.arange(PPR, dtype=jnp.int32)
    opening = slot_ids[None, :] * PLEN + jnp.cumsum(separators, axis=1)
    flat = passage_order.reshape(-1)
    hit = flat[None, :] == jnp.arange(N_SEQ, dtype=jnp.int32)[:, None]
    starts = jnp.sum(jnp.where(hit, opening.reshape(-1)[None, :], 0), axis=1)
    place = jnp.sum(jnp.where(hit, jnp.arange(N_SEQ, dtype=jnp.int32)[None, :], 0), axis=1)
    owners = place // PPR
    prompt_start = opening[:, PPR - 1] + PLEN
    new_index = jnp.arange(PPR * TOKN_DEV, dtype=jnp.int32)
    new_positions = (prompt_start[:, None] + new_index[None, :]).reshape(N_SEQ, TOKN_DEV)
    new_live = (new_index[None, :] < prompt_lengths[:, None]).reshape(N_SEQ, TOKN_DEV)
    picked = starts[:, None] + recompute_index
    positions = jnp.concatenate([picked, new_positions], axis=1)
    return starts, owners, positions, new_live


def partial_attention(queries, keys, values, visible):
    scores = lax.dot_general(
        queries, keys, (((1,), (1,)), ((), ())), preferred_element_type=f32
    ) * HD ** (-0.5)
    scores = jnp.where(visible, scores, MASKED)
    peak = jnp.max(scores, axis=1, keepdims=True)
    weights = jnp.where(visible, jnp.exp(scores - peak), 0.0)
    total = jnp.sum(weights, axis=1, keepdims=True)
    some = total > 0.0
    safe = jnp.where(some, total, 1.0)
    out = jnp.dot(weights.astype(bf16), values, preferred_element_type=f32) / safe
    return out, jnp.where(some, peak + jnp.log(safe), MASKED)


def merge(parts):
    top = parts[0][1]
    for _, level in parts[1:]:
        top = jnp.maximum(top, level)
    num = 0.0
    den = 0.0
    for out, level in parts:
        w = jnp.exp(level - top)
        num = num + w * out
        den = den + w
    return num / den


def pack(out, level):
    high = lax.reduce_precision(level, 8, 7)
    rest = level - high
    mid = lax.reduce_precision(rest, 8, 7)
    low = rest - mid
    tail = jnp.zeros((out.shape[0], HD - 3), f32)
    return jnp.concatenate([out, high, mid, low, tail], axis=1).astype(bf16)


def unpack(block):
    block = block.astype(f32)
    level = block[:, HD : HD + 1] + block[:, HD + 1 : HD + 2] + block[:, HD + 2 : HD + 3]
    return block[:, :HD], level


def merge_and_project(control, own, new_part, returned, weights):
    own_out, own_level = own
    new_out, new_level = new_part
    width = own_out.shape[1]
    count, part, _ = weights[0].shape
    halves = part // width
    blocks = len(weights) * count * halves

    def kernel(c_ref, own_ref, own_l_ref, new_ref, new_l_ref, back_ref, *refs):
        weight_refs, (out_ref, att_ref) = refs[:-2], refs[-2:]
        remote, remote_level = unpack(back_ref[c_ref[0], :SEL, :])
        remote_level = jnp.where(c_ref[4] == 1, MASKED, remote_level)
        att_ref[:SEL, :] = merge([(own_ref[...], own_l_ref[...]), (remote, remote_level)])
        at = pl.multiple_of(SEL + c_ref[3] * TOKN_DEV, TOKN_DEV)
        parts = [(new_ref[...], new_l_ref[...])]
        for i in range(PPR):
            parts.append(unpack(back_ref[c_ref[1 + i], pl.ds(at, TOKN_DEV), :]))
        att_ref[SEL:, :] = merge(parts)
        attention = att_ref[...].astype(bf16)
        for j, ref in enumerate(weight_refs):
            for n in range(count):
                term = lax.dot_general(
                    attention, ref[n], (((1,), (1,)), ((), ())), preferred_element_type=f32
                ).astype(bf16)
                for h in range(halves):
                    out_ref[(j * count + n) * halves + h] = term[:, h * width : (h + 1) * width]

    def whole(a):
        return pl.BlockSpec(a.shape, lambda i: (0,) * a.ndim)

    out_weights = pl.BlockSpec((count, part, width), lambda i: (0, 0, 3))
    return pl.pallas_call(
        kernel,
        grid=(1,),
        out_shape=jax.ShapeDtypeStruct((blocks, ROW_DEV, width), bf16),
        in_specs=[
            pl.BlockSpec(memory_space=pltpu.SMEM),
            whole(own_out),
            whole(own_level),
            whole(new_out),
            whole(new_level),
            whole(returned),
        ]
        + [out_weights] * len(weights),
        out_specs=pl.BlockSpec((blocks, ROW_DEV, width), lambda i: (0, 0, 0)),
        scratch_shapes=[pltpu.VMEM((ROW_DEV, width), f32)],
        compiler_params=pltpu.CompilerParams(vmem_limit_bytes=24 << 20),
        name="merge_and_project",
    )(control, own_out, own_level, new_out, new_level, returned, *weights)


def feed_forward(summed, hidden, gain, parcels, units):
    blocks, rows, part = summed.shape
    model = blocks * part
    count, _, depth = parcels[0].shape
    group = 2
    half = count // group
    parts = len(parcels)
    steps = parts * half
    chunk = group * depth
    each = chunk // part
    per = rows // (NZL * NX)

    def kernel(s_ref, x_ref, g_ref, *refs):
        within_refs, down_refs = refs[:parts], refs[parts : 2 * parts]
        out_ref, mixed_ref, norm_ref, gate_ref, up_ref = refs[2 * parts :]
        k = pl.program_id(0)

        @pl.when(k == 0)
        def _():
            squares = jnp.zeros((rows, part), f32)
            for b in range(blocks):
                block = s_ref[b].astype(f32)
                squares = squares + block * block
            norm_ref[...] = lax.rsqrt(
                jnp.sum(squares, axis=1, keepdims=True) / model + EPSILON
            )
            gate_ref[...] = jnp.zeros_like(gate_ref)
            up_ref[...] = jnp.zeros_like(up_ref)

        for j in range(each):
            cols = slice(j * part, (j + 1) * part)
            mixed_ref[:, cols] = (
                x_ref[:, cols].astype(f32)
                + s_ref[k * each + j].astype(f32) * norm_ref[...] * g_ref[:, cols]
            ).astype(bf16)

        def add(ref):
            for n in range(group):
                mixed = mixed_ref[:, n * depth : (n + 1) * depth]

                def product(weight):
                    return lax.dot_general(
                        mixed, weight, (((1,), (1,)), ((), ())), preferred_element_type=f32
                    )

                gate_ref[...] += product(ref[n, :units])
                up_ref[...] += product(ref[n, units:])

        for j in range(parts):
            pl.when(k // half == j)(functools.partial(add, within_refs[j]))

        @pl.when(k == steps - 1)
        def _():
            to = lax.broadcasted_iota(jnp.int32, (rows, rows), 0)
            at = lax.broadcasted_iota(jnp.int32, (rows, rows), 1)
            source = (to // per) % NZL * (NX * per) + to // (NZL * per) * per + to % per
            move = jnp.where(at == source, 1.0, 0.0).astype(bf16)
            gate = gate_ref[...]
            active = (gate / (1.0 + jnp.exp(-gate)) * up_ref[...]).astype(bf16)
            active = jnp.dot(move, active, preferred_element_type=f32).astype(bf16)
            for j in range(parts):
                for n in range(count):
                    at_col = (j * count + n) * depth
                    out_ref[:, at_col : at_col + depth] = jnp.dot(
                        active, down_refs[j][n], preferred_element_type=f32
                    ).astype(bf16)

    return pl.pallas_call(
        kernel,
        grid=(steps,),
        out_shape=(
            jax.ShapeDtypeStruct((rows, model), bf16),
            jax.ShapeDtypeStruct((rows, model), bf16),
        ),
        in_specs=[
            pl.BlockSpec(summed.shape, lambda k: (0, 0, 0)),
            pl.BlockSpec((rows, chunk), lambda k: (0, k)),
            pl.BlockSpec((1, chunk), lambda k: (0, k)),
        ]
        + [
            pl.BlockSpec(
                (group, 2 * units, depth),
                lambda k, j=j: (jnp.clip(k - j * half, 0, half - 1), 0, 0),
            )
            for j in range(parts)
        ]
        + [pl.BlockSpec((count, units, depth), lambda k: (0, 2, 0))] * parts,
        out_specs=(
            pl.BlockSpec((rows, model), lambda k: (0, 0)),
            pl.BlockSpec((rows, chunk), lambda k: (0, k)),
        ),
        scratch_shapes=[
            pltpu.VMEM((rows, 1), f32),
            pltpu.VMEM((rows, units), f32),
            pltpu.VMEM((rows, units), f32),
        ],
        compiler_params=pltpu.CompilerParams(vmem_limit_bytes=40 << 20),
        name="feed_forward",
    )(summed, hidden, gain, *parcels, *parcels)


def shards(
    hidden_states,
    query_weight,
    key_weight,
    value_weight,
    output_weight,
    query_gain,
    key_gain,
    attention_gain,
    gate_weight,
    up_weight,
    down_weight,
    feedforward_gain,
    cached_keys,
    cached_values,
    passage_order,
    separators,
    recompute_index,
    prompt_lengths,
):
    zh = lax.axis_index("zh")
    core = lax.axis_index("core")
    zl = lax.axis_index("zl")
    x_at = lax.axis_index("x")
    seq = lax.axis_index("y") * 4 + zh * 2 + core
    width = query_weight.shape[1]
    hidden_units = gate_weight.shape[1]
    model = hidden_states.shape[1]
    depth = query_weight.shape[0]

    mine = jnp.concatenate([query_weight, key_weight, value_weight, output_weight.T], axis=1)
    parcel = jnp.concatenate([gate_weight.T, up_weight.T, down_weight])
    parcel = jnp.pad(parcel, ((0, -parcel.shape[0] % 16), (0, 0)))
    theirs = swap(mine, "zh", NZH)
    starts, owners, positions, new_live = layout(
        passage_order, separators, recompute_index, prompt_lengths
    )
    frequency = frequencies()
    my_positions = lax.dynamic_index_in_dim(positions, seq, 0, False)
    angles = my_positions.astype(f32)[:, None] * frequency[None, :]
    cosine, sine = jnp.cos(angles), jnp.sin(angles)
    start = lax.dynamic_index_in_dim(starts, seq, 0, False)
    turn = (start.astype(f32) * frequency)[None, :]
    moved = rotate(cached_keys[0].astype(f32), jnp.cos(turn), jnp.sin(turn)).astype(bf16)
    near = copies_to_all(mine, "y", NY)
    theirs, cosine, sine, moved = lax.optimization_barrier((theirs, cosine, sine, moved))
    near_other = swap(near, "core", NCORE)
    far = copies_to_all(theirs, "y", NY)
    far, parcel = lax.optimization_barrier((far, parcel))
    far_other = swap(far, "core", NCORE)
    parcel_near = lax.all_gather(parcel, "y")

    columns = hidden_states.reshape(ROW_DEV, NY, NZH, NCORE, depth)
    ours = own_first(
        [[columns[:, :, i, j].reshape(ROW_DEV, NY * depth) for j in range(2)] for i in range(2)],
        zh,
        core,
    )

    def product(x, w):
        return jnp.dot(x, w.reshape(NY * depth, 4 * width), preferred_element_type=f32)

    raw = product(ours[0][0], near) + product(ours[0][1], near_other)
    raw = raw + product(ours[1][0], far) + product(ours[1][1], far_other)
    query_raw, key_raw, value_raw = (raw[:, i * width : (i + 1) * width] for i in range(3))

    squares = jnp.stack(
        [jnp.sum(query_raw * query_raw, axis=1), jnp.sum(key_raw * key_raw, axis=1)]
    )
    squares = lax.all_to_all(
        jnp.broadcast_to(squares[None], (NZL * NX,) + squares.shape), BLK, 0, 0, tiled=True
    )
    squares = jnp.sum(squares, axis=0)
    squares, parcel = lax.optimization_barrier((squares, parcel))
    pair = lax.all_gather(parcel, "zh")
    scale = lax.rsqrt(squares / model + EPSILON)
    query = rotate(query_raw * scale[0][:, None] * query_gain, cosine, sine).astype(bf16)
    key = rotate(key_raw * scale[1][:, None] * key_gain, cosine, sine).astype(bf16)
    value = value_raw.astype(bf16)

    picked = lax.dynamic_index_in_dim(recompute_index, seq, 0, False)
    passage_keys = moved.at[picked].set(key[:SEL], unique_indices=True)
    passage_values = cached_values[0].at[picked].set(value[:SEL], unique_indices=True)

    request = lax.dynamic_index_in_dim(owners, seq, 0, False)
    order = passage_order.reshape(-1, PPR)
    chosen = lax.dynamic_index_in_dim(order, request, 0, False)
    all_queries = gather_seq(query)

    def rows_of(table, s):
        return lax.dynamic_index_in_dim(table, s, 0, False)

    sources = [chosen[0], chosen[1], request * 2, request * 2 + 1]
    cuts = [slice(0, SEL), slice(0, SEL), slice(SEL, None), slice(SEL, None)]
    wanted = jnp.concatenate(
        [rows_of(all_queries, seq_slot(s))[c] for s, c in zip(sources, cuts)]
    )
    wanted_at = jnp.concatenate([rows_of(positions, s)[c] for s, c in zip(sources, cuts)])
    key_at = start + jnp.arange(PLEN, dtype=jnp.int32)
    part, level = partial_attention(
        wanted, passage_keys, passage_values, key_at[None, :] <= wanted_at[:, None]
    )

    new_mine = jnp.concatenate([key[SEL:], value[SEL:]])
    new_other = swap(new_mine, "core", NCORE)
    new_keys = jnp.concatenate([key[SEL:], new_other[:TOKN_DEV]])
    new_values = jnp.concatenate([value[SEL:], new_other[TOKN_DEV:]])
    partner = seq + 1 - 2 * core
    new_at = jnp.concatenate([my_positions[SEL:], rows_of(positions, partner)[SEL:]])
    live = jnp.concatenate([rows_of(new_live, seq), rows_of(new_live, partner)])
    new_part = partial_attention(
        query[SEL:],
        new_keys,
        new_values,
        (new_at[None, :] <= my_positions[SEL:][:, None]) & live[None, :],
    )

    returned = copies_to_all(pack(part[SEL:], level[SEL:]), "zh", NZH)
    returned = copies_to_all(returned, "y", NY)
    returned = copies_to_all(returned, "core", NCORE).reshape(N_SEQ, -1, 2 * width)
    first = chosen[0] == seq
    own = (
        jnp.where(first, part[:SEL], part[SEL : 2 * SEL]),
        jnp.where(first, level[:SEL], level[SEL : 2 * SEL]),
    )
    my_order = rows_of(order, seq // 2)
    control = jnp.stack(
        [seq_slot(chosen[0]), seq_slot(my_order[0]), seq_slot(my_order[1]), core, first]
    ).astype(jnp.int32)

    blocks = NX * NZL
    terms = merge_and_project(control, own, new_part, returned, [near, near_other, far, far_other])
    terms, pair = lax.optimization_barrier((terms, pair))
    parcel_far = lax.all_gather(jnp.where(zh == 0, pair[1], pair[0]), "y")
    terms = lax.all_to_all(terms.reshape(NX, NZL, ROW_DEV, width), "x", 0, 0, tiled=True)
    terms = jnp.sum(terms.astype(f32), axis=0).astype(bf16)
    terms = lax.all_to_all(terms, "zl", 0, 0, tiled=True)
    summed = jnp.sum(terms.astype(f32), axis=0).astype(bf16)
    summed = copies_to_all(summed, "zl", NZL)
    summed = copies_to_all(summed, "x", NX).reshape(blocks, ROW_DEV, model // blocks)

    rows = ROW_DEV // blocks
    parcels = [parcel_near, swap(parcel_near, "core", NCORE)]
    parcels += [parcel_far, swap(parcel_far, "core", NCORE)]

    def own_order(a):
        a = a.reshape(NY, NZH, NCORE, depth)
        a = own_first([[a[:, i, j].reshape(1, -1) for j in range(2)] for i in range(2)], zh, core)
        return jnp.concatenate(a[0] + a[1], axis=1)

    terms, mixed = feed_forward(
        summed,
        jnp.concatenate(ours[0] + ours[1], axis=1),
        own_order(attention_gain),
        parcels,
        hidden_units,
    )
    terms = lax.all_to_all(terms.reshape(NX, NZL * rows, model), "x", 0, 0, tiled=True)
    terms = jnp.sum(terms.astype(f32), axis=0).astype(bf16)
    terms = lax.all_to_all(terms.reshape(NZL, rows, model), "zl", 0, 0, tiled=True)
    total = jnp.sum(terms.astype(f32), axis=0)
    norm = lax.rsqrt(jnp.mean(total * total, axis=1, keepdims=True) + EPSILON)
    my_rows = lax.dynamic_slice_in_dim(mixed, (zl * NX + x_at) * rows, rows, 0)
    final = my_rows.astype(f32) + total * norm * own_order(feedforward_gain)
    final = final.astype(bf16).reshape(rows, NZH * NCORE, NY, 1, depth)
    final = own_first([[final[:, 2 * i + j] for j in range(2)] for i in range(2)], zh, core)
    hidden_out = jnp.concatenate(final[0] + final[1], axis=2).reshape(rows, model)
    return (hidden_out, passage_keys[None], passage_values[None])


def solution(mesh):
    fine = Mesh(
        mesh.devices.reshape(NY, NZH, NCORE, NZL, NX), ("y", "zh", "core", "zl", "x")
    )
    by_both = P(SEQ, BLK)
    return jax.shard_map(
        shards,
        mesh=fine,
        in_specs=(
            P(SEQ, None),
            by_both,
            by_both,
            by_both,
            P(BLK, SEQ),
            P(BLK),
            P(BLK),
            P(),
            by_both,
            by_both,
            P(BLK, SEQ),
            P(),
            P(SEQ, None, BLK),
            P(SEQ, None, BLK),
            P(),
            P(),
            P(),
            P(),
        ),
        out_specs=(P(SEQ + BLK, None), P(SEQ, None, BLK), P(SEQ, None, BLK)),
        check_vma=False,
    )
```

```python
import functools
import math

import jax
import jax.numpy as jnp
from jax import lax
from jax.experimental import pallas as pl
from jax.experimental.pallas import tpu as pltpu
from jax.sharding import Mesh, PartitionSpec as P

HD = 128
PLEN = 1024
SEL = 96
PPR = 2
TOKN_DEV = 32
ROW_DEV = 128

EPSILON = 1e-06
ROPE_THETA = 500000.0
MASKED = -1e30

SEQ = ("y", "zh", "core")
BLK = ("zl", "x")
NY, NZH, NCORE, NZL, NX = 4, 2, 2, 8, 4
N_SEQ = NY * NZH * NCORE
bf16 = jnp.bfloat16
f32 = jnp.float32


def frequencies():
    indices = jnp.arange(HD // 2, dtype=f32)
    return jnp.exp(indices * (-2.0 * math.log(ROPE_THETA) / HD))


def copies_to_all(a, axis, count):
    return lax.all_to_all(
        jnp.broadcast_to(a[None], (count,) + a.shape), axis, 0, 0, tiled=True
    )


def gather_seq(a):
    a = copies_to_all(a, "zh", NZH)
    a = copies_to_all(a, "y", NY)
    a = copies_to_all(a, "core", NCORE)
    return a.reshape((N_SEQ,) + a.shape[3:])


def seq_slot(s):
    return (s % 2) * 8 + (s // 4) * 2 + (s // 2) % 2


def swap(a, axis, count):
    return lax.ppermute(a, axis, [(i, i ^ 1) for i in range(count)])


def layout(passage_order, separators, recompute_index, prompt_lengths):
    requests = N_SEQ // PPR
    slot_ids = jnp.arange(PPR, dtype=jnp.int32)
    opening = slot_ids[None, :] * PLEN + jnp.cumsum(separators, axis=1)
    flat = passage_order.reshape(-1)
    hit = flat[None, :] == jnp.arange(N_SEQ, dtype=jnp.int32)[:, None]
    starts = jnp.sum(jnp.where(hit, opening.reshape(-1)[None, :], 0), axis=1)
    place = jnp.sum(jnp.where(hit, jnp.arange(N_SEQ, dtype=jnp.int32)[None, :], 0), axis=1)
    owners = place // PPR
    prompt_start = opening[:, PPR - 1] + PLEN
    new_index = jnp.arange(PPR * TOKN_DEV, dtype=jnp.int32)
    new_positions = (prompt_start[:, None] + new_index[None, :]).reshape(N_SEQ, TOKN_DEV)
    new_live = (new_index[None, :] < prompt_lengths[:, None]).reshape(N_SEQ, TOKN_DEV)
    picked = starts[:, None] + recompute_index
    positions = jnp.concatenate([picked, new_positions], axis=1)
    return starts, owners, positions, new_live


def partial_attention(queries, keys, values, visible):
    scores = lax.dot_general(
        queries, keys, (((1,), (1,)), ((), ())), preferred_element_type=f32
    ) * HD ** (-0.5)
    scores = jnp.where(visible, scores, MASKED)
    peak = jnp.max(scores, axis=1, keepdims=True)
    weights = jnp.where(visible, jnp.exp(scores - peak), 0.0)
    total = jnp.sum(weights, axis=1, keepdims=True)
    some = total > 0.0
    safe = jnp.where(some, total, 1.0)
    out = jnp.dot(weights.astype(bf16), values, preferred_element_type=f32) / safe
    return out, jnp.where(some, peak + jnp.log(safe), MASKED)


def merge(parts):
    top = parts[0][1]
    for _, level in parts[1:]:
        top = jnp.maximum(top, level)
    num = 0.0
    den = 0.0
    for out, level in parts:
        w = jnp.exp(level - top)
        num = num + w * out
        den = den + w
    return num / den


def unpack(block):
    block = block.astype(f32)
    level = block[:, HD : HD + 1] + block[:, HD + 1 : HD + 2] + block[:, HD + 2 : HD + 3]
    return block[:, :HD], level


def whole(a):
    return pl.BlockSpec(a.shape, lambda *k: (0,) * a.ndim)


SMEM = pl.BlockSpec(memory_space=pltpu.SMEM)


def call(kernel, name, out_shape, *args, scratch=(), limit=24):
    small = [a.ndim == 1 for a in args]
    return pl.pallas_call(
        kernel,
        grid=(1,),
        out_shape=out_shape,
        in_specs=[SMEM if one else whole(a) for a, one in zip(args, small)],
        out_specs=jax.tree.map(whole, out_shape),
        scratch_shapes=list(scratch),
        compiler_params=pltpu.CompilerParams(vmem_limit_bytes=limit << 20),
        name=name,
    )(*args)


def shape(dims, dtype):
    return jax.ShapeDtypeStruct(dims, dtype)


def join_weights(query_weight, key_weight, value_weight, output_weight):
    depth, width = query_weight.shape

    def kernel(q_ref, k_ref, v_ref, o_ref, out_ref):
        for n, ref in enumerate((q_ref, k_ref, v_ref)):
            out_ref[:, n * width : (n + 1) * width] = ref[...]
        out_ref[:, 3 * width :] = jnp.transpose(o_ref[...].astype(f32)).astype(bf16)

    return call(
        kernel,
        "join_weights",
        shape((depth, 4 * width), bf16),
        query_weight,
        key_weight,
        value_weight,
        output_weight,
    )


def project(columns, hidden, weights, width, copies):
    rows = hidden.shape[0]
    count, depth, _ = weights[0].shape

    def kernel(c_ref, x_ref, *refs):
        weight_refs, (raw_ref, squares_ref) = refs[:-2], refs[-2:]
        raw = jnp.zeros((rows, 3 * width), f32)
        for m in range(len(weight_refs) * count):
            at = pl.multiple_of(c_ref[m] * depth, depth)
            raw = raw + jnp.dot(
                x_ref[:, pl.ds(at, depth)],
                weight_refs[m // count][m % count, :, : 3 * width],
                preferred_element_type=f32,
            )
        raw_ref[...] = raw
        query, key = raw[:, :width], raw[:, width : 2 * width]
        lane = lax.broadcasted_iota(jnp.int32, (rows, width), 1)
        sums = jnp.where(lane == 0, jnp.sum(query * query, axis=1, keepdims=True), 0.0)
        sums = jnp.where(lane == 1, jnp.sum(key * key, axis=1, keepdims=True), sums)
        sums = jnp.transpose(sums)[:8]
        for b in range(copies):
            squares_ref[b] = sums

    return call(
        kernel,
        "project",
        (shape((rows, 3 * width), f32), shape((copies, 8, rows), f32)),
        columns,
        hidden,
        *weights,
    )


def turn_by(x, cosine, sine):
    return x * cosine + pltpu.roll(x, HD // 2, 1) * sine


def finish_rows(raw, squares, query_gain, key_gain, cosine, sine, model):
    rows = raw.shape[0]
    width = query_gain.shape[1]
    copies = squares.shape[0]

    def kernel(raw_ref, s_ref, gq_ref, gk_ref, c_ref, t_ref, q_ref, k_ref, v_ref, new_ref):
        sums = s_ref[0]
        for b in range(1, copies):
            sums = sums + s_ref[b]
        sums = jnp.concatenate([sums, jnp.zeros((width - 8, rows), f32)], axis=0)
        scale = lax.rsqrt(jnp.transpose(sums) / model + EPSILON)
        raw = raw_ref[...]
        query = raw[:, :width] * scale[:, 0:1] * gq_ref[...]
        key = raw[:, width : 2 * width] * scale[:, 1:2] * gk_ref[...]
        query = turn_by(query, c_ref[...], t_ref[...]).astype(bf16)
        key = turn_by(key, c_ref[...], t_ref[...]).astype(bf16)
        value = raw[:, 2 * width :].astype(bf16)
        for z in range(NZH):
            q_ref[z] = query
        k_ref[...] = key
        v_ref[...] = value
        new_ref[:TOKN_DEV, :] = key[SEL:]
        new_ref[TOKN_DEV:, :] = value[SEL:]

    return call(
        kernel,
        "finish_rows",
        (
            shape((NZH, rows, width), bf16),
            shape((rows, width), bf16),
            shape((rows, width), bf16),
            shape((2 * TOKN_DEV, width), bf16),
        ),
        raw,
        squares,
        query_gain,
        key_gain,
        cosine,
        sine,
    )


def blend(picked, cosine, sine, keys, values, new_keys, new_values):
    _, length, width = keys.shape
    steps = 4
    chunk = length // steps

    def kernel(p_ref, c_ref, t_ref, k_ref, v_ref, nk_ref, nv_ref, bk_ref, bv_ref):
        at = lax.broadcasted_iota(jnp.int32, (chunk, width), 0) + pl.program_id(0) * chunk
        hit = (at == p_ref[...]).astype(f32)
        here = jnp.max(hit, axis=1, keepdims=True) > 0.0
        hit = hit.astype(bf16)
        turned = turn_by(k_ref[0].astype(f32), c_ref[...], t_ref[...])
        placed = jnp.dot(hit, nk_ref[...], preferred_element_type=f32)
        bk_ref[0] = jnp.where(here, placed, turned).astype(bf16)
        placed = jnp.dot(hit, nv_ref[...], preferred_element_type=f32)
        bv_ref[0] = jnp.where(here, placed, v_ref[0].astype(f32)).astype(bf16)

    tile = pl.BlockSpec((1, chunk, width), lambda k: (0, k, 0))
    return pl.pallas_call(
        kernel,
        grid=(steps,),
        out_shape=(shape(keys.shape, bf16), shape(keys.shape, bf16)),
        in_specs=[
            whole(picked),
            whole(cosine),
            whole(sine),
            tile,
            tile,
            whole(new_keys),
            whole(new_values),
        ],
        out_specs=(tile, tile),
        name="blend",
    )(picked, cosine, sine, keys, values, new_keys, new_values)


def attend(control, queries, keys, values, wanted_at, own, new_mine, new_other, new_at, new_key_at):
    width = keys.shape[2]
    length = keys.shape[1]
    cuts = [(0, SEL), (0, SEL), (SEL, ROW_DEV), (SEL, ROW_DEV)]
    count = sum(high - low for low, high in cuts)
    back = count - SEL
    step = 32

    def kernel(
        c_ref, q_ref, k_ref, v_ref, w_ref, own_ref, nm_ref, no_ref, na_ref, nk_ref,
        back_ref, kept_ref, new_ref, rows_ref,
    ):
        at = 0
        for i, (low, high) in enumerate(cuts):
            rows_ref[at : at + high - low, :] = q_ref[c_ref[i], low:high, :]
            at += high - low
        lane = lax.broadcasted_iota(jnp.int32, (step, width), 1)
        key_at = c_ref[4] + lax.broadcasted_iota(jnp.int32, (step, length), 1)
        for n in range(count // step):
            span = slice(n * step, (n + 1) * step)
            out, level = partial_attention(
                rows_ref[span, :], k_ref[0], v_ref[0], key_at <= w_ref[span, :]
            )
            if n * step < 2 * SEL:
                kept_ref[span, :width] = out
                kept_ref[span, width:] = jnp.broadcast_to(level, (step, width))
            if n * step >= SEL:
                high = level.astype(bf16).astype(f32)
                mid = (level - high).astype(bf16).astype(f32)
                low = level - high - mid
                pieces = jnp.where(lane == 0, high, jnp.where(lane == 1, mid, 0.0))
                pieces = jnp.where(lane == 2, low, pieces)
                to = slice(n * step - SEL, (n + 1) * step - SEL)
                for z in range(NZH):
                    back_ref[z, to, :width] = out.astype(bf16)
                    back_ref[z, to, width:] = pieces.astype(bf16)
        new_keys = jnp.concatenate([nm_ref[:TOKN_DEV, :], no_ref[:TOKN_DEV, :]], axis=0)
        new_values = jnp.concatenate([nm_ref[TOKN_DEV:, :], no_ref[TOKN_DEV:, :]], axis=0)
        out, level = partial_attention(
            own_ref[0, SEL:, :], new_keys, new_values, nk_ref[...] <= na_ref[...]
        )
        new_ref[:, :width] = out
        new_ref[:, width:] = jnp.broadcast_to(level, (TOKN_DEV, width))

    return call(
        kernel,
        "attend",
        (
            shape((NZH, back, 2 * width), bf16),
            shape((2 * SEL, 2 * width), f32),
            shape((TOKN_DEV, 2 * width), f32),
        ),
        control,
        queries,
        keys,
        values,
        wanted_at,
        own,
        new_mine,
        new_other,
        new_at,
        new_key_at,
        scratch=[pltpu.VMEM((count, width), bf16)],
    )


def merge_and_project(control, kept, new_part, returned, weights):
    width = new_part.shape[1] // 2
    count, part, _ = weights[0].shape
    halves = part // width
    blocks = len(weights) * count * halves

    def kernel(c_ref, kept_ref, new_ref, back_ref, *refs):
        weight_refs, (out_ref, att_ref) = refs[:-2], refs[-2:]
        first = c_ref[4] == 1
        kept = jnp.where(first, kept_ref[:SEL, :], kept_ref[SEL:, :])
        remote, remote_level = unpack(back_ref[c_ref[0], :SEL, :])
        remote_level = jnp.where(first, MASKED, remote_level)
        att_ref[:SEL, :] = merge(
            [(kept[:, :width], kept[:, width : width + 1]), (remote, remote_level)]
        )
        at = pl.multiple_of(SEL + c_ref[3] * TOKN_DEV, TOKN_DEV)
        parts = [(new_ref[:, :width], new_ref[:, width : width + 1])]
        for i in range(PPR):
            parts.append(unpack(back_ref[c_ref[1 + i], pl.ds(at, TOKN_DEV), :]))
        att_ref[SEL:, :] = merge(parts)
        attention = att_ref[...].astype(bf16)
        for j, ref in enumerate(weight_refs):
            for n in range(count):
                term = lax.dot_general(
                    attention, ref[n], (((1,), (1,)), ((), ())), preferred_element_type=f32
                ).astype(bf16)
                for h in range(halves):
                    out_ref[(j * count + n) * halves + h] = term[:, h * width : (h + 1) * width]

    out_weights = pl.BlockSpec((count, part, width), lambda i: (0, 0, 3))
    return pl.pallas_call(
        kernel,
        grid=(1,),
        out_shape=shape((blocks, ROW_DEV, width), bf16),
        in_specs=[SMEM, whole(kept), whole(new_part), whole(returned)]
        + [out_weights] * len(weights),
        out_specs=pl.BlockSpec((blocks, ROW_DEV, width), lambda i: (0, 0, 0)),
        scratch_shapes=[pltpu.VMEM((ROW_DEV, width), f32)],
        compiler_params=pltpu.CompilerParams(vmem_limit_bytes=24 << 20),
        name="merge_and_project",
    )(control, kept, new_part, returned, *weights)


def feed_forward(columns, summed, hidden, gain, parcels, units):
    blocks, rows, part = summed.shape
    model = blocks * part
    count, _, depth = parcels[0].shape
    group = 2
    half = count // group
    parts = len(parcels)
    steps = parts * half
    split = depth // part
    per = rows // (NZL * NX)
    contract_last = (((1,), (1,)), ((), ()))

    def kernel(c_ref, s_ref, x_ref, g_ref, *refs):
        within_refs, down_refs = refs[:parts], refs[parts : 2 * parts]
        out_ref, mixed_ref, norm_ref, acc_ref = refs[2 * parts :]
        k = pl.program_id(0)

        @pl.when(k == 0)
        def _():
            squares = jnp.zeros((rows, part), f32)
            for b in range(blocks):
                block = s_ref[b].astype(f32)
                squares = squares + block * block
            norm_ref[...] = lax.rsqrt(
                jnp.sum(squares, axis=1, keepdims=True) / model + EPSILON
            )
            acc_ref[...] = jnp.zeros_like(acc_ref)

        def add(ref):
            for n in range(group):
                m = k * group + n
                at = pl.multiple_of(c_ref[m] * depth, depth)
                cols = pl.ds(at, depth)
                summed = jnp.concatenate([s_ref[m * split + h] for h in range(split)], axis=1)
                mixed = (
                    x_ref[:, cols].astype(f32)
                    + summed.astype(f32) * norm_ref[...] * g_ref[:, cols]
                ).astype(bf16)
                mixed_ref[:, cols] = mixed
                acc_ref[...] += lax.dot_general(
                    ref[n], mixed, contract_last, preferred_element_type=f32
                )

        for j in range(parts):
            pl.when(k // half == j)(functools.partial(add, within_refs[j]))

        @pl.when(k == steps - 1)
        def _():
            to = lax.broadcasted_iota(jnp.int32, (rows, rows), 0)
            at = lax.broadcasted_iota(jnp.int32, (rows, rows), 1)
            source = (to // per) % NZL * (NX * per) + to // (NZL * per) * per + to % per
            move = jnp.where(at == source, 1.0, 0.0).astype(bf16)
            gate = acc_ref[:units, :]
            active = (gate / (1.0 + jnp.exp(-gate)) * acc_ref[units:, :]).astype(bf16)
            active = lax.dot_general(
                move, active, contract_last, preferred_element_type=f32
            ).astype(bf16)
            for m in range(parts * count):
                at_col = pl.multiple_of(c_ref[m] * depth, depth)
                out_ref[:, pl.ds(at_col, depth)] = jnp.dot(
                    active, down_refs[m // count][m % count], preferred_element_type=f32
                ).astype(bf16)

    return pl.pallas_call(
        kernel,
        grid=(steps,),
        out_shape=(shape((rows, model), bf16), shape((rows, model), bf16)),
        in_specs=[SMEM, whole(summed), whole(hidden), whole(gain)]
        + [
            pl.BlockSpec(
                (group, 2 * units, depth),
                lambda k, j=j: (jnp.clip(k - j * half, 0, half - 1), 0, 0),
            )
            for j in range(parts)
        ]
        + [pl.BlockSpec((count, units, depth), lambda k: (0, 2, 0))] * parts,
        out_specs=(
            pl.BlockSpec((rows, model), lambda k: (0, 0)),
            pl.BlockSpec((rows, model), lambda k: (0, 0)),
        ),
        scratch_shapes=[pltpu.VMEM((rows, 1), f32), pltpu.VMEM((2 * units, rows), f32)],
        compiler_params=pltpu.CompilerParams(vmem_limit_bytes=40 << 20),
        name="feed_forward",
    )(columns, summed, hidden, gain, *parcels, *parcels)


def shards(
    hidden_states,
    query_weight,
    key_weight,
    value_weight,
    output_weight,
    query_gain,
    key_gain,
    attention_gain,
    gate_weight,
    up_weight,
    down_weight,
    feedforward_gain,
    cached_keys,
    cached_values,
    passage_order,
    separators,
    recompute_index,
    prompt_lengths,
):
    y_at, zh, core = (lax.axis_index(a) for a in SEQ)
    zl, x_at = (lax.axis_index(a) for a in BLK)
    seq = y_at * 4 + zh * 2 + core
    width = query_weight.shape[1]
    hidden_units = gate_weight.shape[1]
    model = hidden_states.shape[1]
    blocks = NX * NZL
    rows = ROW_DEV // blocks

    mine = join_weights(query_weight, key_weight, value_weight, output_weight)
    theirs = swap(mine, "zh", NZH)
    near = copies_to_all(mine, "y", NY)
    parcel = jnp.concatenate([gate_weight.T, up_weight.T, down_weight])
    parcel = jnp.pad(parcel, ((0, -parcel.shape[0] % 16), (0, 0)))

    order_of = jnp.arange(N_SEQ, dtype=jnp.int32)
    columns = order_of % 4 * 4 + (zh ^ (order_of // 8)) * 2 + (core ^ (order_of // 4 % 2))
    starts, owners, positions, new_live = layout(
        passage_order, separators, recompute_index, prompt_lengths
    )

    def rows_of(table, s):
        return lax.dynamic_index_in_dim(table, s, 0, False)

    frequency = frequencies()
    my_positions = rows_of(positions, seq)
    angles = my_positions.astype(f32)[:, None] * frequency[None, :]
    cosine, sine = jnp.cos(angles), jnp.sin(angles)
    cosine = jnp.concatenate([cosine, cosine], axis=1)
    sine = jnp.concatenate([-sine, sine], axis=1)
    start = rows_of(starts, seq)
    turn = (start.astype(f32) * frequency)[None, :]
    turn_cosine, turn_sine = jnp.cos(turn), jnp.sin(turn)
    turn_cosine = jnp.concatenate([turn_cosine, turn_cosine], axis=1)
    turn_sine = jnp.concatenate([-turn_sine, turn_sine], axis=1)
    picked = jnp.pad(rows_of(recompute_index, seq), (0, width - SEL), constant_values=-1)[None]
    request = rows_of(owners, seq)
    order = passage_order.reshape(-1, PPR)
    chosen = rows_of(order, request)
    my_order = rows_of(order, seq // 2)
    sources = [chosen[0], chosen[1], request * 2, request * 2 + 1]
    cuts = [slice(0, SEL), slice(0, SEL), slice(SEL, None), slice(SEL, None)]
    wanted_at = jnp.concatenate([rows_of(positions, s)[c] for s, c in zip(sources, cuts)])[:, None]
    partner = seq + 1 - 2 * core
    far_away = jnp.int32(1 << 30)
    new_key_at = jnp.concatenate(
        [
            jnp.where(rows_of(new_live, s), rows_of(positions, s)[SEL:], far_away)
            for s in (seq, partner)
        ]
    )[None]
    new_at = my_positions[SEL:][:, None]
    first = chosen[0] == seq
    attend_control = jnp.stack([seq_slot(s) for s in sources] + [start]).astype(jnp.int32)
    merge_control = jnp.stack(
        [seq_slot(chosen[0]), seq_slot(my_order[0]), seq_slot(my_order[1]), core, first]
    ).astype(jnp.int32)
    tables = (
        columns,
        cosine,
        sine,
        turn_cosine,
        turn_sine,
        picked,
        wanted_at,
        new_key_at,
        new_at,
        attend_control,
        merge_control,
    )
    theirs, near, tables = lax.optimization_barrier((theirs, near, tables))
    (
        columns,
        cosine,
        sine,
        turn_cosine,
        turn_sine,
        picked,
        wanted_at,
        new_key_at,
        new_at,
        attend_control,
        merge_control,
    ) = tables

    near_other = swap(near, "core", NCORE)
    far = copies_to_all(theirs, "y", NY)
    far_other = swap(far, "core", NCORE)
    parcel_near = lax.all_gather(parcel, "y")
    weights = [near, near_other, far, far_other]
    raw, squares = project(columns, hidden_states, weights, width, blocks)
    squares = lax.all_to_all(squares, BLK, 0, 0, tiled=True)
    squares, parcel, parcel_near = lax.optimization_barrier((squares, parcel, parcel_near))
    pair = lax.all_gather(parcel, "zh")
    query, key, value, new_mine = finish_rows(
        raw, squares, query_gain[None], key_gain[None], cosine, sine, model
    )

    queries = lax.all_to_all(query, "zh", 0, 0, tiled=True)
    queries = copies_to_all(queries, "y", NY)
    queries = copies_to_all(queries, "core", NCORE).reshape(N_SEQ, ROW_DEV, width)
    new_other = swap(new_mine, "core", NCORE)
    blended_keys, blended_values = blend(
        picked, turn_cosine, turn_sine, cached_keys, cached_values, key, value
    )
    returned, kept, new_part = attend(
        attend_control,
        queries,
        blended_keys,
        blended_values,
        wanted_at,
        query,
        new_mine,
        new_other,
        new_at,
        new_key_at,
    )

    returned = lax.all_to_all(returned, "zh", 0, 0, tiled=True)
    returned = copies_to_all(returned, "y", NY)
    returned = copies_to_all(returned, "core", NCORE).reshape(N_SEQ, -1, 2 * width)

    terms = merge_and_project(merge_control, kept, new_part, returned, weights)
    terms, pair = lax.optimization_barrier((terms, pair))
    parcel_far = lax.all_gather(jnp.where(zh == 0, pair[1], pair[0]), "y")
    terms = lax.all_to_all(terms.reshape(NX, NZL, ROW_DEV, width), "x", 0, 0, tiled=True)
    terms = jnp.sum(terms.astype(f32), axis=0).astype(bf16)
    terms = lax.all_to_all(terms, "zl", 0, 0, tiled=True)
    summed = jnp.sum(terms.astype(f32), axis=0).astype(bf16)
    summed = copies_to_all(summed, "zl", NZL)
    summed = copies_to_all(summed, "x", NX).reshape(blocks, ROW_DEV, model // blocks)

    parcels = [parcel_near, swap(parcel_near, "core", NCORE)]
    parcels += [parcel_far, swap(parcel_far, "core", NCORE)]
    terms, mixed = feed_forward(
        columns, summed, hidden_states, attention_gain[None], parcels, hidden_units
    )
    terms = lax.all_to_all(terms.reshape(NX, NZL * rows, model), "x", 0, 0, tiled=True)
    terms = jnp.sum(terms.astype(f32), axis=0).astype(bf16)
    terms = lax.all_to_all(terms.reshape(NZL, rows, model), "zl", 0, 0, tiled=True)
    total = jnp.sum(terms.astype(f32), axis=0)
    norm = lax.rsqrt(jnp.mean(total * total, axis=1, keepdims=True) + EPSILON)
    my_rows = lax.dynamic_slice_in_dim(mixed, (zl * NX + x_at) * rows, rows, 0)
    hidden_out = (my_rows.astype(f32) + total * norm * feedforward_gain).astype(bf16)
    return (hidden_out, blended_keys, blended_values)


def solution(mesh):
    fine = Mesh(
        mesh.devices.reshape(NY, NZH, NCORE, NZL, NX), ("y", "zh", "core", "zl", "x")
    )
    by_both = P(SEQ, BLK)
    return jax.shard_map(
        shards,
        mesh=fine,
        in_specs=(
            P(SEQ, None),
            by_both,
            by_both,
            by_both,
            P(BLK, SEQ),
            P(BLK),
            P(BLK),
            P(),
            by_both,
            by_both,
            P(BLK, SEQ),
            P(),
            P(SEQ, None, BLK),
            P(SEQ, None, BLK),
            P(),
            P(),
            P(),
            P(),
        ),
        out_specs=(P(SEQ + BLK, None), P(SEQ, None, BLK), P(SEQ, None, BLK)),
        check_vma=False,
    )
```

```python
import functools
import math

import jax
import jax.numpy as jnp
from jax import lax
from jax.experimental import pallas as pl
from jax.experimental.pallas import tpu as pltpu
from jax.sharding import Mesh, PartitionSpec as P

HD = 128
PLEN = 1024
SEL = 96
PPR = 2
TOKN_DEV = 32
ROW_DEV = 128

EPSILON = 1e-06
ROPE_THETA = 500000.0
MASKED = -1e30

SEQ = ("y", "zh", "core")
BLK = ("zl", "x")
NY, NZH, NCORE, NZL, NX = 4, 2, 2, 8, 4
N_SEQ = NY * NZH * NCORE
bf16 = jnp.bfloat16
f32 = jnp.float32


def frequencies():
    indices = jnp.arange(HD // 2, dtype=f32)
    return jnp.exp(indices * (-2.0 * math.log(ROPE_THETA) / HD))


def copies_to_all(a, axis, count):
    return lax.all_to_all(
        jnp.broadcast_to(a[None], (count,) + a.shape), axis, 0, 0, tiled=True
    )


def gather_seq(a):
    a = copies_to_all(a, "zh", NZH)
    a = copies_to_all(a, "y", NY)
    a = copies_to_all(a, "core", NCORE)
    return a.reshape((N_SEQ,) + a.shape[3:])


def swap(a, axis, count):
    return lax.ppermute(a, axis, [(i, i ^ 1) for i in range(count)])


def partial_attention(queries, keys, values, visible):
    scores = lax.dot_general(
        queries, keys, (((1,), (1,)), ((), ())), preferred_element_type=f32
    ) * HD ** (-0.5)
    scores = jnp.where(visible, scores, MASKED)
    peak = jnp.max(scores, axis=1, keepdims=True)
    weights = jnp.where(visible, jnp.exp(scores - peak), 0.0)
    total = jnp.sum(weights, axis=1, keepdims=True)
    some = total > 0.0
    safe = jnp.where(some, total, 1.0)
    out = jnp.dot(weights.astype(bf16), values, preferred_element_type=f32) / safe
    return out, jnp.where(some, peak + jnp.log(safe), MASKED)


def merge(parts):
    top = parts[0][1]
    for _, level in parts[1:]:
        top = jnp.maximum(top, level)
    num = 0.0
    den = 0.0
    for out, level in parts:
        w = jnp.exp(level - top)
        num = num + w * out
        den = den + w
    return num / den


def unpack(block):
    block = block.astype(f32)
    level = block[:, HD : HD + 1] + block[:, HD + 1 : HD + 2] + block[:, HD + 2 : HD + 3]
    return block[:, :HD], level


def whole(a):
    return pl.BlockSpec(a.shape, lambda *k: (0,) * len(a.shape))


SMEM = pl.BlockSpec(memory_space=pltpu.SMEM)


def call(kernel, name, out_shape, *args, scratch=(), limit=16):
    small = [a.ndim == 1 for a in args]
    return pl.pallas_call(
        kernel,
        grid=(1,),
        out_shape=out_shape,
        in_specs=[SMEM if one else whole(a) for a, one in zip(args, small)],
        out_specs=jax.tree.map(lambda a: SMEM if len(a.shape) == 1 else whole(a), out_shape),
        scratch_shapes=list(scratch),
        compiler_params=pltpu.CompilerParams(vmem_limit_bytes=limit << 20),
        name=name,
    )(*args)


def shape(dims, dtype):
    return jax.ShapeDtypeStruct(dims, dtype)


def tables(seq, passage_order, separators, prompt_lengths, recompute_index):
    spare = 8

    def kernel(
        s_ref, o_ref, sep_ref, len_ref, i_ref, t_ref,
        at_ref, wanted_ref, picked_ref, new_ref, new_key_ref, attend_ref, merge_ref, column_ref,
    ):
        seq = s_ref[0]
        place = jnp.int32(0)
        for n in range(N_SEQ):
            place = jnp.where(o_ref[n] == seq, n, place)

        def start_of(request, slot):
            first = sep_ref[2 * request]
            return first + jnp.where(slot == 1, PLEN + sep_ref[2 * request + 1], 0)

        request, mine = place >> 1, seq >> 1
        chosen = [o_ref[2 * request + i] for i in range(PPR)]
        start = start_of(request, place & 1)
        base = start_of(request, 1) + PLEN
        my_base = start_of(mine, 1) + PLEN
        my_from = (seq & 1) * TOKN_DEV

        lane = lax.broadcasted_iota(jnp.int32, (SEL, N_SEQ), 1)
        index = t_ref[...].astype(f32)

        def column(passage):
            return jnp.sum(jnp.where(lane == passage, index, 0.0), axis=1, keepdims=True)

        count = PPR * TOKN_DEV
        down = lax.broadcasted_iota(jnp.int32, (count, 1), 0)
        at_ref[:SEL, :] = column(seq) + start.astype(f32)
        at_ref[SEL:ROW_DEV, :] = (my_base + my_from + down[:TOKN_DEV]).astype(f32)
        at_ref[ROW_DEV:, :] = jnp.full((spare, 1), start, jnp.int32).astype(f32)
        for i in range(PPR):
            at = column(chosen[i]) + start_of(request, i).astype(f32)
            wanted_ref[i * SEL : (i + 1) * SEL, :] = at.astype(jnp.int32)
        wanted_ref[PPR * SEL :, :] = base + down
        picked_ref[...] = jnp.full((1, HD), -1, jnp.int32)
        picked_ref[:, :SEL] = i_ref[pl.ds(seq, 1), :]
        new_ref[...] = my_base + my_from + down[:TOKN_DEV]
        across = lax.broadcasted_iota(jnp.int32, (1, count), 1)
        token = across ^ my_from
        new_key_ref[...] = jnp.where(token < len_ref[mine], my_base + token, 1 << 30)

        def slot(s):
            return (s & 1) * 8 + (s >> 2) * 2 + ((s >> 1) & 1)

        attend_ref[0] = slot(chosen[0])
        attend_ref[1] = slot(chosen[1])
        attend_ref[2] = slot(2 * request)
        attend_ref[3] = slot(2 * request + 1)
        attend_ref[4] = start
        merge_ref[0] = slot(chosen[0])
        merge_ref[1] = slot(o_ref[2 * mine])
        merge_ref[2] = slot(o_ref[2 * mine + 1])
        merge_ref[3] = seq & 1
        merge_ref[4] = jnp.where(chosen[0] == seq, 1, 0)
        for m in range(N_SEQ):
            other = (m // 8) * 2 + m // 4 % 2
            column_ref[m] = m % 4 * 4 + ((seq & 3) ^ other)

    i32 = jnp.int32
    return call(
        kernel,
        "tables",
        (
            shape((ROW_DEV + spare, 1), f32),
            shape((PPR * (SEL + TOKN_DEV), 1), i32),
            shape((1, HD), i32),
            shape((TOKN_DEV, 1), i32),
            shape((1, PPR * TOKN_DEV), i32),
            shape((5,), i32),
            shape((5,), i32),
            shape((N_SEQ,), i32),
        ),
        seq[None],
        passage_order,
        separators.reshape(-1),
        prompt_lengths,
        recompute_index,
        recompute_index.T,
    )


def join_weights(query_weight, key_weight, value_weight, output_weight):
    depth, width = query_weight.shape

    def kernel(q_ref, k_ref, v_ref, o_ref, out_ref):
        for n, ref in enumerate((q_ref, k_ref, v_ref)):
            out_ref[:, n * width : (n + 1) * width] = ref[...]
        out_ref[:, 3 * width :] = jnp.transpose(o_ref[...].astype(f32)).astype(bf16)

    return call(
        kernel,
        "join_weights",
        shape((depth, 4 * width), bf16),
        query_weight,
        key_weight,
        value_weight,
        output_weight,
    )


def project(columns, hidden, weights, width, copies):
    rows = hidden.shape[0]
    count, depth, _ = weights[0].shape

    def kernel(c_ref, x_ref, *refs):
        weight_refs, (raw_ref, squares_ref) = refs[:-2], refs[-2:]
        raw = jnp.zeros((rows, 3 * width), f32)
        for m in range(len(weight_refs) * count):
            at = pl.multiple_of(c_ref[m] * depth, depth)
            raw = raw + jnp.dot(
                x_ref[:, pl.ds(at, depth)],
                weight_refs[m // count][m % count, :, : 3 * width],
                preferred_element_type=f32,
            )
        raw_ref[...] = raw
        query, key = raw[:, :width], raw[:, width : 2 * width]
        lane = lax.broadcasted_iota(jnp.int32, (rows, width), 1)
        sums = jnp.where(lane == 0, jnp.sum(query * query, axis=1, keepdims=True), 0.0)
        sums = jnp.where(lane == 1, jnp.sum(key * key, axis=1, keepdims=True), sums)
        sums = jnp.transpose(sums)[:8]
        for b in range(copies):
            squares_ref[b] = sums

    return call(
        kernel,
        "project",
        (shape((rows, 3 * width), f32), shape((copies, 8, rows), f32)),
        columns,
        hidden,
        *weights,
    )


def turn_by(x, cosine, sine):
    return x * cosine + pltpu.roll(x, HD // 2, 1) * sine


def finish_rows(raw, squares, query_gain, key_gain, cosine, sine, model):
    rows = raw.shape[0]
    width = query_gain.shape[1]
    copies = squares.shape[0]

    def kernel(raw_ref, s_ref, gq_ref, gk_ref, c_ref, t_ref, q_ref, k_ref, v_ref, new_ref):
        sums = s_ref[0]
        for b in range(1, copies):
            sums = sums + s_ref[b]
        sums = jnp.concatenate([sums, jnp.zeros((width - 8, rows), f32)], axis=0)
        scale = lax.rsqrt(jnp.transpose(sums) / model + EPSILON)
        raw = raw_ref[...]
        query = raw[:, :width] * scale[:, 0:1] * gq_ref[...]
        key = raw[:, width : 2 * width] * scale[:, 1:2] * gk_ref[...]
        query = turn_by(query, c_ref[...], t_ref[...]).astype(bf16)
        key = turn_by(key, c_ref[...], t_ref[...]).astype(bf16)
        value = raw[:, 2 * width :].astype(bf16)
        for z in range(NZH):
            q_ref[z] = query
        k_ref[...] = key
        v_ref[...] = value
        new_ref[:TOKN_DEV, :] = key[SEL:]
        new_ref[TOKN_DEV:, :] = value[SEL:]

    return call(
        kernel,
        "finish_rows",
        (
            shape((NZH, rows, width), bf16),
            shape((rows, width), bf16),
            shape((rows, width), bf16),
            shape((2 * TOKN_DEV, width), bf16),
        ),
        raw,
        squares,
        query_gain,
        key_gain,
        cosine,
        sine,
    )


def blend(picked, cosine, sine, keys, values, new_keys, new_values):
    _, length, width = keys.shape
    steps = 4
    chunk = length // steps

    def kernel(p_ref, c_ref, t_ref, k_ref, v_ref, nk_ref, nv_ref, bk_ref, bv_ref):
        at = lax.broadcasted_iota(jnp.int32, (chunk, width), 0) + pl.program_id(0) * chunk
        hit = (at == p_ref[...]).astype(f32)
        here = jnp.max(hit, axis=1, keepdims=True) > 0.0
        hit = hit.astype(bf16)
        turned = turn_by(k_ref[0].astype(f32), c_ref[...], t_ref[...])
        placed = jnp.dot(hit, nk_ref[...], preferred_element_type=f32)
        bk_ref[0] = jnp.where(here, placed, turned).astype(bf16)
        placed = jnp.dot(hit, nv_ref[...], preferred_element_type=f32)
        bv_ref[0] = jnp.where(here, placed, v_ref[0].astype(f32)).astype(bf16)

    tile = pl.BlockSpec((1, chunk, width), lambda k: (0, k, 0))
    return pl.pallas_call(
        kernel,
        grid=(steps,),
        out_shape=(shape(keys.shape, bf16), shape(keys.shape, bf16)),
        in_specs=[
            whole(picked),
            whole(cosine),
            whole(sine),
            tile,
            tile,
            whole(new_keys),
            whole(new_values),
        ],
        out_specs=(tile, tile),
        compiler_params=pltpu.CompilerParams(vmem_limit_bytes=8 << 20),
        name="blend",
    )(picked, cosine, sine, keys, values, new_keys, new_values)


def attend(control, queries, keys, values, wanted_at, own, new_mine, new_other, new_at, new_key_at):
    width = keys.shape[2]
    length = keys.shape[1]
    cuts = [(0, SEL), (0, SEL), (SEL, ROW_DEV), (SEL, ROW_DEV)]
    count = sum(high - low for low, high in cuts)
    back = count - SEL
    step = 32

    def kernel(
        c_ref, q_ref, k_ref, v_ref, w_ref, own_ref, nm_ref, no_ref, na_ref, nk_ref,
        back_ref, kept_ref, new_ref, rows_ref,
    ):
        at = 0
        for i, (low, high) in enumerate(cuts):
            rows_ref[at : at + high - low, :] = q_ref[c_ref[i], low:high, :]
            at += high - low
        lane = lax.broadcasted_iota(jnp.int32, (step, width), 1)
        key_at = c_ref[4] + lax.broadcasted_iota(jnp.int32, (step, length), 1)
        for n in range(count // step):
            span = slice(n * step, (n + 1) * step)
            out, level = partial_attention(
                rows_ref[span, :], k_ref[0], v_ref[0], key_at <= w_ref[span, :]
            )
            if n * step < 2 * SEL:
                kept_ref[span, :width] = out
                kept_ref[span, width:] = jnp.broadcast_to(level, (step, width))
            if n * step >= SEL:
                high = level.astype(bf16).astype(f32)
                mid = (level - high).astype(bf16).astype(f32)
                low = level - high - mid
                pieces = jnp.where(lane == 0, high, jnp.where(lane == 1, mid, 0.0))
                pieces = jnp.where(lane == 2, low, pieces)
                to = slice(n * step - SEL, (n + 1) * step - SEL)
                for z in range(NZH):
                    back_ref[z, to, :width] = out.astype(bf16)
                    back_ref[z, to, width:] = pieces.astype(bf16)
        new_keys = jnp.concatenate([nm_ref[:TOKN_DEV, :], no_ref[:TOKN_DEV, :]], axis=0)
        new_values = jnp.concatenate([nm_ref[TOKN_DEV:, :], no_ref[TOKN_DEV:, :]], axis=0)
        out, level = partial_attention(
            own_ref[0, SEL:, :], new_keys, new_values, nk_ref[...] <= na_ref[...]
        )
        new_ref[:, :width] = out
        new_ref[:, width:] = jnp.broadcast_to(level, (TOKN_DEV, width))

    return call(
        kernel,
        "attend",
        (
            shape((NZH, back, 2 * width), bf16),
            shape((2 * SEL, 2 * width), f32),
            shape((TOKN_DEV, 2 * width), f32),
        ),
        control,
        queries,
        keys,
        values,
        wanted_at,
        own,
        new_mine,
        new_other,
        new_at,
        new_key_at,
        scratch=[pltpu.VMEM((count, width), bf16)],
    )


def merge_and_project(control, kept, new_part, returned, weights):
    width = new_part.shape[1] // 2
    count, part, _ = weights[0].shape
    halves = part // width
    blocks = len(weights) * count * halves

    def kernel(c_ref, kept_ref, new_ref, back_ref, *refs):
        weight_refs, (out_ref, att_ref) = refs[:-2], refs[-2:]
        first = c_ref[4] == 1
        kept = jnp.where(first, kept_ref[:SEL, :], kept_ref[SEL:, :])
        remote, remote_level = unpack(back_ref[c_ref[0], :SEL, :])
        remote_level = jnp.where(first, MASKED, remote_level)
        att_ref[:SEL, :] = merge(
            [(kept[:, :width], kept[:, width : width + 1]), (remote, remote_level)]
        )
        at = pl.multiple_of(SEL + c_ref[3] * TOKN_DEV, TOKN_DEV)
        parts = [(new_ref[:, :width], new_ref[:, width : width + 1])]
        for i in range(PPR):
            parts.append(unpack(back_ref[c_ref[1 + i], pl.ds(at, TOKN_DEV), :]))
        att_ref[SEL:, :] = merge(parts)
        attention = att_ref[...].astype(bf16)
        for j, ref in enumerate(weight_refs):
            for n in range(count):
                term = lax.dot_general(
                    attention, ref[n], (((1,), (1,)), ((), ())), preferred_element_type=f32
                ).astype(bf16)
                for h in range(halves):
                    out_ref[(j * count + n) * halves + h] = term[:, h * width : (h + 1) * width]

    out_weights = pl.BlockSpec((count, part, width), lambda i: (0, 0, 3))
    return pl.pallas_call(
        kernel,
        grid=(1,),
        out_shape=shape((blocks, ROW_DEV, width), bf16),
        in_specs=[SMEM, whole(kept), whole(new_part), whole(returned)]
        + [out_weights] * len(weights),
        out_specs=pl.BlockSpec((blocks, ROW_DEV, width), lambda i: (0, 0, 0)),
        scratch_shapes=[pltpu.VMEM((ROW_DEV, width), f32)],
        compiler_params=pltpu.CompilerParams(vmem_limit_bytes=16 << 20),
        name="merge_and_project",
    )(control, kept, new_part, returned, *weights)


def feed_forward(columns, summed, hidden, gain, parcels, units):
    blocks, rows, part = summed.shape
    model = blocks * part
    count, _, depth = parcels[0].shape
    parts = len(parcels)
    split = depth // part
    per = rows // (NZL * NX)
    contract_last = (((1,), (1,)), ((), ()))

    def kernel(c_ref, s_ref, x_ref, g_ref, *refs):
        parcel_refs = refs[:parts]
        out_ref, mixed_ref, within_ref, down_ref, acc_ref, within_sem, down_sem = refs[parts:]
        within = [
            pltpu.make_async_copy(
                parcel_refs[m // count].at[m % count, pl.ds(0, 2 * units)],
                within_ref.at[m],
                within_sem.at[m],
            )
            for m in range(parts * count)
        ]
        down = [
            pltpu.make_async_copy(
                parcel_refs[m // count].at[m % count, pl.ds(2 * units, units)],
                down_ref.at[m],
                down_sem.at[m],
            )
            for m in range(parts * count)
        ]
        for copy in within + down:
            copy.start()
        squares = jnp.zeros((rows, part), f32)
        for b in range(blocks):
            block = s_ref[b].astype(f32)
            squares = squares + block * block
        norm = lax.rsqrt(jnp.sum(squares, axis=1, keepdims=True) / model + EPSILON)
        for m in range(parts * count):
            cols = pl.ds(pl.multiple_of(c_ref[m] * depth, depth), depth)
            summed = jnp.concatenate([s_ref[m * split + h] for h in range(split)], axis=1)
            mixed = (
                x_ref[:, cols].astype(f32) + summed.astype(f32) * norm * g_ref[:, cols]
            ).astype(bf16)
            mixed_ref[:, cols] = mixed
            within[m].wait()
            product = lax.dot_general(
                within_ref[m], mixed, contract_last, preferred_element_type=f32
            )
            acc_ref[...] = product if m == 0 else acc_ref[...] + product
        to = lax.broadcasted_iota(jnp.int32, (rows, rows), 0)
        at = lax.broadcasted_iota(jnp.int32, (rows, rows), 1)
        source = (to // per) % NZL * (NX * per) + to // (NZL * per) * per + to % per
        move = jnp.where(at == source, 1.0, 0.0).astype(bf16)
        gate = acc_ref[:units, :]
        active = (gate / (1.0 + jnp.exp(-gate)) * acc_ref[units:, :]).astype(bf16)
        active = lax.dot_general(
            move, active, contract_last, preferred_element_type=f32
        ).astype(bf16)
        for m in range(parts * count):
            cols = pl.ds(pl.multiple_of(c_ref[m] * depth, depth), depth)
            down[m].wait()
            out_ref[:, cols] = jnp.dot(
                active, down_ref[m], preferred_element_type=f32
            ).astype(bf16)

    return pl.pallas_call(
        kernel,
        grid=(1,),
        out_shape=(shape((rows, model), bf16), shape((rows, model), bf16)),
        in_specs=[SMEM, whole(summed), whole(hidden), whole(gain)]
        + [pl.BlockSpec(memory_space=pl.ANY)] * parts,
        out_specs=(
            pl.BlockSpec((rows, model), lambda k: (0, 0)),
            pl.BlockSpec((rows, model), lambda k: (0, 0)),
        ),
        scratch_shapes=[
            pltpu.VMEM((parts * count, 2 * units, depth), bf16),
            pltpu.VMEM((parts * count, units, depth), bf16),
            pltpu.VMEM((2 * units, rows), f32),
            pltpu.SemaphoreType.DMA((parts * count,)),
            pltpu.SemaphoreType.DMA((parts * count,)),
        ],
        compiler_params=pltpu.CompilerParams(vmem_limit_bytes=24 << 20),
        name="feed_forward",
    )(columns, summed, hidden, gain, *parcels)


def shards(
    hidden_states,
    query_weight,
    key_weight,
    value_weight,
    output_weight,
    query_gain,
    key_gain,
    attention_gain,
    gate_weight,
    up_weight,
    down_weight,
    feedforward_gain,
    cached_keys,
    cached_values,
    passage_order,
    separators,
    recompute_index,
    prompt_lengths,
):
    y_at, zh, core = (lax.axis_index(a) for a in SEQ)
    zl, x_at = (lax.axis_index(a) for a in BLK)
    seq = y_at * 4 + zh * 2 + core
    width = query_weight.shape[1]
    hidden_units = gate_weight.shape[1]
    model = hidden_states.shape[1]
    blocks = NX * NZL
    rows = ROW_DEV // blocks

    mine = join_weights(query_weight, key_weight, value_weight, output_weight)
    theirs = swap(mine, "zh", NZH)
    near = copies_to_all(mine, "y", NY)
    parcel = jnp.concatenate([gate_weight.T, up_weight.T, down_weight])
    parcel = jnp.pad(parcel, ((0, -parcel.shape[0] % 16), (0, 0)))

    at, wanted_at, picked, new_at, new_key_at, attend_control, merge_control, columns = tables(
        seq, passage_order, separators, prompt_lengths, recompute_index
    )
    frequency = frequencies()
    angles = at * jnp.concatenate([frequency, frequency])[None, :]
    sign = jnp.where(jnp.arange(HD) < HD // 2, -1.0, 1.0).astype(f32)
    cosine, sine = jnp.cos(angles), jnp.sin(angles) * sign
    theirs, near, cosine, sine = lax.optimization_barrier((theirs, near, cosine, sine))
    turn_cosine, turn_sine = cosine[ROW_DEV : ROW_DEV + 1], sine[ROW_DEV : ROW_DEV + 1]
    cosine, sine = cosine[:ROW_DEV], sine[:ROW_DEV]

    near_other = swap(near, "core", NCORE)
    far = copies_to_all(theirs, "y", NY)
    far_other = swap(far, "core", NCORE)
    parcel_near = lax.all_gather(parcel, "y")
    weights = [near, near_other, far, far_other]
    raw, squares = project(columns, hidden_states, weights, width, blocks)
    squares = lax.all_to_all(squares, BLK, 0, 0, tiled=True)
    squares, parcel, parcel_near = lax.optimization_barrier((squares, parcel, parcel_near))
    pair = lax.all_gather(parcel, "zh")
    query, key, value, new_mine = finish_rows(
        raw, squares, query_gain[None], key_gain[None], cosine, sine, model
    )

    queries = lax.all_to_all(query, "zh", 0, 0, tiled=True)
    queries = copies_to_all(queries, "y", NY)
    queries = copies_to_all(queries, "core", NCORE).reshape(N_SEQ, ROW_DEV, width)
    new_other = swap(new_mine, "core", NCORE)
    blended_keys, blended_values = blend(
        picked, turn_cosine, turn_sine, cached_keys, cached_values, key, value
    )
    returned, kept, new_part = attend(
        attend_control,
        queries,
        blended_keys,
        blended_values,
        wanted_at,
        query,
        new_mine,
        new_other,
        new_at,
        new_key_at,
    )

    returned = lax.all_to_all(returned, "zh", 0, 0, tiled=True)
    returned = copies_to_all(returned, "y", NY)
    returned = copies_to_all(returned, "core", NCORE).reshape(N_SEQ, -1, 2 * width)

    terms = merge_and_project(merge_control, kept, new_part, returned, weights)
    terms, pair = lax.optimization_barrier((terms, pair))
    parcel_far = lax.all_gather(lax.dynamic_index_in_dim(pair, 1 - zh, 0, False), "y")
    terms = lax.all_to_all(terms.reshape(NX, NZL, ROW_DEV, width), "x", 0, 0, tiled=True)
    terms = jnp.sum(terms.astype(f32), axis=0).astype(bf16)
    terms = lax.all_to_all(terms, "zl", 0, 0, tiled=True)
    summed = jnp.sum(terms.astype(f32), axis=0).astype(bf16)
    summed = copies_to_all(summed, "zl", NZL)
    summed, parcel_far = lax.optimization_barrier((summed, parcel_far))
    summed = copies_to_all(summed, "x", NX).reshape(blocks, ROW_DEV, model // blocks)

    parcels = [parcel_near, swap(parcel_near, "core", NCORE)]
    parcels += [parcel_far, swap(parcel_far, "core", NCORE)]
    terms, mixed = feed_forward(
        columns, summed, hidden_states, attention_gain[None], parcels, hidden_units
    )
    terms = lax.all_to_all(terms.reshape(NX, NZL * rows, model), "x", 0, 0, tiled=True)
    terms = jnp.sum(terms.astype(f32), axis=0).astype(bf16)
    terms = lax.all_to_all(terms.reshape(NZL, rows, model), "zl", 0, 0, tiled=True)
    total = jnp.sum(terms.astype(f32), axis=0)
    norm = lax.rsqrt(jnp.mean(total * total, axis=1, keepdims=True) + EPSILON)
    my_rows = lax.dynamic_slice_in_dim(mixed, (zl * NX + x_at) * rows, rows, 0)
    hidden_out = (my_rows.astype(f32) + total * norm * feedforward_gain).astype(bf16)
    return (hidden_out, blended_keys, blended_values)


def solution(mesh):
    fine = Mesh(
        mesh.devices.reshape(NY, NZH, NCORE, NZL, NX), ("y", "zh", "core", "zl", "x")
    )
    by_both = P(SEQ, BLK)
    return jax.shard_map(
        shards,
        mesh=fine,
        in_specs=(
            P(SEQ, None),
            by_both,
            by_both,
            by_both,
            P(BLK, SEQ),
            P(BLK),
            P(BLK),
            P(),
            by_both,
            by_both,
            P(BLK, SEQ),
            P(),
            P(SEQ, None, BLK),
            P(SEQ, None, BLK),
            P(),
            P(),
            P(),
            P(),
        ),
        out_specs=(P(SEQ + BLK, None), P(SEQ, None, BLK), P(SEQ, None, BLK)),
        check_vma=False,
    )
```

```python
import functools
import math

import jax
import jax.numpy as jnp
from jax import lax
from jax.experimental import pallas as pl
from jax.experimental.pallas import tpu as pltpu
from jax.sharding import Mesh, PartitionSpec as P

HD = 128
PLEN = 1024
SEL = 96
PPR = 2
TOKN_DEV = 32
ROW_DEV = 128
LEVEL_ROWS = 16

EPSILON = 1e-06
ROPE_THETA = 500000.0
MASKED = -1e30

SEQ = ("y", "zh", "core")
BLK = ("zl", "x")
NY, NZH, NCORE, NZL, NX = 4, 2, 2, 8, 4
N_SEQ = NY * NZH * NCORE
bf16 = jnp.bfloat16
f32 = jnp.float32


def frequencies():
    indices = jnp.arange(HD // 2, dtype=f32)
    return jnp.exp(indices * (-2.0 * math.log(ROPE_THETA) / HD))


def copies_to_all(a, axis, count):
    return lax.all_to_all(
        jnp.broadcast_to(a[None], (count,) + a.shape), axis, 0, 0, tiled=True
    )


def gather_seq(a):
    a = copies_to_all(a, "zh", NZH)
    a = copies_to_all(a, "y", NY)
    a = copies_to_all(a, "core", NCORE)
    return a.reshape((N_SEQ,) + a.shape[3:])


def swap(a, axis, count):
    return lax.ppermute(a, axis, [(i, i ^ 1) for i in range(count)])


def partial_attention(queries, keys, values, visible):
    scores = lax.dot_general(
        queries, keys, (((1,), (1,)), ((), ())), preferred_element_type=f32
    ) * HD ** (-0.5)
    scores = jnp.where(visible, scores, MASKED)
    peak = jnp.max(scores, axis=1, keepdims=True)
    weights = jnp.where(visible, jnp.exp(scores - peak), 0.0)
    total = jnp.sum(weights, axis=1, keepdims=True)
    some = total > 0.0
    safe = jnp.where(some, total, 1.0)
    out = jnp.dot(weights.astype(bf16), values, preferred_element_type=f32) / safe
    return out, jnp.where(some, peak + jnp.log(safe), MASKED)


def merge(parts):
    top = parts[0][1]
    for _, level in parts[1:]:
        top = jnp.maximum(top, level)
    num = 0.0
    den = 0.0
    for out, level in parts:
        w = jnp.exp(level - top)
        num = num + w * out
        den = den + w
    return num / den


def pieces_of(level):
    high = level.astype(bf16).astype(f32)
    mid = (level - high).astype(bf16).astype(f32)
    return high, mid, level - high - mid


def whole(a):
    return pl.BlockSpec(a.shape, lambda *k: (0,) * len(a.shape))


SMEM = pl.BlockSpec(memory_space=pltpu.SMEM)


def call(kernel, name, out_shape, *args, scratch=(), limit=16):
    small = [a.ndim == 1 for a in args]
    return pl.pallas_call(
        kernel,
        grid=(1,),
        out_shape=out_shape,
        in_specs=[SMEM if one else whole(a) for a, one in zip(args, small)],
        out_specs=jax.tree.map(lambda a: SMEM if len(a.shape) == 1 else whole(a), out_shape),
        scratch_shapes=list(scratch),
        compiler_params=pltpu.CompilerParams(vmem_limit_bytes=limit << 20),
        name=name,
    )(*args)


def shape(dims, dtype):
    return jax.ShapeDtypeStruct(dims, dtype)


def tables(seq, passage_order, separators, prompt_lengths, recompute_index):
    spare = 8

    def kernel(
        s_ref, o_ref, sep_ref, len_ref, i_ref, t_ref,
        at_ref, wanted_ref, picked_ref, new_ref, new_key_ref, attend_ref, merge_ref, column_ref,
    ):
        seq = s_ref[0]
        place = jnp.int32(0)
        for n in range(N_SEQ):
            place = jnp.where(o_ref[n] == seq, n, place)

        def start_of(request, slot):
            first = sep_ref[2 * request]
            return first + jnp.where(slot == 1, PLEN + sep_ref[2 * request + 1], 0)

        request, mine = place >> 1, seq >> 1
        chosen = [o_ref[2 * request + i] for i in range(PPR)]
        start = start_of(request, place & 1)
        base = start_of(request, 1) + PLEN
        my_base = start_of(mine, 1) + PLEN
        my_from = (seq & 1) * TOKN_DEV

        lane = lax.broadcasted_iota(jnp.int32, (SEL, N_SEQ), 1)
        index = t_ref[...].astype(f32)

        def column(passage):
            return jnp.sum(jnp.where(lane == passage, index, 0.0), axis=1, keepdims=True)

        count = PPR * TOKN_DEV
        down = lax.broadcasted_iota(jnp.int32, (count, 1), 0)
        at_ref[:SEL, :] = column(seq) + start.astype(f32)
        at_ref[SEL:ROW_DEV, :] = (my_base + my_from + down[:TOKN_DEV]).astype(f32)
        at_ref[ROW_DEV:, :] = jnp.full((spare, 1), start, jnp.int32).astype(f32)
        for i in range(PPR):
            at = column(chosen[i]) + start_of(request, i).astype(f32)
            wanted_ref[i * SEL : (i + 1) * SEL, :] = at.astype(jnp.int32)
        wanted_ref[PPR * SEL :, :] = base + down
        picked_ref[...] = jnp.full((1, HD), -1, jnp.int32)
        picked_ref[:, :SEL] = i_ref[pl.ds(seq, 1), :]
        new_ref[...] = my_base + my_from + down[:TOKN_DEV]
        across = lax.broadcasted_iota(jnp.int32, (1, count), 1)
        token = across ^ my_from
        new_key_ref[...] = jnp.where(token < len_ref[mine], my_base + token, 1 << 30)

        def slot(s):
            return (s & 1) * 8 + (s >> 2) * 2 + ((s >> 1) & 1)

        attend_ref[0] = slot(chosen[0])
        attend_ref[1] = slot(chosen[1])
        attend_ref[2] = slot(2 * request)
        attend_ref[3] = slot(2 * request + 1)
        attend_ref[4] = start
        merge_ref[0] = slot(chosen[0])
        merge_ref[1] = slot(o_ref[2 * mine])
        merge_ref[2] = slot(o_ref[2 * mine + 1])
        merge_ref[3] = seq & 1
        merge_ref[4] = jnp.where(chosen[0] == seq, 1, 0)
        for m in range(N_SEQ):
            other = (m // 8) * 2 + m // 4 % 2
            column_ref[m] = m % 4 * 4 + ((seq & 3) ^ other)

    i32 = jnp.int32
    return call(
        kernel,
        "tables",
        (
            shape((ROW_DEV + spare, 1), f32),
            shape((PPR * (SEL + TOKN_DEV), 1), i32),
            shape((1, HD), i32),
            shape((TOKN_DEV, 1), i32),
            shape((1, PPR * TOKN_DEV), i32),
            shape((5,), i32),
            shape((5,), i32),
            shape((N_SEQ,), i32),
        ),
        seq[None],
        passage_order,
        separators.reshape(-1),
        prompt_lengths,
        recompute_index,
        recompute_index.T,
    )


def join_weights(query_weight, key_weight, value_weight, output_weight):
    depth, width = query_weight.shape

    def kernel(q_ref, k_ref, v_ref, o_ref, out_ref):
        for n, ref in enumerate((q_ref, k_ref, v_ref)):
            out_ref[:, n * width : (n + 1) * width] = ref[...]
        out_ref[:, 3 * width :] = jnp.transpose(o_ref[...].astype(f32)).astype(bf16)

    return call(
        kernel,
        "join_weights",
        shape((depth, 4 * width), bf16),
        query_weight,
        key_weight,
        value_weight,
        output_weight,
    )


def project(columns, hidden, weights, width, copies):
    rows = hidden.shape[0]
    count, depth, _ = weights[0].shape

    def kernel(c_ref, x_ref, *refs):
        weight_refs, (raw_ref, squares_ref) = refs[:-2], refs[-2:]
        raw = jnp.zeros((rows, 3 * width), f32)
        for m in range(len(weight_refs) * count):
            at = pl.multiple_of(c_ref[m] * depth, depth)
            raw = raw + jnp.dot(
                x_ref[:, pl.ds(at, depth)],
                weight_refs[m // count][m % count, :, : 3 * width],
                preferred_element_type=f32,
            )
        raw_ref[...] = raw
        query, key = raw[:, :width], raw[:, width : 2 * width]
        lane = lax.broadcasted_iota(jnp.int32, (rows, width), 1)
        sums = jnp.where(lane == 0, jnp.sum(query * query, axis=1, keepdims=True), 0.0)
        sums = jnp.where(lane == 1, jnp.sum(key * key, axis=1, keepdims=True), sums)
        sums = jnp.transpose(sums)[:8]
        for b in range(copies):
            squares_ref[b] = sums

    return call(
        kernel,
        "project",
        (shape((rows, 3 * width), f32), shape((copies, 8, rows), f32)),
        columns,
        hidden,
        *weights,
    )


def turn_by(x, cosine, sine):
    return x * cosine + pltpu.roll(x, HD // 2, 1) * sine


def finish_rows(raw, squares, query_gain, key_gain, cosine, sine, model):
    rows = raw.shape[0]
    width = query_gain.shape[1]
    copies = squares.shape[0]

    def kernel(raw_ref, s_ref, gq_ref, gk_ref, c_ref, t_ref, q_ref, k_ref, v_ref, new_ref):
        sums = s_ref[0]
        for b in range(1, copies):
            sums = sums + s_ref[b]
        sums = jnp.concatenate([sums, jnp.zeros((width - 8, rows), f32)], axis=0)
        scale = lax.rsqrt(jnp.transpose(sums) / model + EPSILON)
        raw = raw_ref[...]
        query = raw[:, :width] * scale[:, 0:1] * gq_ref[...]
        key = raw[:, width : 2 * width] * scale[:, 1:2] * gk_ref[...]
        query = turn_by(query, c_ref[...], t_ref[...]).astype(bf16)
        key = turn_by(key, c_ref[...], t_ref[...]).astype(bf16)
        value = raw[:, 2 * width :].astype(bf16)
        for z in range(NZH):
            q_ref[z] = query
        k_ref[...] = key
        v_ref[...] = value
        new_ref[:TOKN_DEV, :] = key[SEL:]
        new_ref[TOKN_DEV:, :] = value[SEL:]

    return call(
        kernel,
        "finish_rows",
        (
            shape((NZH, rows, width), bf16),
            shape((rows, width), bf16),
            shape((rows, width), bf16),
            shape((2 * TOKN_DEV, width), bf16),
        ),
        raw,
        squares,
        query_gain,
        key_gain,
        cosine,
        sine,
    )


def blend(picked, cosine, sine, keys, values, new_keys, new_values):
    _, length, width = keys.shape
    steps = 4
    chunk = length // steps

    def kernel(p_ref, c_ref, t_ref, k_ref, v_ref, nk_ref, nv_ref, bk_ref, bv_ref):
        at = lax.broadcasted_iota(jnp.int32, (chunk, width), 0) + pl.program_id(0) * chunk
        hit = (at == p_ref[...]).astype(f32)
        here = jnp.max(hit, axis=1, keepdims=True) > 0.0
        hit = hit.astype(bf16)
        turned = turn_by(k_ref[0].astype(f32), c_ref[...], t_ref[...])
        placed = jnp.dot(hit, nk_ref[...], preferred_element_type=f32)
        bk_ref[0] = jnp.where(here, placed, turned).astype(bf16)
        placed = jnp.dot(hit, nv_ref[...], preferred_element_type=f32)
        bv_ref[0] = jnp.where(here, placed, v_ref[0].astype(f32)).astype(bf16)

    tile = pl.BlockSpec((1, chunk, width), lambda k: (0, k, 0))
    return pl.pallas_call(
        kernel,
        grid=(steps,),
        out_shape=(shape(keys.shape, bf16), shape(keys.shape, bf16)),
        in_specs=[
            whole(picked),
            whole(cosine),
            whole(sine),
            tile,
            tile,
            whole(new_keys),
            whole(new_values),
        ],
        out_specs=(tile, tile),
        compiler_params=pltpu.CompilerParams(vmem_limit_bytes=8 << 20),
        name="blend",
    )(picked, cosine, sine, keys, values, new_keys, new_values)


def attend(control, queries, keys, values, wanted_at, own, new_mine, new_other, new_at, new_key_at):
    width = keys.shape[2]
    length = keys.shape[1]
    cuts = [(0, SEL), (0, SEL), (SEL, ROW_DEV), (SEL, ROW_DEV)]
    count = sum(high - low for low, high in cuts)
    back = count - SEL
    step = 32

    def kernel(
        c_ref, q_ref, k_ref, v_ref, w_ref, own_ref, nm_ref, no_ref, na_ref, nk_ref,
        back_ref, kept_ref, new_ref, rows_ref, level_ref,
    ):
        at = 0
        for i, (low, high) in enumerate(cuts):
            rows_ref[at : at + high - low, :] = q_ref[c_ref[i], low:high, :]
            at += high - low
        key_at = c_ref[4] + lax.broadcasted_iota(jnp.int32, (step, length), 1)
        for n in range(count // step):
            span = slice(n * step, (n + 1) * step)
            out, level = partial_attention(
                rows_ref[span, :], k_ref[0], v_ref[0], key_at <= w_ref[span, :]
            )
            level = jnp.broadcast_to(level, (step, width))
            if n * step < 2 * SEL:
                kept_ref[span, :width] = out
                kept_ref[span, width:] = level
            if n * step >= SEL:
                to = slice(n * step - SEL, (n + 1) * step - SEL)
                level_ref[to, :] = level
                for z in range(NZH):
                    back_ref[z, to, :] = out.astype(bf16)
        level_ref[back:, :] = jnp.zeros((2 * width - back, width), f32)
        lines = [jnp.transpose(level_ref[i * width : (i + 1) * width, :])[:1] for i in range(2)]
        lines = [piece for line in lines for piece in pieces_of(line)]
        lines.append(jnp.zeros((LEVEL_ROWS - len(lines), width), f32))
        lines = jnp.concatenate(lines, axis=0).astype(bf16)
        for z in range(NZH):
            back_ref[z, back:, :] = lines
        new_keys = jnp.concatenate([nm_ref[:TOKN_DEV, :], no_ref[:TOKN_DEV, :]], axis=0)
        new_values = jnp.concatenate([nm_ref[TOKN_DEV:, :], no_ref[TOKN_DEV:, :]], axis=0)
        out, level = partial_attention(
            own_ref[0, SEL:, :], new_keys, new_values, nk_ref[...] <= na_ref[...]
        )
        new_ref[:, :width] = out
        new_ref[:, width:] = jnp.broadcast_to(level, (TOKN_DEV, width))

    return call(
        kernel,
        "attend",
        (
            shape((NZH, back + LEVEL_ROWS, width), bf16),
            shape((2 * SEL, 2 * width), f32),
            shape((TOKN_DEV, 2 * width), f32),
        ),
        control,
        queries,
        keys,
        values,
        wanted_at,
        own,
        new_mine,
        new_other,
        new_at,
        new_key_at,
        scratch=[pltpu.VMEM((count, width), bf16), pltpu.VMEM((2 * width, width), f32)],
    )


def merge_and_project(control, kept, new_part, returned, weights):
    width = new_part.shape[1] // 2
    count, part, _ = weights[0].shape
    halves = part // width
    blocks = len(weights) * count * halves
    back = returned.shape[1] - LEVEL_ROWS

    def kernel(c_ref, kept_ref, new_ref, back_ref, *refs):
        weight_refs, (out_ref, att_ref) = refs[:-2], refs[-2:]
        def levels(source):
            lines = back_ref[source, back:, :].astype(f32)
            lines = jnp.concatenate([lines, jnp.zeros((width - LEVEL_ROWS, width), f32)], axis=0)
            lines = jnp.transpose(lines)
            return [
                lines[:, n : n + 1] + lines[:, n + 1 : n + 2] + lines[:, n + 2 : n + 3]
                for n in (0, 3)
            ]

        first = c_ref[4] == 1
        kept = jnp.where(first, kept_ref[:SEL, :], kept_ref[SEL:, :])
        remote = back_ref[c_ref[0], :SEL, :].astype(f32)
        remote_level = jnp.where(first, MASKED, levels(c_ref[0])[0][:SEL])
        att_ref[:SEL, :] = merge(
            [(kept[:, :width], kept[:, width : width + 1]), (remote, remote_level)]
        )
        at = pl.multiple_of(SEL + c_ref[3] * TOKN_DEV, TOKN_DEV)
        parts = [(new_ref[:, :width], new_ref[:, width : width + 1])]
        for i in range(PPR):
            column = levels(c_ref[1 + i])
            level = jnp.where(c_ref[3] == 0, column[0][SEL:], column[1][:TOKN_DEV])
            parts.append((back_ref[c_ref[1 + i], pl.ds(at, TOKN_DEV), :].astype(f32), level))
        att_ref[SEL:, :] = merge(parts)
        attention = att_ref[...].astype(bf16)
        for j, ref in enumerate(weight_refs):
            for n in range(count):
                term = lax.dot_general(
                    attention, ref[n], (((1,), (1,)), ((), ())), preferred_element_type=f32
                ).astype(bf16)
                for h in range(halves):
                    out_ref[(j * count + n) * halves + h] = term[:, h * width : (h + 1) * width]

    out_weights = pl.BlockSpec((count, part, width), lambda i: (0, 0, 3))
    return pl.pallas_call(
        kernel,
        grid=(1,),
        out_shape=shape((blocks, ROW_DEV, width), bf16),
        in_specs=[SMEM, whole(kept), whole(new_part), whole(returned)]
        + [out_weights] * len(weights),
        out_specs=pl.BlockSpec((blocks, ROW_DEV, width), lambda i: (0, 0, 0)),
        scratch_shapes=[pltpu.VMEM((ROW_DEV, width), f32)],
        compiler_params=pltpu.CompilerParams(vmem_limit_bytes=16 << 20),
        name="merge_and_project",
    )(control, kept, new_part, returned, *weights)


def feed_forward(columns, summed, hidden, gain, parcels, units):
    blocks, rows, part = summed.shape
    model = blocks * part
    count, _, depth = parcels[0].shape
    parts = len(parcels)
    split = depth // part
    per = rows // (NZL * NX)
    contract_last = (((1,), (1,)), ((), ()))

    def kernel(c_ref, s_ref, x_ref, g_ref, *refs):
        parcel_refs = refs[:parts]
        out_ref, mixed_ref, within_ref, down_ref, acc_ref, within_sem, down_sem = refs[parts:]
        within = [
            pltpu.make_async_copy(
                parcel_refs[m // count].at[m % count, pl.ds(0, 2 * units)],
                within_ref.at[m],
                within_sem.at[m],
            )
            for m in range(parts * count)
        ]
        down = [
            pltpu.make_async_copy(
                parcel_refs[m // count].at[m % count, pl.ds(2 * units, units)],
                down_ref.at[m],
                down_sem.at[m],
            )
            for m in range(parts * count)
        ]
        for copy in within + down:
            copy.start()
        squares = jnp.zeros((rows, part), f32)
        for b in range(blocks):
            block = s_ref[b].astype(f32)
            squares = squares + block * block
        norm = lax.rsqrt(jnp.sum(squares, axis=1, keepdims=True) / model + EPSILON)
        for m in range(parts * count):
            cols = pl.ds(pl.multiple_of(c_ref[m] * depth, depth), depth)
            summed = jnp.concatenate([s_ref[m * split + h] for h in range(split)], axis=1)
            mixed = (
                x_ref[:, cols].astype(f32) + summed.astype(f32) * norm * g_ref[:, cols]
            ).astype(bf16)
            mixed_ref[:, cols] = mixed
            within[m].wait()
            product = lax.dot_general(
                within_ref[m], mixed, contract_last, preferred_element_type=f32
            )
            acc_ref[...] = product if m == 0 else acc_ref[...] + product
        to = lax.broadcasted_iota(jnp.int32, (rows, rows), 0)
        at = lax.broadcasted_iota(jnp.int32, (rows, rows), 1)
        source = (to // per) % NZL * (NX * per) + to // (NZL * per) * per + to % per
        move = jnp.where(at == source, 1.0, 0.0).astype(bf16)
        gate = acc_ref[:units, :]
        active = (gate / (1.0 + jnp.exp(-gate)) * acc_ref[units:, :]).astype(bf16)
        active = lax.dot_general(
            move, active, contract_last, preferred_element_type=f32
        ).astype(bf16)
        for m in range(parts * count):
            cols = pl.ds(pl.multiple_of(c_ref[m] * depth, depth), depth)
            down[m].wait()
            out_ref[:, cols] = jnp.dot(
                active, down_ref[m], preferred_element_type=f32
            ).astype(bf16)

    return pl.pallas_call(
        kernel,
        grid=(1,),
        out_shape=(shape((rows, model), bf16), shape((rows, model), bf16)),
        in_specs=[SMEM, whole(summed), whole(hidden), whole(gain)]
        + [pl.BlockSpec(memory_space=pl.ANY)] * parts,
        out_specs=(
            pl.BlockSpec((rows, model), lambda k: (0, 0)),
            pl.BlockSpec((rows, model), lambda k: (0, 0)),
        ),
        scratch_shapes=[
            pltpu.VMEM((parts * count, 2 * units, depth), bf16),
            pltpu.VMEM((parts * count, units, depth), bf16),
            pltpu.VMEM((2 * units, rows), f32),
            pltpu.SemaphoreType.DMA((parts * count,)),
            pltpu.SemaphoreType.DMA((parts * count,)),
        ],
        compiler_params=pltpu.CompilerParams(vmem_limit_bytes=24 << 20),
        name="feed_forward",
    )(columns, summed, hidden, gain, *parcels)


def shards(
    hidden_states,
    query_weight,
    key_weight,
    value_weight,
    output_weight,
    query_gain,
    key_gain,
    attention_gain,
    gate_weight,
    up_weight,
    down_weight,
    feedforward_gain,
    cached_keys,
    cached_values,
    passage_order,
    separators,
    recompute_index,
    prompt_lengths,
):
    y_at, zh, core = (lax.axis_index(a) for a in SEQ)
    zl, x_at = (lax.axis_index(a) for a in BLK)
    seq = y_at * 4 + zh * 2 + core
    width = query_weight.shape[1]
    hidden_units = gate_weight.shape[1]
    model = hidden_states.shape[1]
    blocks = NX * NZL
    rows = ROW_DEV // blocks

    mine = join_weights(query_weight, key_weight, value_weight, output_weight)
    theirs = swap(mine, "zh", NZH)
    near = copies_to_all(mine, "y", NY)
    parcel = jnp.concatenate([gate_weight.T, up_weight.T, down_weight])
    parcel = jnp.pad(parcel, ((0, -parcel.shape[0] % 16), (0, 0)))

    at, wanted_at, picked, new_at, new_key_at, attend_control, merge_control, columns = tables(
        seq, passage_order, separators, prompt_lengths, recompute_index
    )
    frequency = frequencies()
    angles = at * jnp.concatenate([frequency, frequency])[None, :]
    sign = jnp.where(jnp.arange(HD) < HD // 2, -1.0, 1.0).astype(f32)
    cosine, sine = jnp.cos(angles), jnp.sin(angles) * sign
    theirs, near, cosine, sine = lax.optimization_barrier((theirs, near, cosine, sine))
    turn_cosine, turn_sine = cosine[ROW_DEV : ROW_DEV + 1], sine[ROW_DEV : ROW_DEV + 1]
    cosine, sine = cosine[:ROW_DEV], sine[:ROW_DEV]

    near_other = swap(near, "core", NCORE)
    far = copies_to_all(theirs, "y", NY)
    far_other = swap(far, "core", NCORE)
    weights = [near, near_other, far, far_other]
    raw, squares = project(columns, hidden_states, weights, width, blocks)
    squares = lax.all_to_all(squares, BLK, 0, 0, tiled=True)
    squares, parcel = lax.optimization_barrier((squares, parcel))
    pair = lax.all_gather(parcel, "zh")
    query, key, value, new_mine = finish_rows(
        raw, squares, query_gain[None], key_gain[None], cosine, sine, model
    )

    queries = lax.all_to_all(query, "zh", 0, 0, tiled=True)
    queries = copies_to_all(queries, "y", NY)
    queries = copies_to_all(queries, "core", NCORE).reshape(N_SEQ, ROW_DEV, width)
    new_other = swap(new_mine, "core", NCORE)
    blended_keys, blended_values = blend(
        picked, turn_cosine, turn_sine, cached_keys, cached_values, key, value
    )
    returned, kept, new_part = attend(
        attend_control,
        queries,
        blended_keys,
        blended_values,
        wanted_at,
        query,
        new_mine,
        new_other,
        new_at,
        new_key_at,
    )

    returned = lax.all_to_all(returned, "zh", 0, 0, tiled=True)
    returned = copies_to_all(returned, "y", NY)
    returned = copies_to_all(returned, "core", NCORE).reshape(N_SEQ, -1, width)

    terms = merge_and_project(merge_control, kept, new_part, returned, weights)
    terms, pair, parcel = lax.optimization_barrier((terms, pair, parcel))
    parcel_near = lax.all_gather(parcel, "y")
    parcel_far = lax.all_gather(lax.dynamic_index_in_dim(pair, 1 - zh, 0, False), "y")
    terms = lax.all_to_all(terms.reshape(NX, NZL, ROW_DEV, width), "x", 0, 0, tiled=True)
    terms = jnp.sum(terms.astype(f32), axis=0).astype(bf16)
    terms = lax.all_to_all(terms, "zl", 0, 0, tiled=True)
    summed = jnp.sum(terms.astype(f32), axis=0).astype(bf16)
    summed = copies_to_all(summed, "zl", NZL)
    summed, parcel_near, parcel_far = lax.optimization_barrier((summed, parcel_near, parcel_far))
    summed = copies_to_all(summed, "x", NX).reshape(blocks, ROW_DEV, model // blocks)

    parcels = [parcel_near, swap(parcel_near, "core", NCORE)]
    parcels += [parcel_far, swap(parcel_far, "core", NCORE)]
    terms, mixed = feed_forward(
        columns, summed, hidden_states, attention_gain[None], parcels, hidden_units
    )
    terms = lax.all_to_all(terms.reshape(NX, NZL * rows, model), "x", 0, 0, tiled=True)
    terms = jnp.sum(terms.astype(f32), axis=0).astype(bf16)
    terms = lax.all_to_all(terms.reshape(NZL, rows, model), "zl", 0, 0, tiled=True)
    total = jnp.sum(terms.astype(f32), axis=0)
    norm = lax.rsqrt(jnp.mean(total * total, axis=1, keepdims=True) + EPSILON)
    my_rows = lax.dynamic_slice_in_dim(mixed, (zl * NX + x_at) * rows, rows, 0)
    hidden_out = (my_rows.astype(f32) + total * norm * feedforward_gain).astype(bf16)
    return (hidden_out, blended_keys, blended_values)


def solution(mesh):
    fine = Mesh(
        mesh.devices.reshape(NY, NZH, NCORE, NZL, NX), ("y", "zh", "core", "zl", "x")
    )
    by_both = P(SEQ, BLK)
    return jax.shard_map(
        shards,
        mesh=fine,
        in_specs=(
            P(SEQ, None),
            by_both,
            by_both,
            by_both,
            P(BLK, SEQ),
            P(BLK),
            P(BLK),
            P(),
            by_both,
            by_both,
            P(BLK, SEQ),
            P(),
            P(SEQ, None, BLK),
            P(SEQ, None, BLK),
            P(),
            P(),
            P(),
            P(),
        ),
        out_specs=(P(SEQ + BLK, None), P(SEQ, None, BLK), P(SEQ, None, BLK)),
        check_vma=False,
    )
```

```python
import functools
import math

import jax
import jax.numpy as jnp
from jax import lax
from jax.experimental import pallas as pl
from jax.experimental.pallas import tpu as pltpu
from jax.sharding import Mesh, PartitionSpec as P

HD = 128
PLEN = 1024
SEL = 96
PPR = 2
TOKN_DEV = 32
ROW_DEV = 128
LEVEL_ROWS = 16

EPSILON = 1e-06
ROPE_THETA = 500000.0
MASKED = -1e30

SEQ = ("y", "zh", "core")
BLK = ("zl", "x")
NY, NZH, NCORE, NZL, NX = 4, 2, 2, 8, 4
N_SEQ = NY * NZH * NCORE
bf16 = jnp.bfloat16
f32 = jnp.float32


def frequencies():
    indices = jnp.arange(HD // 2, dtype=f32)
    return jnp.exp(indices * (-2.0 * math.log(ROPE_THETA) / HD))


def copies_to_all(a, axis, count):
    return lax.all_to_all(
        jnp.broadcast_to(a[None], (count,) + a.shape), axis, 0, 0, tiled=True
    )


def gather_seq(a):
    a = copies_to_all(a, "zh", NZH)
    a = copies_to_all(a, "y", NY)
    a = copies_to_all(a, "core", NCORE)
    return a.reshape((N_SEQ,) + a.shape[3:])


def swap(a, axis, count):
    return lax.ppermute(a, axis, [(i, i ^ 1) for i in range(count)])


def partial_attention(queries, keys, values, visible):
    scores = lax.dot_general(
        queries, keys, (((1,), (1,)), ((), ())), preferred_element_type=f32
    ) * HD ** (-0.5)
    scores = jnp.where(visible, scores, MASKED)
    peak = jnp.max(scores, axis=1, keepdims=True)
    weights = jnp.where(visible, jnp.exp(scores - peak), 0.0)
    total = jnp.sum(weights, axis=1, keepdims=True)
    some = total > 0.0
    safe = jnp.where(some, total, 1.0)
    out = jnp.dot(weights.astype(bf16), values, preferred_element_type=f32) / safe
    return out, jnp.where(some, peak + jnp.log(safe), MASKED)


def merge(parts):
    top = parts[0][1]
    for _, level in parts[1:]:
        top = jnp.maximum(top, level)
    num = 0.0
    den = 0.0
    for out, level in parts:
        w = jnp.exp(level - top)
        num = num + w * out
        den = den + w
    return num / den


def pieces_of(level):
    high = level.astype(bf16).astype(f32)
    mid = (level - high).astype(bf16).astype(f32)
    return high, mid, level - high - mid


def whole(a):
    return pl.BlockSpec(a.shape, lambda *k: (0,) * len(a.shape))


SMEM = pl.BlockSpec(memory_space=pltpu.SMEM)
VMEM = pl.BlockSpec(memory_space=pltpu.VMEM)


def call(kernel, name, out_shape, *args, scratch=(), limit=16):
    small = [a.ndim == 1 for a in args]
    return pl.pallas_call(
        kernel,
        out_shape=out_shape,
        in_specs=[SMEM if one else VMEM for one in small],
        out_specs=jax.tree.map(lambda a: SMEM if len(a.shape) == 1 else VMEM, out_shape),
        scratch_shapes=list(scratch),
        compiler_params=pltpu.CompilerParams(vmem_limit_bytes=limit << 20),
        name=name,
    )(*args)


def shape(dims, dtype):
    return jax.ShapeDtypeStruct(dims, dtype)


def tables(seq, passage_order, separators, prompt_lengths, recompute_index):
    spare = 8

    def kernel(
        s_ref, o_ref, sep_ref, len_ref, i_ref, t_ref,
        at_ref, wanted_ref, picked_ref, new_ref, new_key_ref, attend_ref, merge_ref, column_ref,
    ):
        seq = s_ref[0]
        place = jnp.int32(0)
        for n in range(N_SEQ):
            place = jnp.where(o_ref[n] == seq, n, place)

        def start_of(request, slot):
            first = sep_ref[2 * request]
            return first + jnp.where(slot == 1, PLEN + sep_ref[2 * request + 1], 0)

        request, mine = place >> 1, seq >> 1
        chosen = [o_ref[2 * request + i] for i in range(PPR)]
        start = start_of(request, place & 1)
        base = start_of(request, 1) + PLEN
        my_base = start_of(mine, 1) + PLEN
        my_from = (seq & 1) * TOKN_DEV

        lane = lax.broadcasted_iota(jnp.int32, (SEL, N_SEQ), 1)
        index = t_ref[...].astype(f32)

        def column(passage):
            return jnp.sum(jnp.where(lane == passage, index, 0.0), axis=1, keepdims=True)

        count = PPR * TOKN_DEV
        down = lax.broadcasted_iota(jnp.int32, (count, 1), 0)
        at_ref[:SEL, :] = column(seq) + start.astype(f32)
        at_ref[SEL:ROW_DEV, :] = (my_base + my_from + down[:TOKN_DEV]).astype(f32)
        at_ref[ROW_DEV:, :] = jnp.full((spare, 1), start, jnp.int32).astype(f32)
        for i in range(PPR):
            at = column(chosen[i]) + start_of(request, i).astype(f32)
            wanted_ref[i * SEL : (i + 1) * SEL, :] = at.astype(jnp.int32)
        wanted_ref[PPR * SEL :, :] = base + down
        picked_ref[...] = jnp.full((1, HD), -1, jnp.int32)
        picked_ref[:, :SEL] = i_ref[pl.ds(seq, 1), :]
        new_ref[...] = my_base + my_from + down[:TOKN_DEV]
        across = lax.broadcasted_iota(jnp.int32, (1, count), 1)
        token = across ^ my_from
        new_key_ref[...] = jnp.where(token < len_ref[mine], my_base + token, 1 << 30)

        def slot(s):
            return (s & 1) * 8 + (s >> 2) * 2 + ((s >> 1) & 1)

        attend_ref[0] = slot(chosen[0])
        attend_ref[1] = slot(chosen[1])
        attend_ref[2] = slot(2 * request)
        attend_ref[3] = slot(2 * request + 1)
        attend_ref[4] = start
        merge_ref[0] = slot(chosen[0])
        merge_ref[1] = slot(o_ref[2 * mine])
        merge_ref[2] = slot(o_ref[2 * mine + 1])
        merge_ref[3] = seq & 1
        merge_ref[4] = jnp.where(chosen[0] == seq, 1, 0)
        for m in range(N_SEQ):
            other = (m // 8) * 2 + m // 4 % 2
            column_ref[m] = m % 4 * 4 + ((seq & 3) ^ other)

    i32 = jnp.int32
    return call(
        kernel,
        "tables",
        (
            shape((ROW_DEV + spare, 1), f32),
            shape((PPR * (SEL + TOKN_DEV), 1), i32),
            shape((1, HD), i32),
            shape((TOKN_DEV, 1), i32),
            shape((1, PPR * TOKN_DEV), i32),
            shape((5,), i32),
            shape((5,), i32),
            shape((N_SEQ,), i32),
        ),
        seq[None],
        passage_order,
        separators.reshape(-1),
        prompt_lengths,
        recompute_index,
        recompute_index.T,
    )


def join_weights(query_weight, key_weight, value_weight, output_weight):
    depth, width = query_weight.shape

    def kernel(q_ref, k_ref, v_ref, o_ref, out_ref):
        for n, ref in enumerate((q_ref, k_ref, v_ref)):
            out_ref[:, n * width : (n + 1) * width] = ref[...]
        out_ref[:, 3 * width :] = jnp.transpose(o_ref[...].astype(f32)).astype(bf16)

    return call(
        kernel,
        "join_weights",
        shape((depth, 4 * width), bf16),
        query_weight,
        key_weight,
        value_weight,
        output_weight,
    )


def project(columns, hidden, weights, width, copies):
    rows = hidden.shape[0]
    count, depth, _ = weights[0].shape

    def kernel(c_ref, x_ref, *refs):
        weight_refs, (raw_ref, squares_ref) = refs[:-2], refs[-2:]
        raw = jnp.zeros((rows, 3 * width), f32)
        for m in range(len(weight_refs) * count):
            at = pl.multiple_of(c_ref[m] * depth, depth)
            raw = raw + jnp.dot(
                x_ref[:, pl.ds(at, depth)],
                weight_refs[m // count][m % count, :, : 3 * width],
                preferred_element_type=f32,
            )
        raw_ref[...] = raw
        query, key = raw[:, :width], raw[:, width : 2 * width]
        lane = lax.broadcasted_iota(jnp.int32, (rows, width), 1)
        sums = jnp.where(lane == 0, jnp.sum(query * query, axis=1, keepdims=True), 0.0)
        sums = jnp.where(lane == 1, jnp.sum(key * key, axis=1, keepdims=True), sums)
        sums = jnp.transpose(sums)[:8]
        for b in range(copies):
            squares_ref[b] = sums

    return call(
        kernel,
        "project",
        (shape((rows, 3 * width), f32), shape((copies, 8, rows), f32)),
        columns,
        hidden,
        *weights,
    )


def turn_by(x, cosine, sine):
    return x * cosine + pltpu.roll(x, HD // 2, 1) * sine


def finish_rows(raw, squares, query_gain, key_gain, cosine, sine, model):
    rows = raw.shape[0]
    width = query_gain.shape[1]
    copies = squares.shape[0]

    def kernel(raw_ref, s_ref, gq_ref, gk_ref, c_ref, t_ref, q_ref, k_ref, v_ref, new_ref):
        sums = s_ref[0]
        for b in range(1, copies):
            sums = sums + s_ref[b]
        sums = jnp.concatenate([sums, jnp.zeros((width - 8, rows), f32)], axis=0)
        scale = lax.rsqrt(jnp.transpose(sums) / model + EPSILON)
        raw = raw_ref[...]
        query = raw[:, :width] * scale[:, 0:1] * gq_ref[...]
        key = raw[:, width : 2 * width] * scale[:, 1:2] * gk_ref[...]
        query = turn_by(query, c_ref[...], t_ref[...]).astype(bf16)
        key = turn_by(key, c_ref[...], t_ref[...]).astype(bf16)
        value = raw[:, 2 * width :].astype(bf16)
        for z in range(NZH):
            q_ref[z] = query
        k_ref[...] = key
        v_ref[...] = value
        new_ref[:TOKN_DEV, :] = key[SEL:]
        new_ref[TOKN_DEV:, :] = value[SEL:]

    return call(
        kernel,
        "finish_rows",
        (
            shape((NZH, rows, width), bf16),
            shape((rows, width), bf16),
            shape((rows, width), bf16),
            shape((2 * TOKN_DEV, width), bf16),
        ),
        raw,
        squares,
        query_gain,
        key_gain,
        cosine,
        sine,
    )


def blend(picked, cosine, sine, keys, values, new_keys, new_values):
    _, length, width = keys.shape
    steps = 4
    chunk = length // steps

    def kernel(p_ref, c_ref, t_ref, k_ref, v_ref, nk_ref, nv_ref, bk_ref, bv_ref):
        at = lax.broadcasted_iota(jnp.int32, (chunk, width), 0) + pl.program_id(0) * chunk
        hit = (at == p_ref[...]).astype(f32)
        here = jnp.max(hit, axis=1, keepdims=True) > 0.0
        hit = hit.astype(bf16)
        turned = turn_by(k_ref[0].astype(f32), c_ref[...], t_ref[...])
        placed = jnp.dot(hit, nk_ref[...], preferred_element_type=f32)
        bk_ref[0] = jnp.where(here, placed, turned).astype(bf16)
        placed = jnp.dot(hit, nv_ref[...], preferred_element_type=f32)
        bv_ref[0] = jnp.where(here, placed, v_ref[0].astype(f32)).astype(bf16)

    tile = pl.BlockSpec((1, chunk, width), lambda k: (0, k, 0))
    return pl.pallas_call(
        kernel,
        grid=(steps,),
        out_shape=(shape(keys.shape, bf16), shape(keys.shape, bf16)),
        in_specs=[
            whole(picked),
            whole(cosine),
            whole(sine),
            tile,
            tile,
            whole(new_keys),
            whole(new_values),
        ],
        out_specs=(tile, tile),
        compiler_params=pltpu.CompilerParams(vmem_limit_bytes=8 << 20),
        name="blend",
    )(picked, cosine, sine, keys, values, new_keys, new_values)


def attend(control, queries, keys, values, wanted_at, own, new_mine, new_other, new_at, new_key_at):
    width = keys.shape[2]
    length = keys.shape[1]
    cuts = [(0, SEL), (0, SEL), (SEL, ROW_DEV), (SEL, ROW_DEV)]
    count = sum(high - low for low, high in cuts)
    back = count - SEL
    step = 32

    def kernel(
        c_ref, q_ref, k_ref, v_ref, w_ref, own_ref, nm_ref, no_ref, na_ref, nk_ref,
        back_ref, kept_ref, new_ref, rows_ref, level_ref,
    ):
        at = 0
        for i, (low, high) in enumerate(cuts):
            rows_ref[at : at + high - low, :] = q_ref[c_ref[i], low:high, :]
            at += high - low
        key_at = c_ref[4] + lax.broadcasted_iota(jnp.int32, (step, length), 1)
        for n in range(count // step):
            span = slice(n * step, (n + 1) * step)
            out, level = partial_attention(
                rows_ref[span, :], k_ref[0], v_ref[0], key_at <= w_ref[span, :]
            )
            level = jnp.broadcast_to(level, (step, width))
            if n * step < 2 * SEL:
                kept_ref[span, :width] = out
                kept_ref[span, width:] = level
            if n * step >= SEL:
                to = slice(n * step - SEL, (n + 1) * step - SEL)
                level_ref[to, :] = level
                for z in range(NZH):
                    back_ref[z, to, :] = out.astype(bf16)
        level_ref[back:, :] = jnp.zeros((2 * width - back, width), f32)
        lines = [jnp.transpose(level_ref[i * width : (i + 1) * width, :])[:1] for i in range(2)]
        lines = [piece for line in lines for piece in pieces_of(line)]
        lines.append(jnp.zeros((LEVEL_ROWS - len(lines), width), f32))
        lines = jnp.concatenate(lines, axis=0).astype(bf16)
        for z in range(NZH):
            back_ref[z, back:, :] = lines
        new_keys = jnp.concatenate([nm_ref[:TOKN_DEV, :], no_ref[:TOKN_DEV, :]], axis=0)
        new_values = jnp.concatenate([nm_ref[TOKN_DEV:, :], no_ref[TOKN_DEV:, :]], axis=0)
        out, level = partial_attention(
            own_ref[0, SEL:, :], new_keys, new_values, nk_ref[...] <= na_ref[...]
        )
        new_ref[:, :width] = out
        new_ref[:, width:] = jnp.broadcast_to(level, (TOKN_DEV, width))

    return call(
        kernel,
        "attend",
        (
            shape((NZH, back + LEVEL_ROWS, width), bf16),
            shape((2 * SEL, 2 * width), f32),
            shape((TOKN_DEV, 2 * width), f32),
        ),
        control,
        queries,
        keys,
        values,
        wanted_at,
        own,
        new_mine,
        new_other,
        new_at,
        new_key_at,
        scratch=[pltpu.VMEM((count, width), bf16), pltpu.VMEM((2 * width, width), f32)],
    )


def merge_and_project(control, kept, new_part, returned, weights):
    width = new_part.shape[1] // 2
    count, part, _ = weights[0].shape
    halves = part // width
    blocks = len(weights) * count * halves
    back = returned.shape[1] - LEVEL_ROWS

    def kernel(c_ref, kept_ref, new_ref, back_ref, *refs):
        weight_refs, (out_ref, att_ref) = refs[:-2], refs[-2:]
        def levels(source):
            lines = back_ref[source, back:, :].astype(f32)
            lines = jnp.concatenate([lines, jnp.zeros((width - LEVEL_ROWS, width), f32)], axis=0)
            lines = jnp.transpose(lines)
            return [
                lines[:, n : n + 1] + lines[:, n + 1 : n + 2] + lines[:, n + 2 : n + 3]
                for n in (0, 3)
            ]

        first = c_ref[4] == 1
        kept = jnp.where(first, kept_ref[:SEL, :], kept_ref[SEL:, :])
        remote = back_ref[c_ref[0], :SEL, :].astype(f32)
        remote_level = jnp.where(first, MASKED, levels(c_ref[0])[0][:SEL])
        att_ref[:SEL, :] = merge(
            [(kept[:, :width], kept[:, width : width + 1]), (remote, remote_level)]
        )
        at = pl.multiple_of(SEL + c_ref[3] * TOKN_DEV, TOKN_DEV)
        parts = [(new_ref[:, :width], new_ref[:, width : width + 1])]
        for i in range(PPR):
            column = levels(c_ref[1 + i])
            level = jnp.where(c_ref[3] == 0, column[0][SEL:], column[1][:TOKN_DEV])
            parts.append((back_ref[c_ref[1 + i], pl.ds(at, TOKN_DEV), :].astype(f32), level))
        att_ref[SEL:, :] = merge(parts)
        attention = att_ref[...].astype(bf16)
        for j, ref in enumerate(weight_refs):
            for n in range(count):
                term = lax.dot_general(
                    attention,
                    ref[n, :, 3 * width :],
                    (((1,), (1,)), ((), ())),
                    preferred_element_type=f32,
                ).astype(bf16)
                for h in range(halves):
                    out_ref[(j * count + n) * halves + h] = term[:, h * width : (h + 1) * width]

    return call(
        kernel,
        "merge_and_project",
        shape((blocks, ROW_DEV, width), bf16),
        control,
        kept,
        new_part,
        returned,
        *weights,
        scratch=[pltpu.VMEM((ROW_DEV, width), f32)],
    )


def feed_forward(columns, summed, hidden, gain, parcels, units):
    blocks, rows, part = summed.shape
    model = blocks * part
    count, _, depth = parcels[0].shape
    parts = len(parcels)
    split = depth // part
    per = rows // (NZL * NX)
    contract_last = (((1,), (1,)), ((), ()))

    def kernel(c_ref, s_ref, x_ref, g_ref, *refs):
        parcel_refs = refs[:parts]
        out_ref, mixed_ref, acc_ref = refs[parts:]
        squares = jnp.zeros((rows, part), f32)
        for b in range(blocks):
            block = s_ref[b].astype(f32)
            squares = squares + block * block
        norm = lax.rsqrt(jnp.sum(squares, axis=1, keepdims=True) / model + EPSILON)
        for m in range(parts * count):
            cols = pl.ds(pl.multiple_of(c_ref[m] * depth, depth), depth)
            summed = jnp.concatenate([s_ref[m * split + h] for h in range(split)], axis=1)
            mixed = (
                x_ref[:, cols].astype(f32) + summed.astype(f32) * norm * g_ref[:, cols]
            ).astype(bf16)
            mixed_ref[:, cols] = mixed
            product = lax.dot_general(
                parcel_refs[m // count][m % count, : 2 * units],
                mixed,
                contract_last,
                preferred_element_type=f32,
            )
            acc_ref[...] = product if m == 0 else acc_ref[...] + product
        to = lax.broadcasted_iota(jnp.int32, (rows, rows), 0)
        at = lax.broadcasted_iota(jnp.int32, (rows, rows), 1)
        source = (to // per) % NZL * (NX * per) + to // (NZL * per) * per + to % per
        move = jnp.where(at == source, 1.0, 0.0).astype(bf16)
        gate = acc_ref[:units, :]
        active = (gate / (1.0 + jnp.exp(-gate)) * acc_ref[units:, :]).astype(bf16)
        active = lax.dot_general(
            move, active, contract_last, preferred_element_type=f32
        ).astype(bf16)
        for m in range(parts * count):
            cols = pl.ds(pl.multiple_of(c_ref[m] * depth, depth), depth)
            down = parcel_refs[m // count][m % count, 2 * units : 3 * units]
            out_ref[:, cols] = jnp.dot(active, down, preferred_element_type=f32).astype(bf16)

    return call(
        kernel,
        "feed_forward",
        (shape((rows, model), bf16), shape((rows, model), bf16)),
        columns,
        summed,
        hidden,
        gain,
        *parcels,
        scratch=[pltpu.VMEM((2 * units, rows), f32)],
    )


def shards(
    hidden_states,
    query_weight,
    key_weight,
    value_weight,
    output_weight,
    query_gain,
    key_gain,
    attention_gain,
    gate_weight,
    up_weight,
    down_weight,
    feedforward_gain,
    cached_keys,
    cached_values,
    passage_order,
    separators,
    recompute_index,
    prompt_lengths,
):
    y_at, zh, core = (lax.axis_index(a) for a in SEQ)
    zl, x_at = (lax.axis_index(a) for a in BLK)
    seq = y_at * 4 + zh * 2 + core
    width = query_weight.shape[1]
    hidden_units = gate_weight.shape[1]
    model = hidden_states.shape[1]
    blocks = NX * NZL
    rows = ROW_DEV // blocks

    mine = join_weights(query_weight, key_weight, value_weight, output_weight)
    theirs = swap(mine, "zh", NZH)
    near = copies_to_all(mine, "y", NY)
    parcel = jnp.concatenate([gate_weight.T, up_weight.T, down_weight])
    parcel = jnp.pad(parcel, ((0, -parcel.shape[0] % 16), (0, 0)))

    at, wanted_at, picked, new_at, new_key_at, attend_control, merge_control, columns = tables(
        seq, passage_order, separators, prompt_lengths, recompute_index
    )
    frequency = frequencies()
    angles = at * jnp.concatenate([frequency, frequency])[None, :]
    sign = jnp.where(jnp.arange(HD) < HD // 2, -1.0, 1.0).astype(f32)
    cosine, sine = jnp.cos(angles), jnp.sin(angles) * sign
    theirs, near, cosine, sine = lax.optimization_barrier((theirs, near, cosine, sine))
    turn_cosine, turn_sine = cosine[ROW_DEV : ROW_DEV + 1], sine[ROW_DEV : ROW_DEV + 1]
    cosine, sine = cosine[:ROW_DEV], sine[:ROW_DEV]

    near_other = swap(near, "core", NCORE)
    far = copies_to_all(theirs, "y", NY)
    far, near_parcel = lax.optimization_barrier((far, parcel))
    parcel_near = lax.all_gather(near_parcel, "y")
    far_other = swap(far, "core", NCORE)
    weights = [near, near_other, far, far_other]
    raw, squares = project(columns, hidden_states, weights, width, blocks)
    squares = lax.all_to_all(squares, BLK, 0, 0, tiled=True)
    squares, parcel = lax.optimization_barrier((squares, parcel))
    pair = lax.all_gather(parcel, "zh")
    query, key, value, new_mine = finish_rows(
        raw, squares, query_gain[None], key_gain[None], cosine, sine, model
    )

    queries = lax.all_to_all(query, "zh", 0, 0, tiled=True)
    queries, parcel_near = lax.optimization_barrier((queries, parcel_near))
    queries = copies_to_all(queries, "y", NY)
    queries = copies_to_all(queries, "core", NCORE).reshape(N_SEQ, ROW_DEV, width)
    new_other = swap(new_mine, "core", NCORE)
    blended_keys, blended_values = blend(
        picked, turn_cosine, turn_sine, cached_keys, cached_values, key, value
    )
    returned, kept, new_part = attend(
        attend_control,
        queries,
        blended_keys,
        blended_values,
        wanted_at,
        query,
        new_mine,
        new_other,
        new_at,
        new_key_at,
    )

    returned = lax.all_to_all(returned, "zh", 0, 0, tiled=True)
    returned = copies_to_all(returned, "y", NY)
    returned = copies_to_all(returned, "core", NCORE).reshape(N_SEQ, -1, width)

    terms = merge_and_project(merge_control, kept, new_part, returned, weights)
    terms, pair = lax.optimization_barrier((terms, pair))
    parcel_far = lax.all_gather(lax.dynamic_index_in_dim(pair, 1 - zh, 0, False), "y")
    terms = lax.all_to_all(terms.reshape(NX, NZL, ROW_DEV, width), "x", 0, 0, tiled=True)
    terms = jnp.sum(terms.astype(f32), axis=0).astype(bf16)
    terms = lax.all_to_all(terms, "zl", 0, 0, tiled=True)
    summed = jnp.sum(terms.astype(f32), axis=0).astype(bf16)
    summed = copies_to_all(summed, "zl", NZL)
    summed, parcel_far = lax.optimization_barrier((summed, parcel_far))
    summed = copies_to_all(summed, "x", NX).reshape(blocks, ROW_DEV, model // blocks)

    parcels = [parcel_near, swap(parcel_near, "core", NCORE)]
    parcels += [parcel_far, swap(parcel_far, "core", NCORE)]
    terms, mixed = feed_forward(
        columns, summed, hidden_states, attention_gain[None], parcels, hidden_units
    )
    terms = lax.all_to_all(terms.reshape(NX, NZL * rows, model), "x", 0, 0, tiled=True)
    terms = jnp.sum(terms.astype(f32), axis=0).astype(bf16)
    terms = lax.all_to_all(terms.reshape(NZL, rows, model), "zl", 0, 0, tiled=True)
    total = jnp.sum(terms.astype(f32), axis=0)
    norm = lax.rsqrt(jnp.mean(total * total, axis=1, keepdims=True) + EPSILON)
    my_rows = lax.dynamic_slice_in_dim(mixed, (zl * NX + x_at) * rows, rows, 0)
    hidden_out = (my_rows.astype(f32) + total * norm * feedforward_gain).astype(bf16)
    return (hidden_out, blended_keys, blended_values)


def solution(mesh):
    fine = Mesh(
        mesh.devices.reshape(NY, NZH, NCORE, NZL, NX), ("y", "zh", "core", "zl", "x")
    )
    by_both = P(SEQ, BLK)
    return jax.shard_map(
        shards,
        mesh=fine,
        in_specs=(
            P(SEQ, None),
            by_both,
            by_both,
            by_both,
            P(BLK, SEQ),
            P(BLK),
            P(BLK),
            P(),
            by_both,
            by_both,
            P(BLK, SEQ),
            P(),
            P(SEQ, None, BLK),
            P(SEQ, None, BLK),
            P(),
            P(),
            P(),
            P(),
        ),
        out_specs=(P(SEQ + BLK, None), P(SEQ, None, BLK), P(SEQ, None, BLK)),
        check_vma=False,
    )
```

```python
import functools
import math

import jax
import jax.numpy as jnp
from jax import lax
from jax.experimental import pallas as pl
from jax.experimental.pallas import tpu as pltpu
from jax.sharding import Mesh, PartitionSpec as P

HD = 128
PLEN = 1024
SEL = 96
PPR = 2
TOKN_DEV = 32
ROW_DEV = 128
LEVEL_ROWS = 16

EPSILON = 1e-06
ROPE_THETA = 500000.0
MASKED = -1e30

SEQ = ("y", "zh", "core")
BLK = ("zl", "x")
NY, NZH, NCORE, NZL, NX = 4, 2, 2, 8, 4
N_SEQ = NY * NZH * NCORE
bf16 = jnp.bfloat16
f32 = jnp.float32


def frequencies():
    indices = jnp.arange(HD // 2, dtype=f32)
    return jnp.exp(indices * (-2.0 * math.log(ROPE_THETA) / HD))


def copies_to_all(a, axis, count):
    return lax.all_to_all(
        jnp.broadcast_to(a[None], (count,) + a.shape), axis, 0, 0, tiled=True
    )


def gather_seq(a):
    a = copies_to_all(a, "zh", NZH)
    a = copies_to_all(a, "y", NY)
    a = copies_to_all(a, "core", NCORE)
    return a.reshape((N_SEQ,) + a.shape[3:])


def swap(a, axis, count):
    return lax.ppermute(a, axis, [(i, i ^ 1) for i in range(count)])


def partial_attention(queries, keys, values, visible):
    scores = lax.dot_general(
        queries, keys, (((1,), (1,)), ((), ())), preferred_element_type=f32
    ) * HD ** (-0.5)
    scores = jnp.where(visible, scores, MASKED)
    peak = jnp.max(scores, axis=1, keepdims=True)
    weights = jnp.where(visible, jnp.exp(scores - peak), 0.0)
    total = jnp.sum(weights, axis=1, keepdims=True)
    some = total > 0.0
    safe = jnp.where(some, total, 1.0)
    out = jnp.dot(weights.astype(bf16), values, preferred_element_type=f32) / safe
    return out, jnp.where(some, peak + jnp.log(safe), MASKED)


def merge(parts):
    top = parts[0][1]
    for _, level in parts[1:]:
        top = jnp.maximum(top, level)
    num = 0.0
    den = 0.0
    for out, level in parts:
        w = jnp.exp(level - top)
        num = num + w * out
        den = den + w
    return num / den


def pieces_of(level):
    high = level.astype(bf16).astype(f32)
    mid = (level - high).astype(bf16).astype(f32)
    return high, mid, level - high - mid


def whole(a):
    return pl.BlockSpec(a.shape, lambda *k: (0,) * len(a.shape))


SMEM = pl.BlockSpec(memory_space=pltpu.SMEM)
VMEM = pl.BlockSpec(memory_space=pltpu.VMEM)


def call(kernel, name, out_shape, *args, scratch=(), limit=16):
    small = [a.ndim == 1 for a in args]
    return pl.pallas_call(
        kernel,
        out_shape=out_shape,
        in_specs=[SMEM if one else VMEM for one in small],
        out_specs=jax.tree.map(lambda a: SMEM if len(a.shape) == 1 else VMEM, out_shape),
        scratch_shapes=list(scratch),
        compiler_params=pltpu.CompilerParams(vmem_limit_bytes=limit << 20),
        name=name,
    )(*args)


def shape(dims, dtype):
    return jax.ShapeDtypeStruct(dims, dtype)


def tables(seq, passage_order, separators, prompt_lengths, recompute_index):
    spare = 8

    def kernel(
        s_ref, o_ref, sep_ref, len_ref, i_ref, t_ref,
        at_ref, wanted_ref, picked_ref, new_ref, new_key_ref, attend_ref, merge_ref, column_ref,
    ):
        seq = s_ref[0]
        place = jnp.int32(0)
        for n in range(N_SEQ):
            place = jnp.where(o_ref[n] == seq, n, place)

        def start_of(request, slot):
            first = sep_ref[2 * request]
            return first + jnp.where(slot == 1, PLEN + sep_ref[2 * request + 1], 0)

        request, mine = place >> 1, seq >> 1
        chosen = [o_ref[2 * request + i] for i in range(PPR)]
        start = start_of(request, place & 1)
        base = start_of(request, 1) + PLEN
        my_base = start_of(mine, 1) + PLEN
        my_from = (seq & 1) * TOKN_DEV

        lane = lax.broadcasted_iota(jnp.int32, (SEL, N_SEQ), 1)
        index = t_ref[...].astype(f32)

        def column(passage):
            return jnp.sum(jnp.where(lane == passage, index, 0.0), axis=1, keepdims=True)

        count = PPR * TOKN_DEV
        down = lax.broadcasted_iota(jnp.int32, (count, 1), 0)
        at_ref[:SEL, :] = column(seq) + start.astype(f32)
        at_ref[SEL:ROW_DEV, :] = (my_base + my_from + down[:TOKN_DEV]).astype(f32)
        at_ref[ROW_DEV:, :] = jnp.full((spare, 1), start, jnp.int32).astype(f32)
        for i in range(PPR):
            at = column(chosen[i]) + start_of(request, i).astype(f32)
            wanted_ref[i * SEL : (i + 1) * SEL, :] = at.astype(jnp.int32)
        wanted_ref[PPR * SEL :, :] = base + down
        picked_ref[...] = jnp.full((1, HD), -1, jnp.int32)
        picked_ref[:, :SEL] = i_ref[pl.ds(seq, 1), :]
        new_ref[...] = my_base + my_from + down[:TOKN_DEV]
        across = lax.broadcasted_iota(jnp.int32, (1, count), 1)
        token = across ^ my_from
        new_key_ref[...] = jnp.where(token < len_ref[mine], my_base + token, 1 << 30)

        def slot(s):
            return (s & 1) * 8 + (s >> 2) * 2 + ((s >> 1) & 1)

        attend_ref[0] = slot(chosen[0])
        attend_ref[1] = slot(chosen[1])
        attend_ref[2] = slot(2 * request)
        attend_ref[3] = slot(2 * request + 1)
        attend_ref[4] = start
        merge_ref[0] = slot(chosen[0])
        merge_ref[1] = slot(o_ref[2 * mine])
        merge_ref[2] = slot(o_ref[2 * mine + 1])
        merge_ref[3] = seq & 1
        merge_ref[4] = jnp.where(chosen[0] == seq, 1, 0)
        for m in range(N_SEQ):
            other = (m // 8) * 2 + m // 4 % 2
            column_ref[m] = m % 4 * 4 + ((seq & 3) ^ other)

    i32 = jnp.int32
    return call(
        kernel,
        "tables",
        (
            shape((ROW_DEV + spare, 1), f32),
            shape((PPR * (SEL + TOKN_DEV), 1), i32),
            shape((1, HD), i32),
            shape((TOKN_DEV, 1), i32),
            shape((1, PPR * TOKN_DEV), i32),
            shape((5,), i32),
            shape((5,), i32),
            shape((N_SEQ,), i32),
        ),
        seq[None],
        passage_order,
        separators.reshape(-1),
        prompt_lengths,
        recompute_index,
        recompute_index.T,
    )


def join_weights(query_weight, key_weight, value_weight, output_weight):
    depth, width = query_weight.shape

    def kernel(q_ref, k_ref, v_ref, o_ref, out_ref):
        for n, ref in enumerate((q_ref, k_ref, v_ref)):
            out_ref[:, n * width : (n + 1) * width] = ref[...]
        out_ref[:, 3 * width :] = jnp.transpose(o_ref[...].astype(f32)).astype(bf16)

    return call(
        kernel,
        "join_weights",
        shape((depth, 4 * width), bf16),
        query_weight,
        key_weight,
        value_weight,
        output_weight,
    )


def project(columns, hidden, weights, width, copies):
    rows = hidden.shape[0]
    count, depth, _ = weights[0].shape

    def kernel(c_ref, x_ref, *refs):
        weight_refs, (raw_ref, squares_ref) = refs[:-2], refs[-2:]
        raw = jnp.zeros((rows, 3 * width), f32)
        for m in range(len(weight_refs) * count):
            at = pl.multiple_of(c_ref[m] * depth, depth)
            raw = raw + jnp.dot(
                x_ref[:, pl.ds(at, depth)],
                weight_refs[m // count][m % count, :, : 3 * width],
                preferred_element_type=f32,
            )
        raw_ref[...] = raw
        query, key = raw[:, :width], raw[:, width : 2 * width]
        lane = lax.broadcasted_iota(jnp.int32, (rows, width), 1)
        sums = jnp.where(lane == 0, jnp.sum(query * query, axis=1, keepdims=True), 0.0)
        sums = jnp.where(lane == 1, jnp.sum(key * key, axis=1, keepdims=True), sums)
        sums = jnp.transpose(sums)[:8]
        for b in range(copies):
            squares_ref[b] = sums

    return call(
        kernel,
        "project",
        (shape((rows, 3 * width), f32), shape((copies, 8, rows), f32)),
        columns,
        hidden,
        *weights,
    )


def turn_by(x, cosine, sine):
    return x * cosine + pltpu.roll(x, HD // 2, 1) * sine


def finish_rows(raw, squares, query_gain, key_gain, cosine, sine, model):
    rows = raw.shape[0]
    width = query_gain.shape[1]
    copies = squares.shape[0]

    def kernel(raw_ref, s_ref, gq_ref, gk_ref, c_ref, t_ref, q_ref, k_ref, v_ref, new_ref):
        sums = s_ref[0]
        for b in range(1, copies):
            sums = sums + s_ref[b]
        sums = jnp.concatenate([sums, jnp.zeros((width - 8, rows), f32)], axis=0)
        scale = lax.rsqrt(jnp.transpose(sums) / model + EPSILON)
        raw = raw_ref[...]
        query = raw[:, :width] * scale[:, 0:1] * gq_ref[...]
        key = raw[:, width : 2 * width] * scale[:, 1:2] * gk_ref[...]
        query = turn_by(query, c_ref[:ROW_DEV, :], t_ref[:ROW_DEV, :]).astype(bf16)
        key = turn_by(key, c_ref[:ROW_DEV, :], t_ref[:ROW_DEV, :]).astype(bf16)
        value = raw[:, 2 * width :].astype(bf16)
        for z in range(NZH):
            q_ref[z] = query
        k_ref[...] = key
        v_ref[...] = value
        new_ref[:TOKN_DEV, :] = key[SEL:]
        new_ref[TOKN_DEV:, :] = value[SEL:]

    return call(
        kernel,
        "finish_rows",
        (
            shape((NZH, rows, width), bf16),
            shape((rows, width), bf16),
            shape((rows, width), bf16),
            shape((2 * TOKN_DEV, width), bf16),
        ),
        raw,
        squares,
        query_gain,
        key_gain,
        cosine,
        sine,
    )


def blend(picked, cosine, sine, keys, values, new_keys, new_values):
    _, length, width = keys.shape
    steps = 4
    chunk = length // steps

    def kernel(p_ref, c_ref, t_ref, k_ref, v_ref, nk_ref, nv_ref, bk_ref, bv_ref):
        at = lax.broadcasted_iota(jnp.int32, (chunk, width), 0) + pl.program_id(0) * chunk
        hit = (at == p_ref[...]).astype(f32)
        here = jnp.max(hit, axis=1, keepdims=True) > 0.0
        hit = hit.astype(bf16)
        turn = slice(ROW_DEV, ROW_DEV + 1)
        turned = turn_by(k_ref[0].astype(f32), c_ref[turn, :], t_ref[turn, :])
        placed = jnp.dot(hit, nk_ref[...], preferred_element_type=f32)
        bk_ref[0] = jnp.where(here, placed, turned).astype(bf16)
        placed = jnp.dot(hit, nv_ref[...], preferred_element_type=f32)
        bv_ref[0] = jnp.where(here, placed, v_ref[0].astype(f32)).astype(bf16)

    tile = pl.BlockSpec((1, chunk, width), lambda k: (0, k, 0))
    return pl.pallas_call(
        kernel,
        grid=(steps,),
        out_shape=(shape(keys.shape, bf16), shape(keys.shape, bf16)),
        in_specs=[
            whole(picked),
            whole(cosine),
            whole(sine),
            tile,
            tile,
            whole(new_keys),
            whole(new_values),
        ],
        out_specs=(tile, tile),
        compiler_params=pltpu.CompilerParams(vmem_limit_bytes=8 << 20),
        name="blend",
    )(picked, cosine, sine, keys, values, new_keys, new_values)


def attend(control, queries, keys, values, wanted_at, own, new_mine, new_other, new_at, new_key_at):
    width = keys.shape[2]
    length = keys.shape[1]
    cuts = [(0, SEL), (0, SEL), (SEL, ROW_DEV), (SEL, ROW_DEV)]
    count = sum(high - low for low, high in cuts)
    back = count - SEL
    step = 32

    def kernel(
        c_ref, q_ref, k_ref, v_ref, w_ref, own_ref, nm_ref, no_ref, na_ref, nk_ref,
        back_ref, kept_ref, new_ref, rows_ref, level_ref,
    ):
        at = 0
        for i, (low, high) in enumerate(cuts):
            rows_ref[at : at + high - low, :] = q_ref[c_ref[i], low:high, :]
            at += high - low
        key_at = c_ref[4] + lax.broadcasted_iota(jnp.int32, (step, length), 1)
        for n in range(count // step):
            span = slice(n * step, (n + 1) * step)
            out, level = partial_attention(
                rows_ref[span, :], k_ref[0], v_ref[0], key_at <= w_ref[span, :]
            )
            level = jnp.broadcast_to(level, (step, width))
            if n * step < 2 * SEL:
                kept_ref[span, :width] = out
                kept_ref[span, width:] = level
            if n * step >= SEL:
                to = slice(n * step - SEL, (n + 1) * step - SEL)
                level_ref[to, :] = level
                for z in range(NZH):
                    back_ref[z, to, :] = out.astype(bf16)
        level_ref[back:, :] = jnp.zeros((2 * width - back, width), f32)
        lines = [jnp.transpose(level_ref[i * width : (i + 1) * width, :])[:1] for i in range(2)]
        lines = [piece for line in lines for piece in pieces_of(line)]
        lines.append(jnp.zeros((LEVEL_ROWS - len(lines), width), f32))
        lines = jnp.concatenate(lines, axis=0).astype(bf16)
        for z in range(NZH):
            back_ref[z, back:, :] = lines
        new_keys = jnp.concatenate([nm_ref[:TOKN_DEV, :], no_ref[:TOKN_DEV, :]], axis=0)
        new_values = jnp.concatenate([nm_ref[TOKN_DEV:, :], no_ref[TOKN_DEV:, :]], axis=0)
        out, level = partial_attention(
            own_ref[0, SEL:, :], new_keys, new_values, nk_ref[...] <= na_ref[...]
        )
        new_ref[:, :width] = out
        new_ref[:, width:] = jnp.broadcast_to(level, (TOKN_DEV, width))

    return call(
        kernel,
        "attend",
        (
            shape((NZH, back + LEVEL_ROWS, width), bf16),
            shape((2 * SEL, 2 * width), f32),
            shape((TOKN_DEV, 2 * width), f32),
        ),
        control,
        queries,
        keys,
        values,
        wanted_at,
        own,
        new_mine,
        new_other,
        new_at,
        new_key_at,
        scratch=[pltpu.VMEM((count, width), bf16), pltpu.VMEM((2 * width, width), f32)],
    )


def merge_and_project(control, kept, new_part, returned, weights):
    width = new_part.shape[1] // 2
    count, part, _ = weights[0].shape
    halves = part // width
    blocks = len(weights) * count * halves
    back = returned.shape[1] - LEVEL_ROWS

    def kernel(c_ref, kept_ref, new_ref, back_ref, *refs):
        weight_refs, (out_ref, att_ref) = refs[:-2], refs[-2:]
        def levels(source):
            lines = back_ref[source, back:, :].astype(f32)
            lines = jnp.concatenate([lines, jnp.zeros((width - LEVEL_ROWS, width), f32)], axis=0)
            lines = jnp.transpose(lines)
            return [
                lines[:, n : n + 1] + lines[:, n + 1 : n + 2] + lines[:, n + 2 : n + 3]
                for n in (0, 3)
            ]

        first = c_ref[4] == 1
        kept = jnp.where(first, kept_ref[:SEL, :], kept_ref[SEL:, :])
        remote = back_ref[c_ref[0], :SEL, :].astype(f32)
        remote_level = jnp.where(first, MASKED, levels(c_ref[0])[0][:SEL])
        att_ref[:SEL, :] = merge(
            [(kept[:, :width], kept[:, width : width + 1]), (remote, remote_level)]
        )
        at = pl.multiple_of(SEL + c_ref[3] * TOKN_DEV, TOKN_DEV)
        parts = [(new_ref[:, :width], new_ref[:, width : width + 1])]
        for i in range(PPR):
            column = levels(c_ref[1 + i])
            level = jnp.where(c_ref[3] == 0, column[0][SEL:], column[1][:TOKN_DEV])
            parts.append((back_ref[c_ref[1 + i], pl.ds(at, TOKN_DEV), :].astype(f32), level))
        att_ref[SEL:, :] = merge(parts)
        attention = att_ref[...].astype(bf16)
        for j, ref in enumerate(weight_refs):
            for n in range(count):
                term = lax.dot_general(
                    attention,
                    ref[n, :, 3 * width :],
                    (((1,), (1,)), ((), ())),
                    preferred_element_type=f32,
                ).astype(bf16)
                for h in range(halves):
                    out_ref[(j * count + n) * halves + h] = term[:, h * width : (h + 1) * width]

    return call(
        kernel,
        "merge_and_project",
        shape((blocks, ROW_DEV, width), bf16),
        control,
        kept,
        new_part,
        returned,
        *weights,
        scratch=[pltpu.VMEM((ROW_DEV, width), f32)],
    )


def feed_forward(columns, summed, hidden, gain, parcels, units):
    blocks, rows, part = summed.shape
    model = blocks * part
    count, _, depth = parcels[0].shape
    parts = len(parcels)
    split = depth // part
    per = rows // (NZL * NX)
    contract_last = (((1,), (1,)), ((), ()))

    def kernel(c_ref, s_ref, x_ref, g_ref, *refs):
        parcel_refs = refs[:parts]
        out_ref, mixed_ref, acc_ref = refs[parts:]
        squares = jnp.zeros((rows, part), f32)
        for b in range(blocks):
            block = s_ref[b].astype(f32)
            squares = squares + block * block
        norm = lax.rsqrt(jnp.sum(squares, axis=1, keepdims=True) / model + EPSILON)
        for m in range(parts * count):
            cols = pl.ds(pl.multiple_of(c_ref[m] * depth, depth), depth)
            summed = jnp.concatenate([s_ref[m * split + h] for h in range(split)], axis=1)
            mixed = (
                x_ref[:, cols].astype(f32) + summed.astype(f32) * norm * g_ref[:, cols]
            ).astype(bf16)
            mixed_ref[:, cols] = mixed
            product = lax.dot_general(
                parcel_refs[m // count][m % count, : 2 * units],
                mixed,
                contract_last,
                preferred_element_type=f32,
            )
            acc_ref[...] = product if m == 0 else acc_ref[...] + product
        to = lax.broadcasted_iota(jnp.int32, (rows, rows), 0)
        at = lax.broadcasted_iota(jnp.int32, (rows, rows), 1)
        source = (to // per) % NZL * (NX * per) + to // (NZL * per) * per + to % per
        move = jnp.where(at == source, 1.0, 0.0).astype(bf16)
        gate = acc_ref[:units, :]
        active = (gate / (1.0 + jnp.exp(-gate)) * acc_ref[units:, :]).astype(bf16)
        active = lax.dot_general(
            move, active, contract_last, preferred_element_type=f32
        ).astype(bf16)
        for m in range(parts * count):
            cols = pl.ds(pl.multiple_of(c_ref[m] * depth, depth), depth)
            down = parcel_refs[m // count][m % count, 2 * units : 3 * units]
            out_ref[:, cols] = jnp.dot(active, down, preferred_element_type=f32).astype(bf16)

    return call(
        kernel,
        "feed_forward",
        (shape((rows, model), bf16), shape((rows, model), bf16)),
        columns,
        summed,
        hidden,
        gain,
        *parcels,
        scratch=[pltpu.VMEM((2 * units, rows), f32)],
    )


def shards(
    hidden_states,
    query_weight,
    key_weight,
    value_weight,
    output_weight,
    query_gain,
    key_gain,
    attention_gain,
    gate_weight,
    up_weight,
    down_weight,
    feedforward_gain,
    cached_keys,
    cached_values,
    passage_order,
    separators,
    recompute_index,
    prompt_lengths,
):
    y_at, zh, core = (lax.axis_index(a) for a in SEQ)
    zl, x_at = (lax.axis_index(a) for a in BLK)
    seq = y_at * 4 + zh * 2 + core
    width = query_weight.shape[1]
    hidden_units = gate_weight.shape[1]
    model = hidden_states.shape[1]
    blocks = NX * NZL
    rows = ROW_DEV // blocks

    mine = join_weights(query_weight, key_weight, value_weight, output_weight)
    theirs = swap(mine, "zh", NZH)
    near = copies_to_all(mine, "y", NY)
    parcel = jnp.concatenate([gate_weight.T, up_weight.T, down_weight])
    parcel = jnp.pad(parcel, ((0, -parcel.shape[0] % 16), (0, 0)))

    at, wanted_at, picked, new_at, new_key_at, attend_control, merge_control, columns = tables(
        seq, passage_order, separators, prompt_lengths, recompute_index
    )
    frequency = frequencies()
    angles = at * jnp.concatenate([frequency, frequency])[None, :]
    sign = jnp.where(jnp.arange(HD) < HD // 2, -1.0, 1.0).astype(f32)
    cosine, sine = jnp.cos(angles), jnp.sin(angles) * sign
    theirs, near, cosine, sine = lax.optimization_barrier((theirs, near, cosine, sine))

    near_other = swap(near, "core", NCORE)
    far = copies_to_all(theirs, "y", NY)
    far, near_parcel = lax.optimization_barrier((far, parcel))
    parcel_near = lax.all_gather(near_parcel, "y")
    far_other = swap(far, "core", NCORE)
    weights = [near, near_other, far, far_other]
    raw, squares = project(columns, hidden_states, weights, width, blocks)
    squares = lax.all_to_all(squares, BLK, 0, 0, tiled=True)
    squares, parcel = lax.optimization_barrier((squares, parcel))
    parcel_other = swap(parcel, "zh", NZH)
    query, key, value, new_mine = finish_rows(
        raw, squares, query_gain[None], key_gain[None], cosine, sine, model
    )

    queries = lax.all_to_all(query, "zh", 0, 0, tiled=True)
    queries, parcel_near = lax.optimization_barrier((queries, parcel_near))
    queries = copies_to_all(queries, "y", NY)
    queries = copies_to_all(queries, "core", NCORE).reshape(N_SEQ, ROW_DEV, width)
    new_other = swap(new_mine, "core", NCORE)
    blended_keys, blended_values = blend(
        picked, cosine, sine, cached_keys, cached_values, key, value
    )
    returned, kept, new_part = attend(
        attend_control,
        queries,
        blended_keys,
        blended_values,
        wanted_at,
        query,
        new_mine,
        new_other,
        new_at,
        new_key_at,
    )

    returned = lax.all_to_all(returned, "zh", 0, 0, tiled=True)
    returned = copies_to_all(returned, "y", NY)
    returned = copies_to_all(returned, "core", NCORE).reshape(N_SEQ, -1, width)

    terms = merge_and_project(merge_control, kept, new_part, returned, weights)
    terms, parcel_other = lax.optimization_barrier((terms, parcel_other))
    parcel_far = lax.all_gather(parcel_other, "y")
    terms = lax.all_to_all(terms.reshape(NX, NZL, ROW_DEV, width), "x", 0, 0, tiled=True)
    terms = jnp.sum(terms.astype(f32), axis=0).astype(bf16)
    terms = lax.all_to_all(terms, "zl", 0, 0, tiled=True)
    summed = jnp.sum(terms.astype(f32), axis=0).astype(bf16)
    summed = copies_to_all(summed, "zl", NZL)
    summed, parcel_far = lax.optimization_barrier((summed, parcel_far))
    summed = copies_to_all(summed, "x", NX).reshape(blocks, ROW_DEV, model // blocks)

    parcels = [parcel_near, swap(parcel_near, "core", NCORE)]
    parcels += [parcel_far, swap(parcel_far, "core", NCORE)]
    terms, mixed = feed_forward(
        columns, summed, hidden_states, attention_gain[None], parcels, hidden_units
    )
    terms = lax.all_to_all(terms.reshape(NX, NZL * rows, model), "x", 0, 0, tiled=True)
    terms = jnp.sum(terms.astype(f32), axis=0).astype(bf16)
    terms = lax.all_to_all(terms.reshape(NZL, rows, model), "zl", 0, 0, tiled=True)
    total = jnp.sum(terms.astype(f32), axis=0)
    norm = lax.rsqrt(jnp.mean(total * total, axis=1, keepdims=True) + EPSILON)
    my_rows = lax.dynamic_slice_in_dim(mixed, (zl * NX + x_at) * rows, rows, 0)
    hidden_out = (my_rows.astype(f32) + total * norm * feedforward_gain).astype(bf16)
    return (hidden_out, blended_keys, blended_values)


def solution(mesh):
    fine = Mesh(
        mesh.devices.reshape(NY, NZH, NCORE, NZL, NX), ("y", "zh", "core", "zl", "x")
    )
    by_both = P(SEQ, BLK)
    return jax.shard_map(
        shards,
        mesh=fine,
        in_specs=(
            P(SEQ, None),
            by_both,
            by_both,
            by_both,
            P(BLK, SEQ),
            P(BLK),
            P(BLK),
            P(),
            by_both,
            by_both,
            P(BLK, SEQ),
            P(),
            P(SEQ, None, BLK),
            P(SEQ, None, BLK),
            P(),
            P(),
            P(),
            P(),
        ),
        out_specs=(P(SEQ + BLK, None), P(SEQ, None, BLK), P(SEQ, None, BLK)),
        check_vma=False,
    )
```

```python
import functools
import math

import jax
import jax.numpy as jnp
from jax import lax
from jax.experimental import pallas as pl
from jax.experimental.pallas import tpu as pltpu
from jax.sharding import Mesh, PartitionSpec as P

HD = 128
PLEN = 1024
SEL = 96
PPR = 2
TOKN_DEV = 32
ROW_DEV = 128
LEVEL_ROWS = 16

EPSILON = 1e-06
ROPE_THETA = 500000.0
MASKED = -1e30

SEQ = ("y", "zh", "core")
BLK = ("zl", "x")
NY, NZH, NCORE, NZL, NX = 4, 2, 2, 8, 4
N_SEQ = NY * NZH * NCORE
bf16 = jnp.bfloat16
f32 = jnp.float32


def frequencies():
    indices = jnp.arange(HD // 2, dtype=f32)
    return jnp.exp(indices * (-2.0 * math.log(ROPE_THETA) / HD))


def copies_to_all(a, axis, count):
    return lax.all_to_all(
        jnp.broadcast_to(a[None], (count,) + a.shape), axis, 0, 0, tiled=True
    )


def gather_seq(a):
    a = copies_to_all(a, "zh", NZH)
    a = copies_to_all(a, "y", NY)
    a = copies_to_all(a, "core", NCORE)
    return a.reshape((N_SEQ,) + a.shape[3:])


def swap(a, axis, count):
    return lax.ppermute(a, axis, [(i, i ^ 1) for i in range(count)])


def partial_attention(queries, keys, values, visible):
    scores = lax.dot_general(
        queries, keys, (((1,), (1,)), ((), ())), preferred_element_type=f32
    ) * HD ** (-0.5)
    scores = jnp.where(visible, scores, MASKED)
    peak = jnp.max(scores, axis=1, keepdims=True)
    weights = jnp.where(visible, jnp.exp(scores - peak), 0.0)
    total = jnp.sum(weights, axis=1, keepdims=True)
    some = total > 0.0
    safe = jnp.where(some, total, 1.0)
    out = jnp.dot(weights.astype(bf16), values, preferred_element_type=f32) / safe
    return out, jnp.where(some, peak + jnp.log(safe), MASKED)


def merge(parts):
    top = parts[0][1]
    for _, level in parts[1:]:
        top = jnp.maximum(top, level)
    num = 0.0
    den = 0.0
    for out, level in parts:
        w = jnp.exp(level - top)
        num = num + w * out
        den = den + w
    return num / den


def pieces_of(level):
    high = level.astype(bf16).astype(f32)
    mid = (level - high).astype(bf16).astype(f32)
    return high, mid, level - high - mid


def whole(a):
    return pl.BlockSpec(a.shape, lambda *k: (0,) * len(a.shape))


SMEM = pl.BlockSpec(memory_space=pltpu.SMEM)
VMEM = pl.BlockSpec(memory_space=pltpu.VMEM)


def call(kernel, name, out_shape, *args, scratch=(), limit=16):
    small = [a.ndim == 1 for a in args]
    return pl.pallas_call(
        kernel,
        out_shape=out_shape,
        in_specs=[SMEM if one else VMEM for one in small],
        out_specs=jax.tree.map(lambda a: SMEM if len(a.shape) == 1 else VMEM, out_shape),
        scratch_shapes=list(scratch),
        compiler_params=pltpu.CompilerParams(vmem_limit_bytes=limit << 20),
        name=name,
    )(*args)


def shape(dims, dtype):
    return jax.ShapeDtypeStruct(dims, dtype)


def tables(seq, passage_order, separators, prompt_lengths, recompute_index):
    spare = 8

    def kernel(
        s_ref, o_ref, sep_ref, len_ref, i_ref, t_ref,
        at_ref, wanted_ref, picked_ref, new_ref, new_key_ref, attend_ref, merge_ref, column_ref,
    ):
        seq = s_ref[0]
        place = jnp.int32(0)
        for n in range(N_SEQ):
            place = jnp.where(o_ref[n] == seq, n, place)

        def start_of(request, slot):
            first = sep_ref[2 * request]
            return first + jnp.where(slot == 1, PLEN + sep_ref[2 * request + 1], 0)

        request, mine = place >> 1, seq >> 1
        chosen = [o_ref[2 * request + i] for i in range(PPR)]
        start = start_of(request, place & 1)
        base = start_of(request, 1) + PLEN
        my_base = start_of(mine, 1) + PLEN
        my_from = (seq & 1) * TOKN_DEV

        lane = lax.broadcasted_iota(jnp.int32, (SEL, N_SEQ), 1)
        index = t_ref[...].astype(f32)

        def column(passage):
            return jnp.sum(jnp.where(lane == passage, index, 0.0), axis=1, keepdims=True)

        count = PPR * TOKN_DEV
        down = lax.broadcasted_iota(jnp.int32, (count, 1), 0)
        at_ref[:SEL, :] = column(seq) + start.astype(f32)
        at_ref[SEL:ROW_DEV, :] = (my_base + my_from + down[:TOKN_DEV]).astype(f32)
        at_ref[ROW_DEV:, :] = jnp.full((spare, 1), start, jnp.int32).astype(f32)
        for i in range(PPR):
            at = column(chosen[i]) + start_of(request, i).astype(f32)
            wanted_ref[i * SEL : (i + 1) * SEL, :] = at.astype(jnp.int32)
        wanted_ref[PPR * SEL :, :] = base + down
        picked_ref[...] = jnp.full((1, HD), -1, jnp.int32)
        picked_ref[:, :SEL] = i_ref[pl.ds(seq, 1), :]
        new_ref[...] = my_base + my_from + down[:TOKN_DEV]
        across = lax.broadcasted_iota(jnp.int32, (1, count), 1)
        token = across ^ my_from
        new_key_ref[...] = jnp.where(token < len_ref[mine], my_base + token, 1 << 30)

        def slot(s):
            return (s & 1) * 8 + (s >> 2) * 2 + ((s >> 1) & 1)

        attend_ref[0] = slot(chosen[0])
        attend_ref[1] = slot(chosen[1])
        attend_ref[2] = slot(2 * request)
        attend_ref[3] = slot(2 * request + 1)
        attend_ref[4] = start
        merge_ref[0] = slot(chosen[0])
        merge_ref[1] = slot(o_ref[2 * mine])
        merge_ref[2] = slot(o_ref[2 * mine + 1])
        merge_ref[3] = seq & 1
        merge_ref[4] = jnp.where(chosen[0] == seq, 1, 0)
        for m in range(N_SEQ):
            other = (m // 8) * 2 + m // 4 % 2
            column_ref[m] = m % 4 * 4 + ((seq & 3) ^ other)

    i32 = jnp.int32
    return call(
        kernel,
        "tables",
        (
            shape((ROW_DEV + spare, 1), f32),
            shape((PPR * (SEL + TOKN_DEV), 1), i32),
            shape((1, HD), i32),
            shape((TOKN_DEV, 1), i32),
            shape((1, PPR * TOKN_DEV), i32),
            shape((5,), i32),
            shape((5,), i32),
            shape((N_SEQ,), i32),
        ),
        seq[None],
        passage_order,
        separators.reshape(-1),
        prompt_lengths,
        recompute_index,
        recompute_index.T,
    )


def join_weights(query_weight, key_weight, value_weight, output_weight):
    depth, width = query_weight.shape

    def kernel(q_ref, k_ref, v_ref, o_ref, out_ref):
        for n, ref in enumerate((q_ref, k_ref, v_ref)):
            out_ref[:, n * width : (n + 1) * width] = ref[...]
        out_ref[:, 3 * width :] = jnp.transpose(o_ref[...].astype(f32)).astype(bf16)

    return call(
        kernel,
        "join_weights",
        shape((depth, 4 * width), bf16),
        query_weight,
        key_weight,
        value_weight,
        output_weight,
    )


def project(columns, hidden, weights, width, copies):
    rows = hidden.shape[0]
    count, depth, _ = weights[0].shape

    def kernel(c_ref, x_ref, *refs):
        weight_refs, (raw_ref, squares_ref) = refs[:-2], refs[-2:]
        raw = jnp.zeros((rows, 3 * width), f32)
        for m in range(len(weight_refs) * count):
            at = pl.multiple_of(c_ref[m] * depth, depth)
            raw = raw + jnp.dot(
                x_ref[:, pl.ds(at, depth)],
                weight_refs[m // count][m % count, :, : 3 * width],
                preferred_element_type=f32,
            )
        raw_ref[...] = raw
        query, key = raw[:, :width], raw[:, width : 2 * width]
        lane = lax.broadcasted_iota(jnp.int32, (rows, width), 1)
        sums = jnp.where(lane == 0, jnp.sum(query * query, axis=1, keepdims=True), 0.0)
        sums = jnp.where(lane == 1, jnp.sum(key * key, axis=1, keepdims=True), sums)
        sums = jnp.transpose(sums)[:8]
        for b in range(copies):
            squares_ref[b] = sums

    return call(
        kernel,
        "project",
        (shape((rows, 3 * width), f32), shape((copies, 8, rows), f32)),
        columns,
        hidden,
        *weights,
    )


def turn_by(x, cosine, sine):
    return x * cosine + pltpu.roll(x, HD // 2, 1) * sine


def finish_rows(raw, squares, query_gain, key_gain, cosine, sine, model):
    rows = raw.shape[0]
    width = query_gain.shape[1]
    copies = squares.shape[0]

    def kernel(raw_ref, s_ref, gq_ref, gk_ref, c_ref, t_ref, q_ref, k_ref, v_ref, new_ref):
        sums = s_ref[0]
        for b in range(1, copies):
            sums = sums + s_ref[b]
        sums = jnp.concatenate([sums, jnp.zeros((width - 8, rows), f32)], axis=0)
        scale = lax.rsqrt(jnp.transpose(sums) / model + EPSILON)
        raw = raw_ref[...]
        query = raw[:, :width] * scale[:, 0:1] * gq_ref[...]
        key = raw[:, width : 2 * width] * scale[:, 1:2] * gk_ref[...]
        query = turn_by(query, c_ref[:ROW_DEV, :], t_ref[:ROW_DEV, :]).astype(bf16)
        key = turn_by(key, c_ref[:ROW_DEV, :], t_ref[:ROW_DEV, :]).astype(bf16)
        value = raw[:, 2 * width :].astype(bf16)
        for z in range(NZH):
            q_ref[z] = query
        k_ref[...] = key
        v_ref[...] = value
        new_ref[:TOKN_DEV, :] = key[SEL:]
        new_ref[TOKN_DEV:, :] = value[SEL:]

    return call(
        kernel,
        "finish_rows",
        (
            shape((NZH, rows, width), bf16),
            shape((rows, width), bf16),
            shape((rows, width), bf16),
            shape((2 * TOKN_DEV, width), bf16),
        ),
        raw,
        squares,
        query_gain,
        key_gain,
        cosine,
        sine,
    )


def blend(picked, cosine, sine, keys, values, new_keys, new_values):
    _, length, width = keys.shape
    steps = 4
    chunk = length // steps

    def kernel(p_ref, c_ref, t_ref, k_ref, v_ref, nk_ref, nv_ref, bk_ref, bv_ref):
        at = lax.broadcasted_iota(jnp.int32, (chunk, width), 0) + pl.program_id(0) * chunk
        hit = (at == p_ref[...]).astype(f32)
        here = jnp.max(hit, axis=1, keepdims=True) > 0.0
        hit = hit.astype(bf16)
        turn = slice(ROW_DEV, ROW_DEV + 1)
        turned = turn_by(k_ref[0].astype(f32), c_ref[turn, :], t_ref[turn, :])
        placed = jnp.dot(hit, nk_ref[...], preferred_element_type=f32)
        bk_ref[0] = jnp.where(here, placed, turned).astype(bf16)
        placed = jnp.dot(hit, nv_ref[...], preferred_element_type=f32)
        bv_ref[0] = jnp.where(here, placed, v_ref[0].astype(f32)).astype(bf16)

    tile = pl.BlockSpec((1, chunk, width), lambda k: (0, k, 0))
    return pl.pallas_call(
        kernel,
        grid=(steps,),
        out_shape=(shape(keys.shape, bf16), shape(keys.shape, bf16)),
        in_specs=[
            whole(picked),
            whole(cosine),
            whole(sine),
            tile,
            tile,
            whole(new_keys),
            whole(new_values),
        ],
        out_specs=(tile, tile),
        compiler_params=pltpu.CompilerParams(vmem_limit_bytes=8 << 20),
        name="blend",
    )(picked, cosine, sine, keys, values, new_keys, new_values)


def attend(control, queries, keys, values, wanted_at, own, new_mine, new_other, new_at, new_key_at):
    width = keys.shape[2]
    length = keys.shape[1]
    cuts = [(0, SEL), (0, SEL), (SEL, ROW_DEV), (SEL, ROW_DEV)]
    count = sum(high - low for low, high in cuts)
    back = count - SEL
    step = 32

    def kernel(
        c_ref, q_ref, k_ref, v_ref, w_ref, own_ref, nm_ref, no_ref, na_ref, nk_ref,
        back_ref, kept_ref, new_ref, rows_ref, level_ref,
    ):
        at = 0
        for i, (low, high) in enumerate(cuts):
            rows_ref[at : at + high - low, :] = q_ref[c_ref[i], low:high, :]
            at += high - low
        key_at = c_ref[4] + lax.broadcasted_iota(jnp.int32, (step, length), 1)
        for n in range(count // step):
            span = slice(n * step, (n + 1) * step)
            out, level = partial_attention(
                rows_ref[span, :], k_ref[0], v_ref[0], key_at <= w_ref[span, :]
            )
            level = jnp.broadcast_to(level, (step, width))
            if n * step < 2 * SEL:
                kept_ref[span, :width] = out
                kept_ref[span, width:] = level
            if n * step >= SEL:
                to = slice(n * step - SEL, (n + 1) * step - SEL)
                level_ref[to, :] = level
                for z in range(NZH):
                    back_ref[z, to, :] = out.astype(bf16)
        level_ref[back:, :] = jnp.zeros((2 * width - back, width), f32)
        lines = [jnp.transpose(level_ref[i * width : (i + 1) * width, :])[:1] for i in range(2)]
        lines = [piece for line in lines for piece in pieces_of(line)]
        lines.append(jnp.zeros((LEVEL_ROWS - len(lines), width), f32))
        lines = jnp.concatenate(lines, axis=0).astype(bf16)
        for z in range(NZH):
            back_ref[z, back:, :] = lines
        new_keys = jnp.concatenate([nm_ref[:TOKN_DEV, :], no_ref[:TOKN_DEV, :]], axis=0)
        new_values = jnp.concatenate([nm_ref[TOKN_DEV:, :], no_ref[TOKN_DEV:, :]], axis=0)
        out, level = partial_attention(
            own_ref[0, SEL:, :], new_keys, new_values, nk_ref[...] <= na_ref[...]
        )
        new_ref[:, :width] = out
        new_ref[:, width:] = jnp.broadcast_to(level, (TOKN_DEV, width))

    return call(
        kernel,
        "attend",
        (
            shape((NZH, back + LEVEL_ROWS, width), bf16),
            shape((2 * SEL, 2 * width), f32),
            shape((TOKN_DEV, 2 * width), f32),
        ),
        control,
        queries,
        keys,
        values,
        wanted_at,
        own,
        new_mine,
        new_other,
        new_at,
        new_key_at,
        scratch=[pltpu.VMEM((count, width), bf16), pltpu.VMEM((2 * width, width), f32)],
    )


def merge_and_project(control, kept, new_part, returned, weights):
    width = new_part.shape[1] // 2
    count, part, _ = weights[0].shape
    halves = part // width
    blocks = len(weights) * count * halves
    back = returned.shape[1] - LEVEL_ROWS

    def kernel(c_ref, kept_ref, new_ref, back_ref, *refs):
        weight_refs, (out_ref, att_ref) = refs[:-2], refs[-2:]
        def levels(source):
            lines = back_ref[source, back:, :].astype(f32)
            lines = jnp.concatenate([lines, jnp.zeros((width - LEVEL_ROWS, width), f32)], axis=0)
            lines = jnp.transpose(lines)
            return [
                lines[:, n : n + 1] + lines[:, n + 1 : n + 2] + lines[:, n + 2 : n + 3]
                for n in (0, 3)
            ]

        first = c_ref[4] == 1
        kept = jnp.where(first, kept_ref[:SEL, :], kept_ref[SEL:, :])
        remote = back_ref[c_ref[0], :SEL, :].astype(f32)
        remote_level = jnp.where(first, MASKED, levels(c_ref[0])[0][:SEL])
        att_ref[:SEL, :] = merge(
            [(kept[:, :width], kept[:, width : width + 1]), (remote, remote_level)]
        )
        at = pl.multiple_of(SEL + c_ref[3] * TOKN_DEV, TOKN_DEV)
        parts = [(new_ref[:, :width], new_ref[:, width : width + 1])]
        for i in range(PPR):
            column = levels(c_ref[1 + i])
            level = jnp.where(c_ref[3] == 0, column[0][SEL:], column[1][:TOKN_DEV])
            parts.append((back_ref[c_ref[1 + i], pl.ds(at, TOKN_DEV), :].astype(f32), level))
        att_ref[SEL:, :] = merge(parts)
        attention = att_ref[...].astype(bf16)
        for j, ref in enumerate(weight_refs):
            for n in range(count):
                term = lax.dot_general(
                    attention,
                    ref[n, :, 3 * width :],
                    (((1,), (1,)), ((), ())),
                    preferred_element_type=f32,
                ).astype(bf16)
                for h in range(halves):
                    out_ref[(j * count + n) * halves + h] = term[:, h * width : (h + 1) * width]

    return call(
        kernel,
        "merge_and_project",
        shape((blocks, ROW_DEV, width), bf16),
        control,
        kept,
        new_part,
        returned,
        *weights,
        scratch=[pltpu.VMEM((ROW_DEV, width), f32)],
    )


def feed_forward(columns, summed, hidden, gain, parcels, units):
    blocks, rows, part = summed.shape
    model = blocks * part
    count, _, depth = parcels[0][0].shape
    parts = len(parcels)
    split = depth // part
    per = rows // (NZL * NX)
    contract_last = (((1,), (1,)), ((), ()))

    def kernel(c_ref, s_ref, x_ref, g_ref, *refs):
        refs = list(refs)
        held = [[refs.pop(0) for _ in pieces] for pieces in parcels]
        out_ref, mixed_ref, acc_ref = refs
        squares = jnp.zeros((rows, part), f32)
        for b in range(blocks):
            block = s_ref[b].astype(f32)
            squares = squares + block * block
        norm = lax.rsqrt(jnp.sum(squares, axis=1, keepdims=True) / model + EPSILON)
        for m in range(parts * count):
            cols = pl.ds(pl.multiple_of(c_ref[m] * depth, depth), depth)
            summed = jnp.concatenate([s_ref[m * split + h] for h in range(split)], axis=1)
            mixed = (
                x_ref[:, cols].astype(f32) + summed.astype(f32) * norm * g_ref[:, cols]
            ).astype(bf16)
            mixed_ref[:, cols] = mixed
            low = 0
            for ref in held[m // count]:
                high = min(low + ref.shape[1], 2 * units)
                product = lax.dot_general(
                    ref[m % count, : high - low],
                    mixed,
                    contract_last,
                    preferred_element_type=f32,
                )
                span = slice(low, high)
                acc_ref[span, :] = product if m == 0 else acc_ref[span, :] + product
                low = high
        to = lax.broadcasted_iota(jnp.int32, (rows, rows), 0)
        at = lax.broadcasted_iota(jnp.int32, (rows, rows), 1)
        source = (to // per) % NZL * (NX * per) + to // (NZL * per) * per + to % per
        move = jnp.where(at == source, 1.0, 0.0).astype(bf16)
        gate = acc_ref[:units, :]
        active = (gate / (1.0 + jnp.exp(-gate)) * acc_ref[units:, :]).astype(bf16)
        active = lax.dot_general(
            move, active, contract_last, preferred_element_type=f32
        ).astype(bf16)
        for m in range(parts * count):
            cols = pl.ds(pl.multiple_of(c_ref[m] * depth, depth), depth)
            pieces = held[m // count]
            at_row = 2 * units - sum(ref.shape[1] for ref in pieces[:-1])
            down = pieces[-1][m % count, at_row : at_row + units]
            out_ref[:, cols] = jnp.dot(active, down, preferred_element_type=f32).astype(bf16)

    return call(
        kernel,
        "feed_forward",
        (shape((rows, model), bf16), shape((rows, model), bf16)),
        columns,
        summed,
        hidden,
        gain,
        *[piece for pieces in parcels for piece in pieces],
        scratch=[pltpu.VMEM((2 * units, rows), f32)],
    )


def shards(
    hidden_states,
    query_weight,
    key_weight,
    value_weight,
    output_weight,
    query_gain,
    key_gain,
    attention_gain,
    gate_weight,
    up_weight,
    down_weight,
    feedforward_gain,
    cached_keys,
    cached_values,
    passage_order,
    separators,
    recompute_index,
    prompt_lengths,
):
    y_at, zh, core = (lax.axis_index(a) for a in SEQ)
    zl, x_at = (lax.axis_index(a) for a in BLK)
    seq = y_at * 4 + zh * 2 + core
    width = query_weight.shape[1]
    hidden_units = gate_weight.shape[1]
    model = hidden_states.shape[1]
    blocks = NX * NZL
    rows = ROW_DEV // blocks

    mine = join_weights(query_weight, key_weight, value_weight, output_weight)
    theirs = swap(mine, "zh", NZH)
    near = copies_to_all(mine, "y", NY)
    parcel = jnp.concatenate([gate_weight.T, up_weight.T, down_weight])
    parcel = jnp.pad(parcel, ((0, -parcel.shape[0] % 16), (0, 0)))

    at, wanted_at, picked, new_at, new_key_at, attend_control, merge_control, columns = tables(
        seq, passage_order, separators, prompt_lengths, recompute_index
    )
    frequency = frequencies()
    angles = at * jnp.concatenate([frequency, frequency])[None, :]
    sign = jnp.where(jnp.arange(HD) < HD // 2, -1.0, 1.0).astype(f32)
    cosine, sine = jnp.cos(angles), jnp.sin(angles) * sign
    theirs, near, cosine, sine = lax.optimization_barrier((theirs, near, cosine, sine))

    near_other = swap(near, "core", NCORE)
    far = copies_to_all(theirs, "y", NY)
    far, near_parcel = lax.optimization_barrier((far, parcel))
    parcel_near = lax.all_gather(near_parcel, "y")
    far_other = swap(far, "core", NCORE)
    weights = [near, near_other, far, far_other]
    raw, squares = project(columns, hidden_states, weights, width, blocks)
    squares = lax.all_to_all(squares, BLK, 0, 0, tiled=True)
    squares, parcel = lax.optimization_barrier((squares, parcel))
    early, late = jnp.split(parcel, 2)
    query, key, value, new_mine = finish_rows(
        raw, squares, query_gain[None], key_gain[None], cosine, sine, model
    )

    queries = lax.all_to_all(query, "zh", 0, 0, tiled=True)
    queries, parcel_near, early = lax.optimization_barrier((queries, parcel_near, early))
    early = swap(early, "zh", NZH)
    queries = copies_to_all(queries, "y", NY)
    queries = copies_to_all(queries, "core", NCORE).reshape(N_SEQ, ROW_DEV, width)
    new_other = swap(new_mine, "core", NCORE)
    blended_keys, blended_values = blend(
        picked, cosine, sine, cached_keys, cached_values, key, value
    )
    returned, kept, new_part = attend(
        attend_control,
        queries,
        blended_keys,
        blended_values,
        wanted_at,
        query,
        new_mine,
        new_other,
        new_at,
        new_key_at,
    )

    returned, early = lax.optimization_barrier((returned, early))
    early = lax.all_gather(early, "y")
    returned = lax.all_to_all(returned, "zh", 0, 0, tiled=True)
    returned, late = lax.optimization_barrier((returned, late))
    late = swap(late, "zh", NZH)
    returned = copies_to_all(returned, "y", NY)
    returned = copies_to_all(returned, "core", NCORE).reshape(N_SEQ, -1, width)

    terms = merge_and_project(merge_control, kept, new_part, returned, weights)
    terms = lax.all_to_all(terms.reshape(NX, NZL, ROW_DEV, width), "x", 0, 0, tiled=True)
    terms, late = lax.optimization_barrier((terms, late))
    late = lax.all_gather(late, "y")
    terms = jnp.sum(terms.astype(f32), axis=0).astype(bf16)
    terms = lax.all_to_all(terms, "zl", 0, 0, tiled=True)
    summed = jnp.sum(terms.astype(f32), axis=0).astype(bf16)
    summed = copies_to_all(summed, "zl", NZL)
    summed, early, late = lax.optimization_barrier((summed, early, late))
    summed = copies_to_all(summed, "x", NX).reshape(blocks, ROW_DEV, model // blocks)

    parcels = [(parcel_near,), (swap(parcel_near, "core", NCORE),)]
    parcels += [(early, late), (swap(early, "core", NCORE), swap(late, "core", NCORE))]
    terms, mixed = feed_forward(
        columns, summed, hidden_states, attention_gain[None], parcels, hidden_units
    )
    terms = lax.all_to_all(terms.reshape(NX, NZL * rows, model), "x", 0, 0, tiled=True)
    terms = jnp.sum(terms.astype(f32), axis=0).astype(bf16)
    terms = lax.all_to_all(terms.reshape(NZL, rows, model), "zl", 0, 0, tiled=True)
    total = jnp.sum(terms.astype(f32), axis=0)
    norm = lax.rsqrt(jnp.mean(total * total, axis=1, keepdims=True) + EPSILON)
    my_rows = lax.dynamic_slice_in_dim(mixed, (zl * NX + x_at) * rows, rows, 0)
    hidden_out = (my_rows.astype(f32) + total * norm * feedforward_gain).astype(bf16)
    return (hidden_out, blended_keys, blended_values)


def solution(mesh):
    fine = Mesh(
        mesh.devices.reshape(NY, NZH, NCORE, NZL, NX), ("y", "zh", "core", "zl", "x")
    )
    by_both = P(SEQ, BLK)
    return jax.shard_map(
        shards,
        mesh=fine,
        in_specs=(
            P(SEQ, None),
            by_both,
            by_both,
            by_both,
            P(BLK, SEQ),
            P(BLK),
            P(BLK),
            P(),
            by_both,
            by_both,
            P(BLK, SEQ),
            P(),
            P(SEQ, None, BLK),
            P(SEQ, None, BLK),
            P(),
            P(),
            P(),
            P(),
        ),
        out_specs=(P(SEQ + BLK, None), P(SEQ, None, BLK), P(SEQ, None, BLK)),
        check_vma=False,
    )
```

```python
import functools
import math

import jax
import jax.numpy as jnp
from jax import lax
from jax.experimental import pallas as pl
from jax.experimental.pallas import tpu as pltpu
from jax.sharding import Mesh, PartitionSpec as P

HD = 128
PLEN = 1024
SEL = 96
PPR = 2
TOKN_DEV = 32
ROW_DEV = 128
LEVEL_ROWS = 16

EPSILON = 1e-06
ROPE_THETA = 500000.0
MASKED = -1e30

SEQ = ("y", "zh", "core")
BLK = ("zl", "x")
NY, NZH, NCORE, NZL, NX = 4, 2, 2, 8, 4
N_SEQ = NY * NZH * NCORE
bf16 = jnp.bfloat16
f32 = jnp.float32


def frequencies():
    indices = jnp.arange(HD // 2, dtype=f32)
    return jnp.exp(indices * (-2.0 * math.log(ROPE_THETA) / HD))


def copies_to_all(a, axis, count):
    return lax.all_to_all(
        jnp.broadcast_to(a[None], (count,) + a.shape), axis, 0, 0, tiled=True
    )


def gather_seq(a):
    a = copies_to_all(a, "zh", NZH)
    a = copies_to_all(a, "y", NY)
    a = copies_to_all(a, "core", NCORE)
    return a.reshape((N_SEQ,) + a.shape[3:])


def swap(a, axis, count):
    return lax.ppermute(a, axis, [(i, i ^ 1) for i in range(count)])


def partial_attention(queries, keys, values, visible):
    scores = lax.dot_general(
        queries, keys, (((1,), (1,)), ((), ())), preferred_element_type=f32
    ) * HD ** (-0.5)
    scores = jnp.where(visible, scores, MASKED)
    peak = jnp.max(scores, axis=1, keepdims=True)
    weights = jnp.where(visible, jnp.exp(scores - peak), 0.0)
    total = jnp.sum(weights, axis=1, keepdims=True)
    some = total > 0.0
    safe = jnp.where(some, total, 1.0)
    out = jnp.dot(weights.astype(bf16), values, preferred_element_type=f32) / safe
    return out, jnp.where(some, peak + jnp.log(safe), MASKED)


def merge(parts):
    top = parts[0][1]
    for _, level in parts[1:]:
        top = jnp.maximum(top, level)
    num = 0.0
    den = 0.0
    for out, level in parts:
        w = jnp.exp(level - top)
        num = num + w * out
        den = den + w
    return num / den


def pieces_of(level):
    high = level.astype(bf16).astype(f32)
    mid = (level - high).astype(bf16).astype(f32)
    return high, mid, level - high - mid


def whole(a):
    return pl.BlockSpec(a.shape, lambda *k: (0,) * len(a.shape))


SMEM = pl.BlockSpec(memory_space=pltpu.SMEM)
VMEM = pl.BlockSpec(memory_space=pltpu.VMEM)


def call(kernel, name, out_shape, *args, scratch=(), limit=16):
    small = [a.ndim == 1 for a in args]
    return pl.pallas_call(
        kernel,
        out_shape=out_shape,
        in_specs=[SMEM if one else VMEM for one in small],
        out_specs=jax.tree.map(lambda a: SMEM if len(a.shape) == 1 else VMEM, out_shape),
        scratch_shapes=list(scratch),
        compiler_params=pltpu.CompilerParams(vmem_limit_bytes=limit << 20),
        name=name,
    )(*args)


def shape(dims, dtype):
    return jax.ShapeDtypeStruct(dims, dtype)


def tables(seq, passage_order, separators, prompt_lengths, recompute_index):
    spare = 8

    def kernel(
        s_ref, o_ref, sep_ref, len_ref, i_ref, t_ref,
        at_ref, wanted_ref, picked_ref, new_ref, new_key_ref, attend_ref, merge_ref, column_ref,
    ):
        seq = s_ref[0]
        place = jnp.int32(0)
        for n in range(N_SEQ):
            place = jnp.where(o_ref[n] == seq, n, place)

        def start_of(request, slot):
            first = sep_ref[2 * request]
            return first + jnp.where(slot == 1, PLEN + sep_ref[2 * request + 1], 0)

        request, mine = place >> 1, seq >> 1
        chosen = [o_ref[2 * request + i] for i in range(PPR)]
        start = start_of(request, place & 1)
        base = start_of(request, 1) + PLEN
        my_base = start_of(mine, 1) + PLEN
        my_from = (seq & 1) * TOKN_DEV

        lane = lax.broadcasted_iota(jnp.int32, (SEL, N_SEQ), 1)
        index = t_ref[...].astype(f32)

        def column(passage):
            return jnp.sum(jnp.where(lane == passage, index, 0.0), axis=1, keepdims=True)

        count = PPR * TOKN_DEV
        down = lax.broadcasted_iota(jnp.int32, (count, 1), 0)
        at_ref[:SEL, :] = column(seq) + start.astype(f32)
        at_ref[SEL:ROW_DEV, :] = (my_base + my_from + down[:TOKN_DEV]).astype(f32)
        at_ref[ROW_DEV:, :] = jnp.full((spare, 1), start, jnp.int32).astype(f32)
        for i in range(PPR):
            at = column(chosen[i]) + start_of(request, i).astype(f32)
            wanted_ref[i * SEL : (i + 1) * SEL, :] = at.astype(jnp.int32)
        wanted_ref[PPR * SEL :, :] = base + down
        picked_ref[...] = jnp.full((1, HD), -1, jnp.int32)
        picked_ref[:, :SEL] = i_ref[pl.ds(seq, 1), :]
        new_ref[...] = my_base + my_from + down[:TOKN_DEV]
        across = lax.broadcasted_iota(jnp.int32, (1, count), 1)
        token = across ^ my_from
        new_key_ref[...] = jnp.where(token < len_ref[mine], my_base + token, 1 << 30)

        def slot(s):
            return (s & 1) * 8 + (s >> 2) * 2 + ((s >> 1) & 1)

        attend_ref[0] = slot(chosen[0])
        attend_ref[1] = slot(chosen[1])
        attend_ref[2] = slot(2 * request)
        attend_ref[3] = slot(2 * request + 1)
        attend_ref[4] = start
        merge_ref[0] = slot(chosen[0])
        merge_ref[1] = slot(o_ref[2 * mine])
        merge_ref[2] = slot(o_ref[2 * mine + 1])
        merge_ref[3] = seq & 1
        merge_ref[4] = jnp.where(chosen[0] == seq, 1, 0)
        for m in range(N_SEQ):
            other = (m // 8) * 2 + m // 4 % 2
            column_ref[m] = m % 4 * 4 + ((seq & 3) ^ other)

    i32 = jnp.int32
    return call(
        kernel,
        "tables",
        (
            shape((ROW_DEV + spare, 1), f32),
            shape((PPR * (SEL + TOKN_DEV), 1), i32),
            shape((1, HD), i32),
            shape((TOKN_DEV, 1), i32),
            shape((1, PPR * TOKN_DEV), i32),
            shape((5,), i32),
            shape((5,), i32),
            shape((N_SEQ,), i32),
        ),
        seq[None],
        passage_order,
        separators.reshape(-1),
        prompt_lengths,
        recompute_index,
        recompute_index.T,
    )


def join_weights(query_weight, key_weight, value_weight, output_weight):
    depth, width = query_weight.shape

    def kernel(q_ref, k_ref, v_ref, o_ref, out_ref):
        for n, ref in enumerate((q_ref, k_ref, v_ref)):
            out_ref[:, n * width : (n + 1) * width] = ref[...]
        out_ref[:, 3 * width :] = jnp.transpose(o_ref[...].astype(f32)).astype(bf16)

    return call(
        kernel,
        "join_weights",
        shape((depth, 4 * width), bf16),
        query_weight,
        key_weight,
        value_weight,
        output_weight,
    )


def project(columns, hidden, weights, width, copies):
    rows = hidden.shape[0]
    count, depth, _ = weights[0].shape

    def kernel(c_ref, x_ref, *refs):
        weight_refs, (raw_ref, squares_ref) = refs[:-2], refs[-2:]
        raw = jnp.zeros((rows, 3 * width), f32)
        for m in range(len(weight_refs) * count):
            at = pl.multiple_of(c_ref[m] * depth, depth)
            raw = raw + jnp.dot(
                x_ref[:, pl.ds(at, depth)],
                weight_refs[m // count][m % count, :, : 3 * width],
                preferred_element_type=f32,
            )
        raw_ref[...] = raw
        query, key = raw[:, :width], raw[:, width : 2 * width]
        lane = lax.broadcasted_iota(jnp.int32, (rows, width), 1)
        sums = jnp.where(lane == 0, jnp.sum(query * query, axis=1, keepdims=True), 0.0)
        sums = jnp.where(lane == 1, jnp.sum(key * key, axis=1, keepdims=True), sums)
        sums = jnp.transpose(sums)[:8]
        for b in range(copies):
            squares_ref[b] = sums

    return call(
        kernel,
        "project",
        (shape((rows, 3 * width), f32), shape((copies, 8, rows), f32)),
        columns,
        hidden,
        *weights,
    )


def turn_by(x, cosine, sine):
    return x * cosine + pltpu.roll(x, HD // 2, 1) * sine


def finish_rows(raw, squares, query_gain, key_gain, cosine, sine, model):
    rows = raw.shape[0]
    width = query_gain.shape[1]
    copies = squares.shape[0]

    def kernel(raw_ref, s_ref, gq_ref, gk_ref, c_ref, t_ref, q_ref, k_ref, v_ref, new_ref):
        sums = s_ref[0]
        for b in range(1, copies):
            sums = sums + s_ref[b]
        sums = jnp.concatenate([sums, jnp.zeros((width - 8, rows), f32)], axis=0)
        scale = lax.rsqrt(jnp.transpose(sums) / model + EPSILON)
        raw = raw_ref[...]
        query = raw[:, :width] * scale[:, 0:1] * gq_ref[...]
        key = raw[:, width : 2 * width] * scale[:, 1:2] * gk_ref[...]
        query = turn_by(query, c_ref[:ROW_DEV, :], t_ref[:ROW_DEV, :]).astype(bf16)
        key = turn_by(key, c_ref[:ROW_DEV, :], t_ref[:ROW_DEV, :]).astype(bf16)
        value = raw[:, 2 * width :].astype(bf16)
        for z in range(NZH):
            q_ref[z] = query
        k_ref[...] = key
        v_ref[...] = value
        new_ref[:TOKN_DEV, :] = key[SEL:]
        new_ref[TOKN_DEV:, :] = value[SEL:]

    return call(
        kernel,
        "finish_rows",
        (
            shape((NZH, rows, width), bf16),
            shape((rows, width), bf16),
            shape((rows, width), bf16),
            shape((2 * TOKN_DEV, width), bf16),
        ),
        raw,
        squares,
        query_gain,
        key_gain,
        cosine,
        sine,
    )


def blend(picked, cosine, sine, keys, values, new_keys, new_values):
    _, length, width = keys.shape
    steps = 4
    chunk = length // steps

    def kernel(p_ref, c_ref, t_ref, k_ref, v_ref, nk_ref, nv_ref, bk_ref, bv_ref):
        at = lax.broadcasted_iota(jnp.int32, (chunk, width), 0) + pl.program_id(0) * chunk
        hit = (at == p_ref[...]).astype(f32)
        here = jnp.max(hit, axis=1, keepdims=True) > 0.0
        hit = hit.astype(bf16)
        turn = slice(ROW_DEV, ROW_DEV + 1)
        turned = turn_by(k_ref[0].astype(f32), c_ref[turn, :], t_ref[turn, :])
        placed = jnp.dot(hit, nk_ref[...], preferred_element_type=f32)
        bk_ref[0] = jnp.where(here, placed, turned).astype(bf16)
        placed = jnp.dot(hit, nv_ref[...], preferred_element_type=f32)
        bv_ref[0] = jnp.where(here, placed, v_ref[0].astype(f32)).astype(bf16)

    tile = pl.BlockSpec((1, chunk, width), lambda k: (0, k, 0))
    return pl.pallas_call(
        kernel,
        grid=(steps,),
        out_shape=(shape(keys.shape, bf16), shape(keys.shape, bf16)),
        in_specs=[
            whole(picked),
            whole(cosine),
            whole(sine),
            tile,
            tile,
            whole(new_keys),
            whole(new_values),
        ],
        out_specs=(tile, tile),
        compiler_params=pltpu.CompilerParams(vmem_limit_bytes=8 << 20),
        name="blend",
    )(picked, cosine, sine, keys, values, new_keys, new_values)


def attend(control, queries, keys, values, wanted_at, own, new_mine, new_other, new_at, new_key_at):
    width = keys.shape[2]
    length = keys.shape[1]
    cuts = [(0, SEL), (0, SEL), (SEL, ROW_DEV), (SEL, ROW_DEV)]
    count = sum(high - low for low, high in cuts)
    back = count - SEL
    step = 32

    def kernel(
        c_ref, q_ref, k_ref, v_ref, w_ref, own_ref, nm_ref, no_ref, na_ref, nk_ref,
        back_ref, kept_ref, new_ref, rows_ref, level_ref,
    ):
        at = 0
        for i, (low, high) in enumerate(cuts):
            rows_ref[at : at + high - low, :] = q_ref[c_ref[i], low:high, :]
            at += high - low
        key_at = c_ref[4] + lax.broadcasted_iota(jnp.int32, (step, length), 1)
        for n in range(count // step):
            span = slice(n * step, (n + 1) * step)
            out, level = partial_attention(
                rows_ref[span, :], k_ref[0], v_ref[0], key_at <= w_ref[span, :]
            )
            level = jnp.broadcast_to(level, (step, width))
            if n * step < 2 * SEL:
                kept_ref[span, :width] = out
                kept_ref[span, width:] = level
            if n * step >= SEL:
                to = slice(n * step - SEL, (n + 1) * step - SEL)
                level_ref[to, :] = level
                for z in range(NZH):
                    back_ref[z, to, :] = out.astype(bf16)
        level_ref[back:, :] = jnp.zeros((2 * width - back, width), f32)
        lines = [jnp.transpose(level_ref[i * width : (i + 1) * width, :])[:1] for i in range(2)]
        lines = [piece for line in lines for piece in pieces_of(line)]
        lines.append(jnp.zeros((LEVEL_ROWS - len(lines), width), f32))
        lines = jnp.concatenate(lines, axis=0).astype(bf16)
        for z in range(NZH):
            back_ref[z, back:, :] = lines
        new_keys = jnp.concatenate([nm_ref[:TOKN_DEV, :], no_ref[:TOKN_DEV, :]], axis=0)
        new_values = jnp.concatenate([nm_ref[TOKN_DEV:, :], no_ref[TOKN_DEV:, :]], axis=0)
        out, level = partial_attention(
            own_ref[0, SEL:, :], new_keys, new_values, nk_ref[...] <= na_ref[...]
        )
        new_ref[:, :width] = out
        new_ref[:, width:] = jnp.broadcast_to(level, (TOKN_DEV, width))

    return call(
        kernel,
        "attend",
        (
            shape((NZH, back + LEVEL_ROWS, width), bf16),
            shape((2 * SEL, 2 * width), f32),
            shape((TOKN_DEV, 2 * width), f32),
        ),
        control,
        queries,
        keys,
        values,
        wanted_at,
        own,
        new_mine,
        new_other,
        new_at,
        new_key_at,
        scratch=[pltpu.VMEM((count, width), bf16), pltpu.VMEM((2 * width, width), f32)],
    )


def merge_and_project(control, kept, new_part, returned, weights):
    width = new_part.shape[1] // 2
    count, part, _ = weights[0].shape
    halves = part // width
    blocks = len(weights) * count * halves
    back = returned.shape[1] - LEVEL_ROWS

    def kernel(c_ref, kept_ref, new_ref, back_ref, *refs):
        weight_refs, (out_ref, att_ref) = refs[:-2], refs[-2:]
        def levels(source):
            lines = back_ref[source, back:, :].astype(f32)
            lines = jnp.concatenate([lines, jnp.zeros((width - LEVEL_ROWS, width), f32)], axis=0)
            lines = jnp.transpose(lines)
            return [
                lines[:, n : n + 1] + lines[:, n + 1 : n + 2] + lines[:, n + 2 : n + 3]
                for n in (0, 3)
            ]

        first = c_ref[4] == 1
        kept = jnp.where(first, kept_ref[:SEL, :], kept_ref[SEL:, :])
        remote = back_ref[c_ref[0], :SEL, :].astype(f32)
        remote_level = jnp.where(first, MASKED, levels(c_ref[0])[0][:SEL])
        att_ref[:SEL, :] = merge(
            [(kept[:, :width], kept[:, width : width + 1]), (remote, remote_level)]
        )
        at = pl.multiple_of(SEL + c_ref[3] * TOKN_DEV, TOKN_DEV)
        parts = [(new_ref[:, :width], new_ref[:, width : width + 1])]
        for i in range(PPR):
            column = levels(c_ref[1 + i])
            level = jnp.where(c_ref[3] == 0, column[0][SEL:], column[1][:TOKN_DEV])
            parts.append((back_ref[c_ref[1 + i], pl.ds(at, TOKN_DEV), :].astype(f32), level))
        att_ref[SEL:, :] = merge(parts)
        attention = att_ref[...].astype(bf16)
        for j, ref in enumerate(weight_refs):
            for n in range(count):
                term = lax.dot_general(
                    attention,
                    ref[n, :, 3 * width :],
                    (((1,), (1,)), ((), ())),
                    preferred_element_type=f32,
                ).astype(bf16)
                for h in range(halves):
                    out_ref[(j * count + n) * halves + h] = term[:, h * width : (h + 1) * width]

    return call(
        kernel,
        "merge_and_project",
        shape((blocks, ROW_DEV, width), bf16),
        control,
        kept,
        new_part,
        returned,
        *weights,
        scratch=[pltpu.VMEM((ROW_DEV, width), f32)],
    )


def feed_forward(columns, summed, hidden, gain, parcels, units):
    blocks, rows, part = summed.shape
    model = blocks * part
    count, _, depth = parcels[0].shape
    parts = len(parcels)
    split = depth // part
    per = rows // (NZL * NX)
    contract_last = (((1,), (1,)), ((), ()))

    def kernel(c_ref, s_ref, x_ref, g_ref, *refs):
        parcel_refs = refs[:parts]
        out_ref, mixed_ref, acc_ref = refs[parts:]
        squares = jnp.zeros((rows, part), f32)
        for b in range(blocks):
            block = s_ref[b].astype(f32)
            squares = squares + block * block
        norm = lax.rsqrt(jnp.sum(squares, axis=1, keepdims=True) / model + EPSILON)
        for m in range(parts * count):
            cols = pl.ds(pl.multiple_of(c_ref[m] * depth, depth), depth)
            summed = jnp.concatenate([s_ref[m * split + h] for h in range(split)], axis=1)
            mixed = (
                x_ref[:, cols].astype(f32) + summed.astype(f32) * norm * g_ref[:, cols]
            ).astype(bf16)
            mixed_ref[:, cols] = mixed
            product = lax.dot_general(
                parcel_refs[m // count][m % count, : 2 * units],
                mixed,
                contract_last,
                preferred_element_type=f32,
            )
            acc_ref[...] = product if m == 0 else acc_ref[...] + product
        to = lax.broadcasted_iota(jnp.int32, (rows, rows), 0)
        at = lax.broadcasted_iota(jnp.int32, (rows, rows), 1)
        source = (to // per) % NZL * (NX * per) + to // (NZL * per) * per + to % per
        move = jnp.where(at == source, 1.0, 0.0).astype(bf16)
        gate = acc_ref[:units, :]
        active = (gate / (1.0 + jnp.exp(-gate)) * acc_ref[units:, :]).astype(bf16)
        active = lax.dot_general(
            move, active, contract_last, preferred_element_type=f32
        ).astype(bf16)
        for m in range(parts * count):
            cols = pl.ds(pl.multiple_of(c_ref[m] * depth, depth), depth)
            down = parcel_refs[m // count][m % count, 2 * units : 3 * units]
            out_ref[:, cols] = jnp.dot(active, down, preferred_element_type=f32).astype(bf16)

    return call(
        kernel,
        "feed_forward",
        (shape((rows, model), bf16), shape((rows, model), bf16)),
        columns,
        summed,
        hidden,
        gain,
        *parcels,
        scratch=[pltpu.VMEM((2 * units, rows), f32)],
    )


def shards(
    hidden_states,
    query_weight,
    key_weight,
    value_weight,
    output_weight,
    query_gain,
    key_gain,
    attention_gain,
    gate_weight,
    up_weight,
    down_weight,
    feedforward_gain,
    cached_keys,
    cached_values,
    passage_order,
    separators,
    recompute_index,
    prompt_lengths,
):
    y_at, zh, core = (lax.axis_index(a) for a in SEQ)
    zl, x_at = (lax.axis_index(a) for a in BLK)
    seq = y_at * 4 + zh * 2 + core
    width = query_weight.shape[1]
    hidden_units = gate_weight.shape[1]
    model = hidden_states.shape[1]
    blocks = NX * NZL
    rows = ROW_DEV // blocks

    mine = join_weights(query_weight, key_weight, value_weight, output_weight)
    theirs = swap(mine, "zh", NZH)
    near = copies_to_all(mine, "y", NY)
    parcel = jnp.concatenate([gate_weight.T, up_weight.T, down_weight])
    parcel = jnp.pad(parcel, ((0, -parcel.shape[0] % 16), (0, 0)))

    at, wanted_at, picked, new_at, new_key_at, attend_control, merge_control, columns = tables(
        seq, passage_order, separators, prompt_lengths, recompute_index
    )
    frequency = frequencies()
    angles = at * jnp.concatenate([frequency, frequency])[None, :]
    sign = jnp.where(jnp.arange(HD) < HD // 2, -1.0, 1.0).astype(f32)
    cosine, sine = jnp.cos(angles), jnp.sin(angles) * sign
    theirs, near, cosine, sine = lax.optimization_barrier((theirs, near, cosine, sine))

    near_other = swap(near, "core", NCORE)
    far = copies_to_all(theirs, "y", NY)
    far_other = swap(far, "core", NCORE)
    parcel_near = lax.all_gather(parcel, "y")
    weights = [near, near_other, far, far_other]
    raw, squares = project(columns, hidden_states, weights, width, blocks)
    squares = lax.all_to_all(squares, BLK, 0, 0, tiled=True)
    squares, parcel, parcel_near = lax.optimization_barrier((squares, parcel, parcel_near))
    pair = lax.all_gather(parcel, "zh")
    query, key, value, new_mine = finish_rows(
        raw, squares, query_gain[None], key_gain[None], cosine, sine, model
    )

    queries = lax.all_to_all(query, "zh", 0, 0, tiled=True)
    queries = copies_to_all(queries, "y", NY)
    queries = copies_to_all(queries, "core", NCORE).reshape(N_SEQ, ROW_DEV, width)
    new_other = swap(new_mine, "core", NCORE)
    blended_keys, blended_values = blend(
        picked, cosine, sine, cached_keys, cached_values, key, value
    )
    returned, kept, new_part = attend(
        attend_control,
        queries,
        blended_keys,
        blended_values,
        wanted_at,
        query,
        new_mine,
        new_other,
        new_at,
        new_key_at,
    )

    returned = lax.all_to_all(returned, "zh", 0, 0, tiled=True)
    returned = copies_to_all(returned, "y", NY)
    returned = copies_to_all(returned, "core", NCORE).reshape(N_SEQ, -1, width)

    terms = merge_and_project(merge_control, kept, new_part, returned, weights)
    terms, pair = lax.optimization_barrier((terms, pair))
    parcel_far = lax.all_gather(lax.dynamic_index_in_dim(pair, 1 - zh, 0, False), "y")
    terms = lax.all_to_all(terms.reshape(NX, NZL, ROW_DEV, width), "x", 0, 0, tiled=True)
    terms = jnp.sum(terms.astype(f32), axis=0).astype(bf16)
    terms = lax.all_to_all(terms, "zl", 0, 0, tiled=True)
    summed = jnp.sum(terms.astype(f32), axis=0).astype(bf16)
    summed = copies_to_all(summed, "zl", NZL)
    summed, parcel_far = lax.optimization_barrier((summed, parcel_far))
    summed = copies_to_all(summed, "x", NX).reshape(blocks, ROW_DEV, model // blocks)

    parcels = [parcel_near, swap(parcel_near, "core", NCORE)]
    parcels += [parcel_far, swap(parcel_far, "core", NCORE)]
    terms, mixed = feed_forward(
        columns, summed, hidden_states, attention_gain[None], parcels, hidden_units
    )
    terms = lax.all_to_all(terms.reshape(NX, NZL * rows, model), "x", 0, 0, tiled=True)
    terms = jnp.sum(terms.astype(f32), axis=0).astype(bf16)
    terms = lax.all_to_all(terms.reshape(NZL, rows, model), "zl", 0, 0, tiled=True)
    total = jnp.sum(terms.astype(f32), axis=0)
    norm = lax.rsqrt(jnp.mean(total * total, axis=1, keepdims=True) + EPSILON)
    my_rows = lax.dynamic_slice_in_dim(mixed, (zl * NX + x_at) * rows, rows, 0)
    hidden_out = (my_rows.astype(f32) + total * norm * feedforward_gain).astype(bf16)
    return (hidden_out, blended_keys, blended_values)


def solution(mesh):
    fine = Mesh(
        mesh.devices.reshape(NY, NZH, NCORE, NZL, NX), ("y", "zh", "core", "zl", "x")
    )
    by_both = P(SEQ, BLK)
    return jax.shard_map(
        shards,
        mesh=fine,
        in_specs=(
            P(SEQ, None),
            by_both,
            by_both,
            by_both,
            P(BLK, SEQ),
            P(BLK),
            P(BLK),
            P(),
            by_both,
            by_both,
            P(BLK, SEQ),
            P(),
            P(SEQ, None, BLK),
            P(SEQ, None, BLK),
            P(),
            P(),
            P(),
            P(),
        ),
        out_specs=(P(SEQ + BLK, None), P(SEQ, None, BLK), P(SEQ, None, BLK)),
        check_vma=False,
    )
```
